1024 devices in a mesh: shot: 32 (over x, y_hi, core), slab: 32 (over z, y_lo).
Axes of the slice: x: 4, y: 8 (y_hi: 4, y_lo: 2; y = y_hi * 2 + y_lo), z: 16, core: 2. Of those that a mesh axis runs over, the one named last changes fastest.
Arguments:
- velocity: float32 [256, 64, 128], P('slab'), may hold values from 0.2 to 0.4
- wave_state: float32 [2, 32, 2, 256, 64, 128], P(None, 'shot', None, 'slab'), may hold values from -6 to 6
- source_cells: int32 [32, 4], P('shot'), may hold values from 0 to 2097151
- source_codes: int32 [32, 4], P('shot'), may hold values from 0 to 7
- wavelets: float32 [8, 2], replicated, may hold values from -48 to 48
- receiver_cells: int32 [32, 256], P('shot'), may hold values from 0 to 2097151
- residuals: float32 [32, 2, 256], P('shot'), may hold values from -48 to 48
- momentum: float32 [256, 64, 128], P('slab', 'shot'), may hold values from -6 to 6
- diffusivity: float32 [3, 256, 64, 128], P(None, 'slab', 'shot'), may hold values from 0.02 to 0.15
Outputs:
- final_fields: float32 [32, 2, 256, 64, 128], P('shot', None, 'slab')
- new_momentum: float32 [256, 64, 128], P('slab', 'shot')
- new_velocity: float32 [256, 64, 128], P('slab', 'shot')
The draws below stay inside these ranges and needn't reach their ends.
All inputs are finite; a program needn't handle non-finite values.
Results may differ from the reference program's by a relative error of at most 0.000076.
Values sent between devices are 32-bit elements; how exact they have to be, the bound alone decides.
A program may use at most 32 MiB of HBM per device.

```python
import math
import jax
import jax.numpy as jnp
from jax import lax

NX = 64
NY = 128
STEPS = 2
SRC = 4
REC = 256
CODES = 8
NZ = 256
GROUPS = 32


def set_ends(values, rng, smallest, largest):
    place = [jax.random.randint(jax.random.fold_in(rng, axis), (), 0, length) for axis, length in enumerate(values.shape)]
    widest = values.shape.index(max(values.shape))
    beside = place[:widest] + [(place[widest] + 1) % values.shape[widest]] + place[widest + 1:]
    return values.at[tuple(place)].set(smallest).at[tuple(beside)].set(largest)


def shard_levels(stream_key, extent, split, smallest, high):
    def one(dim, parts):
        heights = jax.random.uniform(jax.random.fold_in(jax.random.fold_in(stream_key, 6), dim), (parts,), jnp.float32, smallest / len(split), high / len(split))
        return jnp.repeat(jnp.exp(heights), extent[dim] // parts).reshape((-1,) + (1,) * (len(extent) - dim - 1))

    level = one(*split[0])
    for cut in split[1:]:
        level = level * one(*cut)
    return level


def normal_values(own_key, shape, width, most, cuts=(), kind=jnp.bfloat16):
    entries = jax.random.normal(own_key, shape, jnp.float32) * width
    if len(cuts) > 0:
        entries = shard_levels(own_key, shape, cuts, -0.22, 0.18) * entries
    return jnp.clip(entries, min=-most, max=most).astype(kind)


def setup_inputs(seed: int = 0) -> dict:
    streams_of = jax.random.split(jax.random.key(seed), 10)
    velocity = jnp.clip(0.2 + 0.2 * jax.random.uniform(streams_of[0], (NZ, NX, NY), jnp.float32) ** shard_levels(streams_of[0], (NZ, NX, NY), ((0, 32),), -0.2, 0.2), 0.2, 0.4)
    wave_state = normal_values(streams_of[1], (2, GROUPS, 2, NZ, NX, NY), 1.0, 6.0, ((1, 32), (3, 32)), jnp.float32)
    source_cells = set_ends(jax.random.randint(streams_of[2], (GROUPS, SRC), 0, NZ * NX * NY), jax.random.fold_in(streams_of[2], 1), 0, (NZ * NX * NY) - 1).astype(jnp.int32)
    source_codes = set_ends(jax.random.randint(streams_of[3], (GROUPS, SRC), 0, CODES), jax.random.fold_in(streams_of[3], 1), 0, CODES - 1).astype(jnp.int32)
    wavelets = normal_values(streams_of[4], (CODES, STEPS), 8.0, 48.0, (), jnp.float32)
    receiver_cells = set_ends(jax.random.randint(streams_of[5], (GROUPS, REC), 0, NZ * NX * NY), jax.random.fold_in(streams_of[5], 1), 0, (NZ * NX * NY) - 1).astype(jnp.int32)
    residuals = normal_values(streams_of[6], (GROUPS, STEPS, REC), 8.0, 48.0, ((0, 32),), jnp.float32)
    momentum = normal_values(streams_of[7], (NZ, NX, NY), 1.0, 6.0, ((0, 32), (1, 32)), jnp.float32)
    diffusivity = jnp.clip(0.02 + 0.13000001 * jax.random.uniform(streams_of[8], (3, NZ, NX, NY), jnp.float32) ** shard_levels(streams_of[8], (3, NZ, NX, NY), ((1, 32), (2, 32)), -0.2, 0.2), 0.02, 0.15)
    return dict(velocity=velocity, wave_state=wave_state, source_cells=source_cells, source_codes=source_codes, wavelets=wavelets, receiver_cells=receiver_cells, residuals=residuals, momentum=momentum, diffusivity=diffusivity)


STENCIL_TAPS = (-205.0 / 72.0, 8.0 / 5.0, -1.0 / 5.0, 8.0 / 315.0, -1.0 / 560.0)

def laplacian(padded):
    leading = padded.ndim - 2
    lateral = jnp.pad(padded, [(0, 0)] * leading + [(4, 4), (4, 4)])
    row_count = padded.shape[-3] - 8
    size_x = padded.shape[-2]
    size_y = padded.shape[-1]

    def shifted(off_z, off_x, off_y):
        return lateral[..., 4 + off_z:4 + off_z + row_count, 4 + off_x:4 + off_x + size_x, 4 + off_y:4 + off_y + size_y]
    summed = 3.0 * STENCIL_TAPS[0] * shifted(0, 0, 0)
    for radius in range(1, 5):
        cycle_sum = shifted(radius, 0, 0) + shifted(-radius, 0, 0) + shifted(0, radius, 0) + shifted(0, -radius, 0) + shifted(0, 0, radius) + shifted(0, 0, -radius)
        summed = summed + STENCIL_TAPS[radius] * cycle_sum
    return summed

def smooth_step(extended, kappas):
    lateral = jnp.pad(extended, ((0, 0), (0, 0), (1, 1)))
    centre = extended[1:-1, 1:-1, :]
    along_z = extended[2:, 1:-1, :] - 2.0 * centre + extended[:-2, 1:-1, :]
    along_x = extended[1:-1, 2:, :] - 2.0 * centre + extended[1:-1, :-2, :]
    along_y = lateral[1:-1, 1:-1, 2:] - 2.0 * centre + lateral[1:-1, 1:-1, :-2]
    return centre + kappas[0] * along_z + kappas[1] * along_x + kappas[2] * along_y

def reference(velocity, wave_state, source_cells, source_codes, wavelets, receiver_cells, residuals, momentum, diffusivity):
    speed_sq = velocity * velocity
    amplitude = wavelets[source_codes]
    volume = NZ * NX * NY

    def one_group(imaging, inputs):
        previous, current, src_ids, src_amounts, rec_ids, rec_amounts = inputs
        for moment in range(STEPS):
            padded = jnp.pad(current, ((0, 0), (4, 4), (0, 0), (0, 0)))
            source_grid = jnp.zeros((volume,), jnp.float32).at[src_ids].add(src_amounts[:, moment]).reshape(NZ, NX, NY)
            rec_grid = jnp.zeros((volume,), jnp.float32).at[rec_ids].add(rec_amounts[moment]).reshape(NZ, NX, NY)
            driven = speed_sq * (laplacian(padded) + jnp.stack([source_grid, rec_grid]))
            imaging = imaging + driven[0] * current[1]
            previous, current = (current, 2.0 * current - previous + driven)
        return (imaging, current)
    imaging, finals = lax.scan(one_group, jnp.zeros((NZ, NX, NY), jnp.float32), (wave_state[0], wave_state[1], source_cells, amplitude, receiver_cells, residuals))
    gradient = -0.2 * imaging / (velocity * math.sqrt(GROUPS * STEPS))
    smoothed = gradient
    for repeat in range(2):
        smoothed = smooth_step(jnp.pad(smoothed, ((1, 1), (1, 1), (0, 0))), diffusivity)
    new_momentum = 0.9 * momentum + smoothed
    new_velocity = velocity - 0.02 * new_momentum
    return (finals, new_momentum, new_velocity)
```

```python
import math

import jax
import jax.numpy as jnp
from jax import lax
from jax.experimental import pallas as pl
from jax.experimental.pallas import tpu as pltpu
from jax.sharding import PartitionSpec as P

TAPS = (-205.0 / 72.0, 8.0 / 5.0, -1.0 / 5.0, 8.0 / 315.0, -1.0 / 560.0)
MESH = pl.DeviceIdType.MESH
ROWS, NX, NY = 8, 64, 128
SLABS, SHOTS = 32, 32
STEPS = 2
PLANE = NX * NY
SCALE = math.sqrt(SHOTS * STEPS)


def shifted(plane, offset, axis, index):
    size = plane.shape[axis]
    rolled = pltpu.roll(plane, (-offset) % size, axis)
    keep = index < size - offset if offset > 0 else index >= -offset
    return jnp.where(keep, rolled, 0.0)


def lateral(plane):
    along_x = lax.broadcasted_iota(jnp.int32, plane.shape, 0)
    along_y = lax.broadcasted_iota(jnp.int32, plane.shape, 1)
    total = (3.0 * TAPS[0]) * plane
    for r in range(1, 5):
        pairs = shifted(plane, r, 0, along_x) + shifted(plane, -r, 0, along_x)
        pairs = pairs + shifted(plane, r, 1, along_y) + shifted(plane, -r, 1, along_y)
        total = total + TAPS[r] * pairs
    return total


def kernel(
    src_cells,
    src_codes,
    wavelets,
    velocity,
    waves,
    rec_cells_hbm,
    residuals_hbm,
    momentum,
    diffusivity,
    fields,
    new_momentum,
    new_velocity,
    ext,
    prev,
    vel,
    lat,
    inject,
    rec_cells,
    residuals,
    spread,
    image,
    image_t,
    pair_in,
    pair_sum,
    group_in,
    mom,
    dif,
    held,
    around,
    load_sem,
    halo_send,
    halo_recv,
    pair_sem,
    group_send,
    group_recv,
    near_send,
    near_recv,
    ready,
):
    shot = lax.axis_index("shot")
    slab = lax.axis_index("slab")
    cx, cy, core = shot // 8, (shot // 2) % 4, shot % 2
    above, below = (slab + 1) % SLABS, (slab + SLABS - 1) % SLABS

    def at(x, y, c):
        return (x % 4) * 8 + (y % 4) * 2 + c

    partners = [(shot, above), (shot, below), (at(cx, cy, 1 - core), slab)]
    partners += [(at(cx + d, cy, core), slab) for d in (1, 2, 3)]
    partners += [(at(cx, cy + d, core), slab) for d in (1, 3)]

    loads = [
        pltpu.make_async_copy(waves.at[1, 0, 0], ext.at[0, 0, pl.ds(4, ROWS)], load_sem.at[0]),
        pltpu.make_async_copy(waves.at[1, 0, 1], ext.at[0, 1, pl.ds(4, ROWS)], load_sem.at[1]),
        pltpu.make_async_copy(rec_cells_hbm, rec_cells, load_sem.at[2]),
        pltpu.make_async_copy(residuals_hbm, residuals, load_sem.at[3]),
        pltpu.make_async_copy(velocity, vel, load_sem.at[4]),
        pltpu.make_async_copy(waves.at[0, 0], prev, load_sem.at[5]),
        pltpu.make_async_copy(momentum, mom, load_sem.at[6]),
        pltpu.make_async_copy(diffusivity, dif, load_sem.at[7]),
    ]
    barrier = pltpu.get_barrier_semaphore()

    def greet(semaphore):
        for partner in partners:
            pl.semaphore_signal(semaphore, inc=1, device_id=partner, device_id_type=MESH)

    greet(barrier)
    for load in loads:
        load.start()
    pl.semaphore_wait(barrier, len(partners))

    def halo(step, field):
        copies = []
        for way, (target, first, landing) in enumerate(((above, 4, 0), (below, 0, 12))):
            if step == 0:
                source = waves.at[1, 0, field, pl.ds(first, 4)]
            else:
                source = ext.at[1, field, pl.ds(4 + first, 4)]
            copies.append(
                pltpu.make_async_remote_copy(
                    src_ref=source,
                    dst_ref=ext.at[step, field, pl.ds(landing, 4)],
                    send_sem=halo_send.at[step, field, way],
                    recv_sem=halo_recv.at[step, field, way],
                    device_id=(shot, target),
                    device_id_type=MESH,
                )
            )
        return copies

    def start(copies):
        for copy in copies:
            copy.start()

    def arrive(copies, step, field):
        for copy in copies:
            copy.wait_recv()

        @pl.when(slab == 0)
        def _():
            ext[step, field, pl.ds(0, 4)] = jnp.zeros((4, NX, NY), jnp.float32)

        @pl.when(slab == SLABS - 1)
        def _():
            ext[step, field, pl.ds(12, 4)] = jnp.zeros((4, NX, NY), jnp.float32)

    u0, q0 = halo(0, 0), halo(0, 1)
    start(u0)
    start(q0)
    greet(ready.at[0])

    def near_part(step, field):
        def body(z, carry):
            lat[field, z] = lateral(ext[step, field, 4 + z])
            return carry

        lax.fori_loop(0, ROWS, body, 0)

    def advance(step, field):
        def body(z, carry):
            now = ext[step, field, 4 + z]
            total = lat[field, z] + inject[field, step, z]
            for r in range(1, 5):
                total = total + TAPS[r] * (
                    ext[step, field, 4 + z + r] + ext[step, field, 4 + z - r]
                )
            drive = (vel[z] * vel[z]) * total
            before = prev[field, z] if step == 0 else ext[0, field, 4 + z]
            after = 2.0 * now - before + drive
            if step == 0:
                ext[1, field, 4 + z] = after
            else:
                fields[0, field, z] = after
            if field == 0:
                rows = pl.ds(pl.multiple_of(z * NX, NX), NX)
                product = drive * ext[step, 1, 4 + z]
                image[rows, :] = product if step == 0 else image[rows, :] + product
            return carry

        lax.fori_loop(0, ROWS, body, 0)

    base = slab * (ROWS * PLANE)
    cells = [src_cells[0, k] - base for k in range(4)]
    amounts = [[wavelets[t, src_codes[0, k]] for k in range(4)] for t in range(STEPS)]

    def source_row(z, carry):
        cell = lax.broadcasted_iota(jnp.int32, (NX, NY), 0) * NY
        cell = cell + lax.broadcasted_iota(jnp.int32, (NX, NY), 1) + z * PLANE
        grids = [jnp.zeros((NX, NY), jnp.float32) for _ in range(STEPS)]
        for k in range(4):
            here = cell == cells[k]
            for t in range(STEPS):
                grids[t] = grids[t] + jnp.where(here, amounts[t][k], 0.0)
        for t in range(STEPS):
            inject[0, t, z] = grids[t]
        return carry

    lax.fori_loop(0, ROWS, source_row, 0)

    loads[0].wait()
    near_part(0, 0)
    pl.semaphore_wait(ready.at[0], len(partners))
    greet(ready.at[1])

    loads[2].wait()
    loads[3].wait()
    cell = rec_cells[...] - base
    line = cell >> 7
    lane = cell & (NY - 1)
    count = cell.shape[1]
    for t in range(STEPS):
        here = lax.broadcasted_iota(jnp.int32, (NY, count), 0) == lane
        rest = jnp.where(here, residuals[0, pl.ds(t, 1), :], 0.0)
        for part in range(3):
            piece = rest.astype(jnp.bfloat16)
            spread[part, pl.ds(t * NY, NY), :] = piece
            rest = rest - piece.astype(jnp.float32)

    def receiver_row(z, carry):
        here = lax.broadcasted_iota(jnp.int32, (NX, count), 0) + z * NX == line
        chosen = jnp.where(here, 1.0, 0.0).astype(jnp.bfloat16)
        grid = jnp.zeros((NX, STEPS * NY), jnp.float32)
        for part in range(3):
            grid = grid + lax.dot_general(
                chosen,
                spread[part],
                (((1,), (1,)), ((), ())),
                preferred_element_type=jnp.float32,
            )
        for t in range(STEPS):
            inject[1, t, z] = grid[:, t * NY : (t + 1) * NY]
        return carry

    lax.fori_loop(0, ROWS, receiver_row, 0)
    pl.semaphore_wait(ready.at[1], len(partners))

    loads[1].wait()
    near_part(0, 1)
    loads[4].wait()
    loads[5].wait()

    arrive(u0, 0, 0)
    advance(0, 0)
    u1 = halo(1, 0)
    start(u1)
    near_part(1, 0)

    arrive(q0, 0, 1)
    advance(0, 1)
    q1 = halo(1, 1)
    start(q1)

    arrive(u1, 1, 0)
    advance(1, 0)

    def turn(i, carry):
        for inner in range(4):
            strip = image[pl.ds(i * 4 + inner, ROWS, stride=NX), :]
            image_t[i, inner // 2, inner % 2] = strip
        return carry

    lax.fori_loop(0, NX // 4, turn, 0)
    pair = pltpu.make_async_remote_copy(
        src_ref=image_t.at[:, 1 - core],
        dst_ref=pair_in,
        send_sem=pair_sem.at[0],
        recv_sem=pair_sem.at[1],
        device_id=(at(cx, cy, 1 - core), slab),
        device_id_type=MESH,
    )
    pair.start()
    near_part(1, 1)
    pair.wait_recv()

    def join(i, carry):
        pair_sum[i] = image_t[i, core] + pair_in[i]
        return carry

    lax.fori_loop(0, 16, join, 0)

    def group(k):
        tx, ty = (cx + k // 4) % 4, (cy + k % 4) % 4
        return pltpu.make_async_remote_copy(
            src_ref=pair_sum.at[tx * 4 + ty],
            dst_ref=group_in.at[k],
            send_sem=group_send.at[k],
            recv_sem=group_recv.at[k],
            device_id=(at(tx, ty, core), slab),
            device_id_type=MESH,
        )

    def send_group(k, carry):
        group(k).start()
        return carry

    lax.fori_loop(1, 16, send_group, 0)

    arrive(q1, 1, 1)
    advance(1, 1)
    loads[6].wait()
    loads[7].wait()

    def take_group(k, total):
        group(k).wait_recv()
        return total + group_in[k]

    total = lax.fori_loop(1, 16, take_group, pair_sum[cx * 4 + cy])

    depth = lax.broadcasted_iota(jnp.int32, (ROWS, NY), 0)
    along_y = lax.broadcasted_iota(jnp.int32, (ROWS, NY), 1)
    speed = []
    smooth = []
    for i in range(2):
        rows = [vel[z, pl.ds(shot * 2 + i, 1), :] for z in range(ROWS)]
        speed.append(jnp.concatenate(rows, axis=0))
        smooth.append((-0.2 * total[i]) / (speed[i] * SCALE))
    left, right = (shot + SHOTS - 1) % SHOTS, (shot + 1) % SHOTS
    for turn_no in range(2):
        for i in range(2):
            held[turn_no, i] = smooth[i]
        copies = []
        for way, target in enumerate(((shot, above), (shot, below), (right, slab), (left, slab))):
            copy = pltpu.make_async_remote_copy(
                src_ref=held.at[turn_no],
                dst_ref=around.at[turn_no, way],
                send_sem=near_send.at[turn_no, way],
                recv_sem=near_recv.at[turn_no, way],
                device_id=target,
                device_id_type=MESH,
            )
            copy.start()
            copies.append(copy)
        for copy in copies:
            copy.wait_recv()
        fresh = []
        for i in range(2):
            centre = smooth[i]
            low = jnp.where(slab > 0, around[turn_no, 0, i], 0.0)
            high = jnp.where(slab < SLABS - 1, around[turn_no, 1, i], 0.0)
            down = jnp.where(depth == 0, pltpu.roll(low, 1, 0), pltpu.roll(centre, 1, 0))
            up = jnp.where(depth == ROWS - 1, pltpu.roll(high, ROWS - 1, 0), pltpu.roll(centre, ROWS - 1, 0))
            if i == 0:
                before = jnp.where(shot > 0, around[turn_no, 2, 1], 0.0)
                after = smooth[1]
            else:
                before = smooth[0]
                after = jnp.where(shot < SHOTS - 1, around[turn_no, 3, 0], 0.0)
            along_z = up - 2.0 * centre + down
            along_x = after - 2.0 * centre + before
            sides = shifted(centre, 1, 1, along_y) + shifted(centre, -1, 1, along_y)
            fresh.append(
                centre
                + dif[0, :, i, :] * along_z
                + dif[1, :, i, :] * along_x
                + dif[2, :, i, :] * (sides - 2.0 * centre)
            )
        smooth = fresh
        for copy in copies:
            copy.wait_send()
    for i in range(2):
        updated = 0.9 * mom[:, i, :] + smooth[i]
        new_momentum[:, i, :] = updated
        new_velocity[:, i, :] = speed[i] - 0.02 * updated

    for copies in (u0, q0, u1, q1):
        for copy in copies:
            copy.wait_send()
    pair.wait_send()

    def drain_group(k, carry):
        group(k).wait_send()
        return carry

    lax.fori_loop(1, 16, drain_group, 0)


def on_device(
    velocity,
    wave_state,
    source_cells,
    source_codes,
    wavelets,
    receiver_cells,
    residuals,
    momentum,
    diffusivity,
):
    hbm = pl.BlockSpec(memory_space=pl.ANY)
    smem = pl.BlockSpec(memory_space=pltpu.SMEM)
    vmem = pl.BlockSpec(memory_space=pltpu.VMEM)
    f32 = jnp.float32
    return pl.pallas_call(
        kernel,
        out_shape=(
            jax.ShapeDtypeStruct((1, 2, ROWS, NX, NY), f32),
            jax.ShapeDtypeStruct((ROWS, 2, NY), f32),
            jax.ShapeDtypeStruct((ROWS, 2, NY), f32),
        ),
        in_specs=[smem, smem, smem] + [hbm] * 6,
        out_specs=(vmem, vmem, vmem),
        scratch_shapes=[
            pltpu.VMEM((STEPS, 2, 16, NX, NY), f32),
            pltpu.VMEM((2, ROWS, NX, NY), f32),
            pltpu.VMEM((ROWS, NX, NY), f32),
            pltpu.VMEM((2, ROWS, NX, NY), f32),
            pltpu.VMEM((2, STEPS, ROWS, NX, NY), f32),
            pltpu.VMEM(receiver_cells.shape, jnp.int32),
            pltpu.VMEM(residuals.shape, f32),
            pltpu.VMEM((3, STEPS * NY, receiver_cells.shape[1]), jnp.bfloat16),
            pltpu.VMEM((ROWS * NX, NY), f32),
            pltpu.VMEM((16, 2, 2, ROWS, NY), f32),
            pltpu.VMEM((16, 2, ROWS, NY), f32),
            pltpu.VMEM((16, 2, ROWS, NY), f32),
            pltpu.VMEM((16, 2, ROWS, NY), f32),
            pltpu.VMEM((ROWS, 2, NY), f32),
            pltpu.VMEM((3, ROWS, 2, NY), f32),
            pltpu.VMEM((2, 2, ROWS, NY), f32),
            pltpu.VMEM((2, 4, 2, ROWS, NY), f32),
            pltpu.SemaphoreType.DMA((8,)),
            pltpu.SemaphoreType.DMA((STEPS, 2, 2)),
            pltpu.SemaphoreType.DMA((STEPS, 2, 2)),
            pltpu.SemaphoreType.DMA((2,)),
            pltpu.SemaphoreType.DMA((16,)),
            pltpu.SemaphoreType.DMA((16,)),
            pltpu.SemaphoreType.DMA((2, 4)),
            pltpu.SemaphoreType.DMA((2, 4)),
            pltpu.SemaphoreType.REGULAR((2,)),
        ],
        compiler_params=pltpu.CompilerParams(collective_id=0, has_side_effects=True),
    )(
        source_cells,
        source_codes,
        wavelets.T,
        velocity,
        wave_state,
        receiver_cells,
        residuals,
        momentum,
        diffusivity,
    )


def solution(mesh):
    return jax.shard_map(
        on_device,
        mesh=mesh,
        in_specs=(
            P("slab", None, None),
            P(None, "shot", None, "slab", None, None),
            P("shot", None),
            P("shot", None),
            P(),
            P("shot", None),
            P("shot", None, None),
            P("slab", "shot", None),
            P(None, "slab", "shot", None),
        ),
        out_specs=(
            P("shot", None, "slab", None, None),
            P("slab", "shot", None),
            P("slab", "shot", None),
        ),
        check_vma=False,
    )
```

```python
import math

import jax
import jax.numpy as jnp
from jax import lax
from jax.experimental import pallas as pl
from jax.experimental.pallas import tpu as pltpu
from jax.sharding import PartitionSpec as P

TAPS = (-205.0 / 72.0, 8.0 / 5.0, -1.0 / 5.0, 8.0 / 315.0, -1.0 / 560.0)
MESH = pl.DeviceIdType.MESH
ROWS, NX, NY = 8, 64, 128
SLABS, SHOTS = 32, 32
STEPS = 2
PLANE = NX * NY
SCALE = math.sqrt(SHOTS * STEPS)


def shifted(plane, offset, axis, index):
    size = plane.shape[axis]
    rolled = pltpu.roll(plane, (-offset) % size, axis)
    keep = index < size - offset if offset > 0 else index >= -offset
    return jnp.where(keep, rolled, 0.0)


def lateral(plane):
    along_x = lax.broadcasted_iota(jnp.int32, plane.shape, 0)
    along_y = lax.broadcasted_iota(jnp.int32, plane.shape, 1)
    total = (3.0 * TAPS[0]) * plane
    for r in range(1, 5):
        pairs = shifted(plane, r, 0, along_x) + shifted(plane, -r, 0, along_x)
        pairs = pairs + shifted(plane, r, 1, along_y) + shifted(plane, -r, 1, along_y)
        total = total + TAPS[r] * pairs
    return total


def kernel(
    src_cells_hbm,
    src_codes_hbm,
    wavelets_hbm,
    velocity,
    waves,
    rec_cells_hbm,
    residuals_hbm,
    momentum,
    diffusivity,
    fields,
    new_momentum,
    new_velocity,
    src_cells,
    src_codes,
    wavelets,
    ext,
    prev,
    vel,
    lat,
    inject,
    rec_cells,
    residuals,
    spread,
    image,
    image_t,
    pair_in,
    pair_sum,
    group_in,
    mom,
    dif,
    held,
    around,
    load_sem,
    halo_send,
    halo_recv,
    pair_sem,
    group_send,
    group_recv,
    near_send,
    near_recv,
    ready,
):
    shot = lax.axis_index("shot")
    slab = lax.axis_index("slab")
    cx, cy, core = shot // 8, (shot // 2) % 4, shot % 2
    above, below = slab + 1, slab - 1
    has_above, has_below = slab < SLABS - 1, slab > 0

    def at(x, y, c):
        return (x % 4) * 8 + (y % 4) * 2 + c

    partners = [(at(cx, cy, 1 - core), slab)]
    partners += [(at(cx, cy + d, core), slab) for d in (1, 3)]
    partners += [(at(cx + d, cy, core), slab) for d in (1, 2, 3)]

    loads = [
        pltpu.make_async_copy(waves.at[1, 0, 0], ext.at[0, 0, pl.ds(4, ROWS)], load_sem.at[0]),
        pltpu.make_async_copy(waves.at[1, 0, 1], ext.at[0, 1, pl.ds(4, ROWS)], load_sem.at[1]),
        pltpu.make_async_copy(rec_cells_hbm, rec_cells, load_sem.at[2]),
        pltpu.make_async_copy(residuals_hbm, residuals, load_sem.at[3]),
        pltpu.make_async_copy(velocity, vel, load_sem.at[4]),
        pltpu.make_async_copy(waves.at[0, 0], prev, load_sem.at[5]),
        pltpu.make_async_copy(momentum, mom, load_sem.at[6]),
        pltpu.make_async_copy(diffusivity, dif, load_sem.at[7]),
        pltpu.make_async_copy(src_cells_hbm, src_cells, load_sem.at[8]),
        pltpu.make_async_copy(src_codes_hbm, src_codes, load_sem.at[9]),
        pltpu.make_async_copy(wavelets_hbm, wavelets, load_sem.at[10]),
    ]
    barrier = pltpu.get_barrier_semaphore()

    def greet(semaphore):
        for partner in partners:
            pl.semaphore_signal(semaphore, inc=1, device_id=partner, device_id_type=MESH)

    def meet(target):
        pl.semaphore_signal(barrier, inc=1, device_id=(shot, target), device_id_type=MESH)

    pl.when(has_above)(lambda: meet(above))
    pl.when(has_below)(lambda: meet(below))
    greet(barrier)
    for load in loads:
        load.start()

    @pl.when(slab == 0)
    def _():
        ext[:, :, pl.ds(0, 4)] = jnp.zeros((STEPS, 2, 4, NX, NY), jnp.float32)
        around[:, 0] = jnp.zeros((2, 2, ROWS, NY), jnp.float32)

    @pl.when(slab == SLABS - 1)
    def _():
        ext[:, :, pl.ds(12, 4)] = jnp.zeros((STEPS, 2, 4, NX, NY), jnp.float32)
        around[:, 1] = jnp.zeros((2, 2, ROWS, NY), jnp.float32)

    pl.semaphore_wait(
        barrier,
        len(partners) + has_above.astype(jnp.int32) + has_below.astype(jnp.int32),
    )

    def halo(step, field):
        copies = []
        for way, (target, first, landing) in enumerate(((above, 4, 0), (below, 0, 12))):
            if step == 0:
                source = waves.at[1, 0, field, pl.ds(first, 4)]
            else:
                source = ext.at[1, field, pl.ds(4 + first, 4)]
            copies.append(
                pltpu.make_async_remote_copy(
                    src_ref=source,
                    dst_ref=ext.at[step, field, pl.ds(landing, 4)],
                    send_sem=halo_send.at[step, field, way],
                    recv_sem=halo_recv.at[step, field, way],
                    device_id=(shot, target),
                    device_id_type=MESH,
                )
            )
        return copies

    def start(copies):
        pl.when(has_above)(copies[0].start)
        pl.when(has_below)(copies[1].start)

    def arrive(copies):
        pl.when(has_below)(copies[0].wait_recv)
        pl.when(has_above)(copies[1].wait_recv)

    def leave(copies):
        pl.when(has_above)(copies[0].wait_send)
        pl.when(has_below)(copies[1].wait_send)

    u0, q0 = halo(0, 0), halo(0, 1)
    start(u0)
    start(q0)
    greet(ready.at[0])

    def near_part(step, field):
        def body(z, carry):
            lat[field, z] = lateral(ext[step, field, 4 + z])
            return carry

        lax.fori_loop(0, ROWS, body, 0)

    def advance(step, field):
        def body(z, carry):
            now = ext[step, field, 4 + z]
            total = lat[field, z] + inject[field, step, z]
            for r in range(1, 5):
                total = total + TAPS[r] * (
                    ext[step, field, 4 + z + r] + ext[step, field, 4 + z - r]
                )
            drive = (vel[z] * vel[z]) * total
            before = prev[field, z] if step == 0 else ext[0, field, 4 + z]
            after = 2.0 * now - before + drive
            if step == 0:
                ext[1, field, 4 + z] = after
            else:
                fields[0, field, z] = after
            if field == 0:
                rows = pl.ds(pl.multiple_of(z * NX, NX), NX)
                product = drive * ext[step, 1, 4 + z]
                image[rows, :] = product if step == 0 else image[rows, :] + product
            return carry

        lax.fori_loop(0, ROWS, body, 0)

    for load in loads[8:]:
        load.wait()
    base = slab * (ROWS * PLANE)
    cells = [src_cells[0, k] - base for k in range(4)]
    amounts = [[wavelets[t, src_codes[0, k]] for k in range(4)] for t in range(STEPS)]

    def source_row(z, carry):
        cell = lax.broadcasted_iota(jnp.int32, (NX, NY), 0) * NY
        cell = cell + lax.broadcasted_iota(jnp.int32, (NX, NY), 1) + z * PLANE
        grids = [jnp.zeros((NX, NY), jnp.float32) for _ in range(STEPS)]
        for k in range(4):
            here = cell == cells[k]
            for t in range(STEPS):
                grids[t] = grids[t] + jnp.where(here, amounts[t][k], 0.0)
        for t in range(STEPS):
            inject[0, t, z] = grids[t]
        return carry

    lax.fori_loop(0, ROWS, source_row, 0)

    loads[0].wait()
    near_part(0, 0)
    pl.semaphore_wait(ready.at[0], len(partners))
    greet(ready.at[1])

    loads[2].wait()
    loads[3].wait()
    cell = rec_cells[...] - base
    line = cell >> 7
    lane = cell & (NY - 1)
    count = cell.shape[1]
    for t in range(STEPS):
        here = lax.broadcasted_iota(jnp.int32, (NY, count), 0) == lane
        rest = jnp.where(here, residuals[0, pl.ds(t, 1), :], 0.0)
        for part in range(3):
            piece = rest.astype(jnp.bfloat16)
            spread[part, pl.ds(t * NY, NY), :] = piece
            rest = rest - piece.astype(jnp.float32)

    def receiver_row(z, carry):
        here = lax.broadcasted_iota(jnp.int32, (NX, count), 0) + z * NX == line
        chosen = jnp.where(here, 1.0, 0.0).astype(jnp.bfloat16)
        grid = jnp.zeros((NX, STEPS * NY), jnp.float32)
        for part in range(3):
            grid = grid + lax.dot_general(
                chosen,
                spread[part],
                (((1,), (1,)), ((), ())),
                preferred_element_type=jnp.float32,
            )
        for t in range(STEPS):
            inject[1, t, z] = grid[:, t * NY : (t + 1) * NY]
        return carry

    lax.fori_loop(0, ROWS, receiver_row, 0)
    pl.semaphore_wait(ready.at[1], len(partners))

    loads[1].wait()
    near_part(0, 1)
    loads[4].wait()
    loads[5].wait()

    arrive(u0)
    advance(0, 0)
    u1 = halo(1, 0)
    start(u1)
    near_part(1, 0)

    arrive(q0)
    advance(0, 1)
    q1 = halo(1, 1)
    pl.when(has_above)(q1[0].start)

    arrive(u1)
    advance(1, 0)

    def turn(i, carry):
        for inner in range(4):
            strip = image[pl.ds(i * 4 + inner, ROWS, stride=NX), :]
            image_t[i, inner // 2, inner % 2] = strip
        return carry

    lax.fori_loop(0, NX // 4, turn, 0)
    pair = pltpu.make_async_remote_copy(
        src_ref=image_t.at[:, 1 - core],
        dst_ref=pair_in,
        send_sem=pair_sem.at[0],
        recv_sem=pair_sem.at[1],
        device_id=(at(cx, cy, 1 - core), slab),
        device_id_type=MESH,
    )
    pair.start()
    near_part(1, 1)
    pair.wait_recv()

    def join(i, carry):
        pair_sum[i] = image_t[i, core] + pair_in[i]
        return carry

    lax.fori_loop(0, 16, join, 0)

    def group(k):
        tx, ty = (cx + k // 4) % 4, (cy + k % 4) % 4
        return pltpu.make_async_remote_copy(
            src_ref=pair_sum.at[tx * 4 + ty],
            dst_ref=group_in.at[k],
            send_sem=group_send.at[k],
            recv_sem=group_recv.at[k],
            device_id=(at(tx, ty, core), slab),
            device_id_type=MESH,
        )

    def send_group(k, carry):
        group(k).start()
        return carry

    lax.fori_loop(1, 16, send_group, 0)
    pl.when(has_below)(q1[1].start)

    arrive(q1)
    advance(1, 1)
    loads[6].wait()
    loads[7].wait()

    def take_group(k, total):
        group(k).wait_recv()
        return total + group_in[k]

    total = lax.fori_loop(1, 16, take_group, pair_sum[cx * 4 + cy])

    depth = lax.broadcasted_iota(jnp.int32, (ROWS, NY), 0)
    along_y = lax.broadcasted_iota(jnp.int32, (ROWS, NY), 1)
    speed = []
    smooth = []
    for i in range(2):
        rows = [vel[z, pl.ds(shot * 2 + i, 1), :] for z in range(ROWS)]
        speed.append(jnp.concatenate(rows, axis=0))
        smooth.append((-0.2 * total[i]) / (speed[i] * SCALE))
    left, right = (shot + SHOTS - 1) % SHOTS, (shot + 1) % SHOTS
    for turn_no in range(2):
        for i in range(2):
            held[turn_no, i] = smooth[i]
        copies = []
        for way, target in enumerate(((shot, above), (shot, below), (right, slab), (left, slab))):
            copy = pltpu.make_async_remote_copy(
                src_ref=held.at[turn_no],
                dst_ref=around.at[turn_no, way],
                send_sem=near_send.at[turn_no, way],
                recv_sem=near_recv.at[turn_no, way],
                device_id=target,
                device_id_type=MESH,
            )
            copies.append(copy)
        start(copies[:2])
        copies[2].start()
        copies[3].start()
        copies[2].wait_recv()
        copies[3].wait_recv()
        arrive(copies[:2])
        fresh = []
        for i in range(2):
            centre = smooth[i]
            low, high = around[turn_no, 0, i], around[turn_no, 1, i]
            down = jnp.where(depth == 0, pltpu.roll(low, 1, 0), pltpu.roll(centre, 1, 0))
            up = jnp.where(depth == ROWS - 1, pltpu.roll(high, ROWS - 1, 0), pltpu.roll(centre, ROWS - 1, 0))
            if i == 0:
                before = jnp.where(shot > 0, around[turn_no, 2, 1], 0.0)
                after = smooth[1]
            else:
                before = smooth[0]
                after = jnp.where(shot < SHOTS - 1, around[turn_no, 3, 0], 0.0)
            along_z = up - 2.0 * centre + down
            along_x = after - 2.0 * centre + before
            sides = shifted(centre, 1, 1, along_y) + shifted(centre, -1, 1, along_y)
            fresh.append(
                centre
                + dif[0, :, i, :] * along_z
                + dif[1, :, i, :] * along_x
                + dif[2, :, i, :] * (sides - 2.0 * centre)
            )
        smooth = fresh
        leave(copies[:2])
        copies[2].wait_send()
        copies[3].wait_send()
    for i in range(2):
        updated = 0.9 * mom[:, i, :] + smooth[i]
        new_momentum[:, i, :] = updated
        new_velocity[:, i, :] = speed[i] - 0.02 * updated

    for copies in (u0, q0, u1, q1):
        leave(copies)
    pair.wait_send()

    def drain_group(k, carry):
        group(k).wait_send()
        return carry

    lax.fori_loop(1, 16, drain_group, 0)


def on_device(
    velocity,
    wave_state,
    source_cells,
    source_codes,
    wavelets,
    receiver_cells,
    residuals,
    momentum,
    diffusivity,
):
    hbm = pl.BlockSpec(memory_space=pltpu.HBM)
    vmem = pl.BlockSpec(memory_space=pltpu.VMEM)
    f32 = jnp.float32
    return pl.pallas_call(
        kernel,
        out_shape=(
            jax.ShapeDtypeStruct((1, 2, ROWS, NX, NY), f32),
            jax.ShapeDtypeStruct((ROWS, 2, NY), f32),
            jax.ShapeDtypeStruct((ROWS, 2, NY), f32),
        ),
        in_specs=[hbm] * 9,
        out_specs=(vmem, vmem, vmem),
        scratch_shapes=[
            pltpu.SMEM(source_cells.shape, jnp.int32),
            pltpu.SMEM(source_codes.shape, jnp.int32),
            pltpu.SMEM(wavelets.shape[::-1], f32),
            pltpu.VMEM((STEPS, 2, 16, NX, NY), f32),
            pltpu.VMEM((2, ROWS, NX, NY), f32),
            pltpu.VMEM((ROWS, NX, NY), f32),
            pltpu.VMEM((2, ROWS, NX, NY), f32),
            pltpu.VMEM((2, STEPS, ROWS, NX, NY), f32),
            pltpu.VMEM(receiver_cells.shape, jnp.int32),
            pltpu.VMEM(residuals.shape, f32),
            pltpu.VMEM((3, STEPS * NY, receiver_cells.shape[1]), jnp.bfloat16),
            pltpu.VMEM((ROWS * NX, NY), f32),
            pltpu.VMEM((16, 2, 2, ROWS, NY), f32),
            pltpu.VMEM((16, 2, ROWS, NY), f32),
            pltpu.VMEM((16, 2, ROWS, NY), f32),
            pltpu.VMEM((16, 2, ROWS, NY), f32),
            pltpu.VMEM((ROWS, 2, NY), f32),
            pltpu.VMEM((3, ROWS, 2, NY), f32),
            pltpu.VMEM((2, 2, ROWS, NY), f32),
            pltpu.VMEM((2, 4, 2, ROWS, NY), f32),
            pltpu.SemaphoreType.DMA((11,)),
            pltpu.SemaphoreType.DMA((STEPS, 2, 2)),
            pltpu.SemaphoreType.DMA((STEPS, 2, 2)),
            pltpu.SemaphoreType.DMA((2,)),
            pltpu.SemaphoreType.DMA((16,)),
            pltpu.SemaphoreType.DMA((16,)),
            pltpu.SemaphoreType.DMA((2, 4)),
            pltpu.SemaphoreType.DMA((2, 4)),
            pltpu.SemaphoreType.REGULAR((2,)),
        ],
        compiler_params=pltpu.CompilerParams(collective_id=0, has_side_effects=True, vmem_limit_bytes=16 * 2**20),
    )(
        *(
            pltpu.with_memory_space_constraint(operand, pltpu.HBM)
            for operand in (
                source_cells,
                source_codes,
                wavelets.T,
                velocity,
                wave_state,
                receiver_cells,
                residuals,
                momentum,
                diffusivity,
            )
        )
    )


def solution(mesh):
    return jax.shard_map(
        on_device,
        mesh=mesh,
        in_specs=(
            P("slab", None, None),
            P(None, "shot", None, "slab", None, None),
            P("shot", None),
            P("shot", None),
            P(),
            P("shot", None),
            P("shot", None, None),
            P("slab", "shot", None),
            P(None, "slab", "shot", None),
        ),
        out_specs=(
            P("shot", None, "slab", None, None),
            P("slab", "shot", None),
            P("slab", "shot", None),
        ),
        check_vma=False,
    )
```

```python
import math

import jax
import jax.numpy as jnp
from jax import lax
from jax.experimental import pallas as pl
from jax.experimental.pallas import tpu as pltpu
from jax.sharding import PartitionSpec as P

TAPS = (-205.0 / 72.0, 8.0 / 5.0, -1.0 / 5.0, 8.0 / 315.0, -1.0 / 560.0)
MESH = pl.DeviceIdType.MESH
ROWS, NX, NY = 8, 64, 128
SLABS, SHOTS = 32, 32
STEPS = 2
PLANE = NX * NY
SCALE = math.sqrt(SHOTS * STEPS)


def shifted(plane, offset, axis, index):
    size = plane.shape[axis]
    rolled = pltpu.roll(plane, (-offset) % size, axis)
    keep = index < size - offset if offset > 0 else index >= -offset
    return jnp.where(keep, rolled, 0.0)


def lateral(plane):
    along_x = lax.broadcasted_iota(jnp.int32, plane.shape, 0)
    along_y = lax.broadcasted_iota(jnp.int32, plane.shape, 1)
    total = (3.0 * TAPS[0]) * plane
    for r in range(1, 5):
        pairs = shifted(plane, r, 0, along_x) + shifted(plane, -r, 0, along_x)
        pairs = pairs + shifted(plane, r, 1, along_y) + shifted(plane, -r, 1, along_y)
        total = total + TAPS[r] * pairs
    return total


def kernel(
    src_cells_hbm,
    src_codes_hbm,
    wavelets_hbm,
    velocity,
    waves,
    rec_cells_hbm,
    residuals_hbm,
    momentum,
    diffusivity,
    fields,
    new_momentum,
    new_velocity,
    src_cells,
    src_codes,
    wavelets,
    ext,
    prev,
    vel,
    lat,
    inject,
    rec_cells,
    residuals,
    spread,
    image,
    image_t,
    pair_in,
    pair_sum,
    group_in,
    mom,
    dif,
    dif_t,
    dif_pack,
    dif_side,
    dif_edge,
    held,
    beyond_z,
    beyond_x,
    corner,
    load_sem,
    halo_send,
    halo_recv,
    pair_sem,
    group_send,
    group_recv,
    dif_send,
    dif_recv,
    near_send,
    near_recv,
    ready,
):
    shot = lax.axis_index("shot")
    slab = lax.axis_index("slab")
    cx, cy, core = shot // 8, (shot // 2) % 4, shot % 2
    above, below = slab + 1, slab - 1
    left, right = shot - 1, shot + 1
    has_above, has_below = slab < SLABS - 1, slab > 0
    has_left, has_right = shot > 0, shot < SHOTS - 1

    def at(x, y, c):
        return (x % 4) * 8 + (y % 4) * 2 + c

    partners = [(at(cx, cy, 1 - core), slab)]
    partners += [(at(cx, cy + d, core), slab) for d in (1, 3)]
    partners += [(at(cx + d, cy, core), slab) for d in (1, 2, 3)]

    loads = [
        pltpu.make_async_copy(waves.at[1, 0, 0], ext.at[0, 0, pl.ds(4, ROWS)], load_sem.at[0]),
        pltpu.make_async_copy(waves.at[1, 0, 1], ext.at[0, 1, pl.ds(4, ROWS)], load_sem.at[1]),
        pltpu.make_async_copy(rec_cells_hbm, rec_cells, load_sem.at[2]),
        pltpu.make_async_copy(residuals_hbm, residuals, load_sem.at[3]),
        pltpu.make_async_copy(velocity, vel, load_sem.at[4]),
        pltpu.make_async_copy(waves.at[0, 0], prev, load_sem.at[5]),
        pltpu.make_async_copy(momentum, mom, load_sem.at[6]),
        pltpu.make_async_copy(diffusivity, dif, load_sem.at[7]),
        pltpu.make_async_copy(src_cells_hbm, src_cells, load_sem.at[8]),
        pltpu.make_async_copy(src_codes_hbm, src_codes, load_sem.at[9]),
        pltpu.make_async_copy(wavelets_hbm, wavelets, load_sem.at[10]),
    ]
    barrier = pltpu.get_barrier_semaphore()

    def greet(semaphore):
        for partner in partners:
            pl.semaphore_signal(semaphore, inc=1, device_id=partner, device_id_type=MESH)

    def meet(target):
        pl.semaphore_signal(barrier, inc=1, device_id=(shot, target), device_id_type=MESH)

    pl.when(has_above)(lambda: meet(above))
    pl.when(has_below)(lambda: meet(below))
    greet(barrier)
    for load in loads:
        load.start()

    @pl.when(slab == 0)
    def _():
        ext[:, :, pl.ds(0, 4)] = jnp.zeros((STEPS, 2, 4, NX, NY), jnp.float32)
        beyond_z[0] = jnp.zeros((2, ROWS, NY), jnp.float32)
        corner[0] = jnp.zeros((2, ROWS, NY), jnp.float32)

    @pl.when(slab == SLABS - 1)
    def _():
        ext[:, :, pl.ds(12, 4)] = jnp.zeros((STEPS, 2, 4, NX, NY), jnp.float32)
        beyond_z[1] = jnp.zeros((2, ROWS, NY), jnp.float32)
        corner[1] = jnp.zeros((2, ROWS, NY), jnp.float32)

    @pl.when(shot == 0)
    def _():
        beyond_x[0] = jnp.zeros((2, ROWS, NY), jnp.float32)
        corner[:, 0] = jnp.zeros((2, ROWS, NY), jnp.float32)

    @pl.when(shot == SHOTS - 1)
    def _():
        beyond_x[1] = jnp.zeros((2, ROWS, NY), jnp.float32)
        corner[:, 1] = jnp.zeros((2, ROWS, NY), jnp.float32)

    pl.semaphore_wait(
        barrier,
        len(partners) + has_above.astype(jnp.int32) + has_below.astype(jnp.int32),
    )

    def halo(step, field):
        copies = []
        for way, (target, first, landing) in enumerate(((above, 4, 0), (below, 0, 12))):
            if step == 0:
                source = waves.at[1, 0, field, pl.ds(first, 4)]
            else:
                source = ext.at[1, field, pl.ds(4 + first, 4)]
            copies.append(
                pltpu.make_async_remote_copy(
                    src_ref=source,
                    dst_ref=ext.at[step, field, pl.ds(landing, 4)],
                    send_sem=halo_send.at[step, field, way],
                    recv_sem=halo_recv.at[step, field, way],
                    device_id=(shot, target),
                    device_id_type=MESH,
                )
            )
        return copies

    def start(copies):
        pl.when(has_above)(copies[0].start)
        pl.when(has_below)(copies[1].start)

    def arrive(copies):
        pl.when(has_below)(copies[0].wait_recv)
        pl.when(has_above)(copies[1].wait_recv)

    def leave(copies):
        pl.when(has_above)(copies[0].wait_send)
        pl.when(has_below)(copies[1].wait_send)

    u0, q0 = halo(0, 0), halo(0, 1)
    start(u0)
    start(q0)
    greet(ready.at[0])

    def near_part(step, field):
        def body(z, carry):
            lat[field, z] = lateral(ext[step, field, 4 + z])
            return carry

        lax.fori_loop(0, ROWS, body, 0)

    def advance(step, field):
        def body(z, carry):
            now = ext[step, field, 4 + z]
            total = lat[field, z] + inject[field, step, z]
            for r in range(1, 5):
                total = total + TAPS[r] * (
                    ext[step, field, 4 + z + r] + ext[step, field, 4 + z - r]
                )
            drive = (vel[z] * vel[z]) * total
            before = prev[field, z] if step == 0 else ext[0, field, 4 + z]
            after = 2.0 * now - before + drive
            if step == 0:
                ext[1, field, 4 + z] = after
            else:
                fields[0, field, z] = after
            if field == 0:
                rows = pl.ds(pl.multiple_of(z * NX, NX), NX)
                product = drive * ext[step, 1, 4 + z]
                image[rows, :] = product if step == 0 else image[rows, :] + product
            return carry

        lax.fori_loop(0, ROWS, body, 0)

    for load in loads[8:]:
        load.wait()
    base = slab * (ROWS * PLANE)
    cells = [src_cells[0, k] - base for k in range(4)]
    amounts = [[wavelets[t, src_codes[0, k]] for k in range(4)] for t in range(STEPS)]

    def source_row(z, carry):
        cell = lax.broadcasted_iota(jnp.int32, (NX, NY), 0) * NY
        cell = cell + lax.broadcasted_iota(jnp.int32, (NX, NY), 1) + z * PLANE
        grids = [jnp.zeros((NX, NY), jnp.float32) for _ in range(STEPS)]
        for k in range(4):
            here = cell == cells[k]
            for t in range(STEPS):
                grids[t] = grids[t] + jnp.where(here, amounts[t][k], 0.0)
        for t in range(STEPS):
            inject[0, t, z] = grids[t]
        return carry

    lax.fori_loop(0, ROWS, source_row, 0)

    loads[0].wait()
    near_part(0, 0)
    pl.semaphore_wait(ready.at[0], len(partners))
    greet(ready.at[1])

    loads[2].wait()
    loads[3].wait()
    cell = rec_cells[...] - base
    line = cell >> 7
    lane = cell & (NY - 1)
    count = cell.shape[1]
    for t in range(STEPS):
        here = lax.broadcasted_iota(jnp.int32, (NY, count), 0) == lane
        rest = jnp.where(here, residuals[0, pl.ds(t, 1), :], 0.0)
        for part in range(3):
            piece = rest.astype(jnp.bfloat16)
            spread[part, pl.ds(t * NY, NY), :] = piece
            rest = rest - piece.astype(jnp.float32)

    def receiver_row(z, carry):
        here = lax.broadcasted_iota(jnp.int32, (NX, count), 0) + z * NX == line
        chosen = jnp.where(here, 1.0, 0.0).astype(jnp.bfloat16)
        grid = jnp.zeros((NX, STEPS * NY), jnp.float32)
        for part in range(3):
            grid = grid + lax.dot_general(
                chosen,
                spread[part],
                (((1,), (1,)), ((), ())),
                preferred_element_type=jnp.float32,
            )
        for t in range(STEPS):
            inject[1, t, z] = grid[:, t * NY : (t + 1) * NY]
        return carry

    lax.fori_loop(0, ROWS, receiver_row, 0)
    pl.semaphore_wait(ready.at[1], len(partners))

    loads[6].wait()
    loads[7].wait()
    dif_pack[...] = jnp.zeros((2, ROWS, NY), jnp.float32)
    for i in range(2):
        for k in range(3):
            tile = dif[k, :, i, :]
            dif_t[i, k] = tile
            dif_pack[0, pl.ds(3 * i + k, 1), :] = tile[ROWS - 1 :]
            dif_pack[1, pl.ds(3 * i + k, 1), :] = tile[:1]

    def near(source, landing, send_sem, recv_sem, target, goes, comes):
        copy = pltpu.make_async_remote_copy(
            src_ref=source,
            dst_ref=landing,
            send_sem=send_sem,
            recv_sem=recv_sem,
            device_id=target,
            device_id_type=MESH,
        )
        return copy, goes, comes

    dif_ways = [
        (dif_pack.at[0], dif_edge.at[0], (shot, above), has_above, has_below),
        (dif_pack.at[1], dif_edge.at[1], (shot, below), has_below, has_above),
        (dif_t.at[1], dif_side.at[0], (right, slab), has_right, has_left),
        (dif_t.at[0], dif_side.at[1], (left, slab), has_left, has_right),
    ]
    dif_copies = [
        near(source, landing, dif_send.at[n], dif_recv.at[n], target, goes, comes)
        for n, (source, landing, target, goes, comes) in enumerate(dif_ways)
    ]
    near_ways = [
        (held, beyond_z.at[0], (shot, above), has_above, has_below),
        (held, beyond_z.at[1], (shot, below), has_below, has_above),
        (held, beyond_x.at[0], (right, slab), has_right, has_left),
        (held, beyond_x.at[1], (left, slab), has_left, has_right),
        (held.at[1], corner.at[0, 0], (right, above), has_right & has_above, has_left & has_below),
        (held.at[0], corner.at[0, 1], (left, above), has_left & has_above, has_right & has_below),
        (held.at[1], corner.at[1, 0], (right, below), has_right & has_below, has_left & has_above),
        (held.at[0], corner.at[1, 1], (left, below), has_left & has_below, has_right & has_above),
    ]
    near_copies = [
        near(source, landing, near_send.at[n], near_recv.at[n], target, goes, comes)
        for n, (source, landing, target, goes, comes) in enumerate(near_ways)
    ]

    loads[1].wait()
    near_part(0, 1)
    loads[4].wait()
    loads[5].wait()

    arrive(u0)
    advance(0, 0)
    u1 = halo(1, 0)
    start(u1)
    for copy, goes, _ in dif_copies:
        pl.when(goes)(copy.start)
    near_part(1, 0)

    arrive(q0)
    advance(0, 1)
    q1 = halo(1, 1)
    pl.when(has_above)(q1[0].start)

    arrive(u1)
    advance(1, 0)

    def turn(i, carry):
        for inner in range(4):
            strip = image[pl.ds(i * 4 + inner, ROWS, stride=NX), :]
            image_t[i, inner // 2, inner % 2] = strip
        return carry

    lax.fori_loop(0, NX // 4, turn, 0)
    pair = pltpu.make_async_remote_copy(
        src_ref=image_t.at[:, 1 - core],
        dst_ref=pair_in,
        send_sem=pair_sem.at[0],
        recv_sem=pair_sem.at[1],
        device_id=(at(cx, cy, 1 - core), slab),
        device_id_type=MESH,
    )
    pair.start()
    near_part(1, 1)
    pair.wait_recv()

    def join(i, carry):
        pair_sum[i] = image_t[i, core] + pair_in[i]
        return carry

    lax.fori_loop(0, 16, join, 0)

    def group(k):
        tx, ty = (cx + k // 4) % 4, (cy + k % 4) % 4
        return pltpu.make_async_remote_copy(
            src_ref=pair_sum.at[tx * 4 + ty],
            dst_ref=group_in.at[k],
            send_sem=group_send.at[k],
            recv_sem=group_recv.at[k],
            device_id=(at(tx, ty, core), slab),
            device_id_type=MESH,
        )

    def send_group(k, carry):
        group(k).start()
        return carry

    lax.fori_loop(1, 16, send_group, 0)
    pl.when(has_below)(q1[1].start)

    arrive(q1)
    advance(1, 1)
    for copy, _, comes in dif_copies:
        pl.when(comes)(copy.wait_recv)

    def take_group(k, total):
        group(k).wait_recv()
        return total + group_in[k]

    total = lax.fori_loop(1, 16, take_group, pair_sum[cx * 4 + cy])

    depth = lax.broadcasted_iota(jnp.int32, (ROWS, NY), 0)
    along_y = lax.broadcasted_iota(jnp.int32, (ROWS, NY), 1)
    speed = []
    smooth = []
    for i in range(2):
        rows = [vel[z, pl.ds(shot * 2 + i, 1), :] for z in range(ROWS)]
        speed.append(jnp.concatenate(rows, axis=0))
        smooth.append((-0.2 * total[i]) / (speed[i] * SCALE))
    for i in range(2):
        held[i] = smooth[i]
    for n in (4, 5, 6, 7, 2, 3, 0, 1):
        copy, goes, _ = near_copies[n]
        pl.when(goes)(copy.start)

    def step(centre, down, up, before, after, kappas):
        sides = shifted(centre, 1, 1, along_y) + shifted(centre, -1, 1, along_y)
        return (
            centre
            + kappas[0] * (up - 2.0 * centre + down)
            + kappas[1] * (after - 2.0 * centre + before)
            + kappas[2] * (sides - 2.0 * centre)
        )

    def down_of(centre, low):
        return jnp.where(depth == 0, pltpu.roll(low, 1, 0), pltpu.roll(centre, 1, 0))

    def up_of(centre, high):
        last = ROWS - 1
        return jnp.where(depth == last, pltpu.roll(high, last, 0), pltpu.roll(centre, last, 0))

    own = [[dif_t[i, k] for k in range(3)] for i in range(2)]
    side = [[dif_side[i, k] for k in range(3)] for i in range(2)]
    edge = [
        [
            [jnp.broadcast_to(dif_edge[z, pl.ds(3 * i + k, 1), :], (ROWS, NY)) for k in range(3)]
            for i in range(2)
        ]
        for z in range(2)
    ]
    for copy, _, comes in near_copies:
        pl.when(comes)(copy.wait_recv)
    low, high = [[beyond_z[z, i] for i in range(2)] for z in range(2)]
    (far_left, near_left), (near_right, far_right) = [
        [beyond_x[x, i] for i in range(2)] for x in range(2)
    ]
    (low_left, low_right), (high_left, high_right) = [
        [corner[z, x] for x in range(2)] for z in range(2)
    ]
    before = [near_left, smooth[0]]
    after = [smooth[1], near_right]
    once = [
        step(
            smooth[i],
            down_of(smooth[i], low[i]),
            up_of(smooth[i], high[i]),
            before[i],
            after[i],
            own[i],
        )
        for i in range(2)
    ]
    once_left = step(
        near_left,
        down_of(near_left, low_left),
        up_of(near_left, high_left),
        far_left,
        smooth[0],
        side[0],
    )
    once_right = step(
        near_right,
        down_of(near_right, low_right),
        up_of(near_right, high_right),
        smooth[1],
        far_right,
        side[1],
    )
    once_left = jnp.where(has_left, once_left, 0.0)
    once_right = jnp.where(has_right, once_right, 0.0)
    low_before, low_after = [low_left, low[0]], [low[1], low_right]
    high_before, high_after = [high_left, high[0]], [high[1], high_right]
    last = ROWS - 1
    twice = []
    for i in range(2):
        once_low = step(
            low[i],
            pltpu.roll(low[i], 1, 0),
            up_of(low[i], smooth[i]),
            low_before[i],
            low_after[i],
            edge[0][i],
        )
        once_high = step(
            high[i],
            down_of(high[i], smooth[i]),
            pltpu.roll(high[i], last, 0),
            high_before[i],
            high_after[i],
            edge[1][i],
        )
        once_low = jnp.where(has_below, once_low, 0.0)
        once_high = jnp.where(has_above, once_high, 0.0)
        twice.append(
            step(
                once[i],
                down_of(once[i], once_low),
                up_of(once[i], once_high),
                once_left if i == 0 else once[0],
                once[1] if i == 0 else once_right,
                own[i],
            )
        )
    smooth = twice
    for i in range(2):
        updated = 0.9 * mom[:, i, :] + smooth[i]
        new_momentum[:, i, :] = updated
        new_velocity[:, i, :] = speed[i] - 0.02 * updated

    for copies in (u0, q0, u1, q1):
        leave(copies)
    pair.wait_send()
    for copy, goes, _ in dif_copies + near_copies:
        pl.when(goes)(copy.wait_send)

    def drain_group(k, carry):
        group(k).wait_send()
        return carry

    lax.fori_loop(1, 16, drain_group, 0)


def store(*refs):
    sources, targets, sem = refs[:3], refs[3:6], refs[6]
    copies = [
        pltpu.make_async_copy(source, target, sem.at[n])
        for n, (source, target) in enumerate(zip(sources, targets))
    ]
    for copy in copies:
        copy.start()
    for copy in copies:
        copy.wait()


def on_device(
    velocity,
    wave_state,
    source_cells,
    source_codes,
    wavelets,
    receiver_cells,
    residuals,
    momentum,
    diffusivity,
):
    hbm = pl.BlockSpec(memory_space=pltpu.HBM)
    vmem = pl.BlockSpec(memory_space=pltpu.VMEM)
    f32 = jnp.float32
    results = (
        jax.ShapeDtypeStruct((1, 2, ROWS, NX, NY), f32),
        jax.ShapeDtypeStruct((ROWS, 2, NY), f32),
        jax.ShapeDtypeStruct((ROWS, 2, NY), f32),
    )
    held = pl.pallas_call(
        kernel,
        out_shape=results,
        in_specs=[hbm] * 9,
        out_specs=(vmem, vmem, vmem),
        scratch_shapes=[
            pltpu.SMEM(source_cells.shape, jnp.int32),
            pltpu.SMEM(source_codes.shape, jnp.int32),
            pltpu.SMEM(wavelets.shape[::-1], f32),
            pltpu.VMEM((STEPS, 2, 16, NX, NY), f32),
            pltpu.VMEM((2, ROWS, NX, NY), f32),
            pltpu.VMEM((ROWS, NX, NY), f32),
            pltpu.VMEM((2, ROWS, NX, NY), f32),
            pltpu.VMEM((2, STEPS, ROWS, NX, NY), f32),
            pltpu.VMEM(receiver_cells.shape, jnp.int32),
            pltpu.VMEM(residuals.shape, f32),
            pltpu.VMEM((3, STEPS * NY, receiver_cells.shape[1]), jnp.bfloat16),
            pltpu.VMEM((ROWS * NX, NY), f32),
            pltpu.VMEM((16, 2, 2, ROWS, NY), f32),
            pltpu.VMEM((16, 2, ROWS, NY), f32),
            pltpu.VMEM((16, 2, ROWS, NY), f32),
            pltpu.VMEM((16, 2, ROWS, NY), f32),
            pltpu.VMEM((ROWS, 2, NY), f32),
            pltpu.VMEM((3, ROWS, 2, NY), f32),
            pltpu.VMEM((2, 3, ROWS, NY), f32),
            pltpu.VMEM((2, ROWS, NY), f32),
            pltpu.VMEM((2, 3, ROWS, NY), f32),
            pltpu.VMEM((2, ROWS, NY), f32),
            pltpu.VMEM((2, ROWS, NY), f32),
            pltpu.VMEM((2, 2, ROWS, NY), f32),
            pltpu.VMEM((2, 2, ROWS, NY), f32),
            pltpu.VMEM((2, 2, ROWS, NY), f32),
            pltpu.SemaphoreType.DMA((11,)),
            pltpu.SemaphoreType.DMA((STEPS, 2, 2)),
            pltpu.SemaphoreType.DMA((STEPS, 2, 2)),
            pltpu.SemaphoreType.DMA((2,)),
            pltpu.SemaphoreType.DMA((16,)),
            pltpu.SemaphoreType.DMA((16,)),
            pltpu.SemaphoreType.DMA((4,)),
            pltpu.SemaphoreType.DMA((4,)),
            pltpu.SemaphoreType.DMA((8,)),
            pltpu.SemaphoreType.DMA((8,)),
            pltpu.SemaphoreType.REGULAR((2,)),
        ],
        compiler_params=pltpu.CompilerParams(collective_id=0, has_side_effects=True, vmem_limit_bytes=16 * 2**20),
    )(
        *(
            pltpu.with_memory_space_constraint(operand, pltpu.HBM)
            for operand in (
                source_cells,
                source_codes,
                wavelets.T,
                velocity,
                wave_state,
                receiver_cells,
                residuals,
                momentum,
                diffusivity,
            )
        )
    )
    return pl.pallas_call(
        store,
        out_shape=results,
        in_specs=[vmem] * 3,
        out_specs=(hbm,) * 3,
        scratch_shapes=[pltpu.SemaphoreType.DMA((3,))],
        compiler_params=pltpu.CompilerParams(vmem_limit_bytes=2**20),
    )(*held)


def solution(mesh):
    return jax.shard_map(
        on_device,
        mesh=mesh,
        in_specs=(
            P("slab", None, None),
            P(None, "shot", None, "slab", None, None),
            P("shot", None),
            P("shot", None),
            P(),
            P("shot", None),
            P("shot", None, None),
            P("slab", "shot", None),
            P(None, "slab", "shot", None),
        ),
        out_specs=(
            P("shot", None, "slab", None, None),
            P("slab", "shot", None),
            P("slab", "shot", None),
        ),
        check_vma=False,
    )
```

```python
import math

import jax
import jax.numpy as jnp
from jax import lax
from jax.experimental import pallas as pl
from jax.experimental.pallas import tpu as pltpu
from jax.sharding import PartitionSpec as P

TAPS = (-205.0 / 72.0, 8.0 / 5.0, -1.0 / 5.0, 8.0 / 315.0, -1.0 / 560.0)
MESH = pl.DeviceIdType.MESH
ROWS, NX, NY = 8, 64, 128
SLABS, SHOTS = 32, 32
STEPS = 2
PLANE = NX * NY
SCALE = math.sqrt(SHOTS * STEPS)


def shifted(plane, offset, axis, index):
    size = plane.shape[axis]
    rolled = pltpu.roll(plane, (-offset) % size, axis)
    keep = index < size - offset if offset > 0 else index >= -offset
    return jnp.where(keep, rolled, 0.0)


def lateral(plane):
    along_x = lax.broadcasted_iota(jnp.int32, plane.shape, 0)
    along_y = lax.broadcasted_iota(jnp.int32, plane.shape, 1)
    total = (3.0 * TAPS[0]) * plane
    for r in range(1, 5):
        pairs = shifted(plane, r, 0, along_x) + shifted(plane, -r, 0, along_x)
        pairs = pairs + shifted(plane, r, 1, along_y) + shifted(plane, -r, 1, along_y)
        total = total + TAPS[r] * pairs
    return total


def kernel(
    src_cells_hbm,
    src_codes_hbm,
    wavelets_hbm,
    velocity,
    waves,
    rec_cells_hbm,
    residuals_hbm,
    momentum,
    diffusivity,
    fields,
    new_momentum,
    new_velocity,
    src_cells,
    src_codes,
    wavelets,
    ext,
    prev,
    vel,
    lat,
    inject,
    rec_cells,
    residuals,
    spread,
    image,
    pair_out,
    pair_in,
    pair_sum,
    group_in,
    mom,
    dif,
    dif_t,
    dif_pack,
    dif_side,
    dif_edge,
    held,
    beyond_z,
    beyond_x,
    corner,
    load_sem,
    halo_send,
    halo_recv,
    pair_sem,
    group_send,
    group_recv,
    dif_send,
    dif_recv,
    near_send,
    near_recv,
    ready,
):
    shot = lax.axis_index("shot")
    slab = lax.axis_index("slab")
    cx, cy, core = shot // 8, (shot // 2) % 4, shot % 2
    above, below = slab + 1, slab - 1
    left, right = shot - 1, shot + 1
    has_above, has_below = slab < SLABS - 1, slab > 0
    has_left, has_right = shot > 0, shot < SHOTS - 1

    def at(x, y, c):
        return (x % 4) * 8 + (y % 4) * 2 + c

    partners = [(at(cx, cy, 1 - core), slab)]
    partners += [(at(cx, cy + d, core), slab) for d in (1, 3)]
    partners += [(at(cx + d, cy, core), slab) for d in (1, 2, 3)]

    loads = [
        pltpu.make_async_copy(waves.at[1, 0, 0], ext.at[0, 0, pl.ds(4, ROWS)], load_sem.at[0]),
        pltpu.make_async_copy(waves.at[1, 0, 1], ext.at[0, 1, pl.ds(4, ROWS)], load_sem.at[1]),
        pltpu.make_async_copy(rec_cells_hbm, rec_cells, load_sem.at[2]),
        pltpu.make_async_copy(residuals_hbm, residuals, load_sem.at[3]),
        pltpu.make_async_copy(velocity, vel, load_sem.at[4]),
        pltpu.make_async_copy(waves.at[0, 0], prev, load_sem.at[5]),
        pltpu.make_async_copy(momentum, mom, load_sem.at[6]),
        pltpu.make_async_copy(diffusivity, dif, load_sem.at[7]),
        pltpu.make_async_copy(src_cells_hbm, src_cells, load_sem.at[8]),
        pltpu.make_async_copy(src_codes_hbm, src_codes, load_sem.at[9]),
        pltpu.make_async_copy(wavelets_hbm, wavelets, load_sem.at[10]),
    ]
    barrier = pltpu.get_barrier_semaphore()

    def greet(semaphore):
        for partner in partners:
            pl.semaphore_signal(semaphore, inc=1, device_id=partner, device_id_type=MESH)

    def meet(target):
        pl.semaphore_signal(barrier, inc=1, device_id=(shot, target), device_id_type=MESH)

    pl.when(has_above)(lambda: meet(above))
    pl.when(has_below)(lambda: meet(below))
    greet(barrier)
    for load in loads:
        load.start()

    @pl.when(slab == 0)
    def _():
        ext[:, :, pl.ds(0, 4)] = jnp.zeros((STEPS, 2, 4, NX, NY), jnp.float32)
        beyond_z[0] = jnp.zeros((2, ROWS, NY), jnp.float32)
        corner[0] = jnp.zeros((2, ROWS, NY), jnp.float32)

    @pl.when(slab == SLABS - 1)
    def _():
        ext[:, :, pl.ds(12, 4)] = jnp.zeros((STEPS, 2, 4, NX, NY), jnp.float32)
        beyond_z[1] = jnp.zeros((2, ROWS, NY), jnp.float32)
        corner[1] = jnp.zeros((2, ROWS, NY), jnp.float32)

    @pl.when(shot == 0)
    def _():
        beyond_x[0] = jnp.zeros((2, ROWS, NY), jnp.float32)
        corner[:, 0] = jnp.zeros((2, ROWS, NY), jnp.float32)

    @pl.when(shot == SHOTS - 1)
    def _():
        beyond_x[1] = jnp.zeros((2, ROWS, NY), jnp.float32)
        corner[:, 1] = jnp.zeros((2, ROWS, NY), jnp.float32)

    pl.semaphore_wait(
        barrier,
        len(partners) + has_above.astype(jnp.int32) + has_below.astype(jnp.int32),
    )

    def halo(step, field, half):
        across = pl.ds(half * (NX // 2), NX // 2)
        copies = []
        for way, (target, first, landing) in enumerate(((above, 4, 0), (below, 0, 12))):
            if step == 0:
                source = waves.at[1, 0, field, pl.ds(first, 4), across]
            else:
                source = ext.at[1, field, pl.ds(4 + first, 4), across]
            copies.append(
                pltpu.make_async_remote_copy(
                    src_ref=source,
                    dst_ref=ext.at[step, field, pl.ds(landing, 4), across],
                    send_sem=halo_send.at[step, field, half, way],
                    recv_sem=halo_recv.at[step, field, half, way],
                    device_id=(shot, target),
                    device_id_type=MESH,
                )
            )
        return copies

    def start(copies):
        pl.when(has_above)(copies[0].start)
        pl.when(has_below)(copies[1].start)

    def arrive(copies):
        pl.when(has_below)(copies[0].wait_recv)
        pl.when(has_above)(copies[1].wait_recv)

    def leave(copies):
        pl.when(has_above)(copies[0].wait_send)
        pl.when(has_below)(copies[1].wait_send)

    (u0, q0), (u1, q1) = [
        [[halo(step, field, half) for half in range(2)] for field in range(2)]
        for step in range(STEPS)
    ]
    for copies in u0 + q0:
        start(copies)
    greet(ready.at[0])

    def near_part(step, field):
        def body(z, carry):
            lat[field, z] = lateral(ext[step, field, 4 + z])
            return carry

        lax.fori_loop(0, ROWS, body, 0)

    def advance(step, field, first=0, count=NX):
        across = pl.ds(first, count)

        def body(z, carry):
            now = ext[step, field, 4 + z, across]
            total = lat[field, z, across] + inject[field, step, z, across]
            for r in range(1, 5):
                total = total + TAPS[r] * (
                    ext[step, field, 4 + z + r, across] + ext[step, field, 4 + z - r, across]
                )
            speed_here = vel[z, across]
            drive = (speed_here * speed_here) * total
            before = prev[field, z, across] if step == 0 else ext[0, field, 4 + z, across]
            after = 2.0 * now - before + drive
            if step == 0:
                ext[1, field, 4 + z, across] = after
            else:
                fields[0, field, z, across] = after
            if field == 0:
                rows = pl.ds(pl.multiple_of(z * NX + first, NX // 2), count)
                product = drive * ext[step, 1, 4 + z, across]
                image[rows, :] = product if step == 0 else image[rows, :] + product
            return carry

        lax.fori_loop(0, ROWS, body, 0)

    for load in loads[8:]:
        load.wait()
    base = slab * (ROWS * PLANE)
    cells = [src_cells[0, k] - base for k in range(4)]
    amounts = [[wavelets[t, src_codes[0, k]] for k in range(4)] for t in range(STEPS)]

    def source_row(z, carry):
        cell = lax.broadcasted_iota(jnp.int32, (NX, NY), 0) * NY
        cell = cell + lax.broadcasted_iota(jnp.int32, (NX, NY), 1) + z * PLANE
        grids = [jnp.zeros((NX, NY), jnp.float32) for _ in range(STEPS)]
        for k in range(4):
            here = cell == cells[k]
            for t in range(STEPS):
                grids[t] = grids[t] + jnp.where(here, amounts[t][k], 0.0)
        for t in range(STEPS):
            inject[0, t, z] = grids[t]
        return carry

    lax.fori_loop(0, ROWS, source_row, 0)

    loads[0].wait()
    near_part(0, 0)
    pl.semaphore_wait(ready.at[0], len(partners))
    greet(ready.at[1])

    loads[2].wait()
    loads[3].wait()
    cell = rec_cells[...] - base
    line = cell >> 7
    lane = cell & (NY - 1)
    count = cell.shape[1]
    for t in range(STEPS):
        here = lax.broadcasted_iota(jnp.int32, (NY, count), 0) == lane
        rest = jnp.where(here, residuals[0, pl.ds(t, 1), :], 0.0)
        for part in range(3):
            piece = rest.astype(jnp.bfloat16)
            spread[part, pl.ds(t * NY, NY), :] = piece
            rest = rest - piece.astype(jnp.float32)

    def receiver_row(z, carry):
        here = lax.broadcasted_iota(jnp.int32, (NX, count), 0) + z * NX == line
        chosen = jnp.where(here, 1.0, 0.0).astype(jnp.bfloat16)
        grid = jnp.zeros((NX, STEPS * NY), jnp.float32)
        for part in range(3):
            grid = grid + lax.dot_general(
                chosen,
                spread[part],
                (((1,), (1,)), ((), ())),
                preferred_element_type=jnp.float32,
            )
        for t in range(STEPS):
            inject[1, t, z] = grid[:, t * NY : (t + 1) * NY]
        return carry

    lax.fori_loop(0, ROWS, receiver_row, 0)
    pl.semaphore_wait(ready.at[1], len(partners))

    loads[6].wait()
    loads[7].wait()
    dif_pack[...] = jnp.zeros((2, ROWS, NY), jnp.float32)
    for i in range(2):
        for k in range(3):
            tile = dif[k, :, i, :]
            dif_t[i, k] = tile
            dif_pack[0, pl.ds(3 * i + k, 1), :] = tile[ROWS - 1 :]
            dif_pack[1, pl.ds(3 * i + k, 1), :] = tile[:1]

    def near(source, landing, send_sem, recv_sem, target, goes, comes):
        copy = pltpu.make_async_remote_copy(
            src_ref=source,
            dst_ref=landing,
            send_sem=send_sem,
            recv_sem=recv_sem,
            device_id=target,
            device_id_type=MESH,
        )
        return copy, goes, comes

    dif_ways = [
        (dif_pack.at[0], dif_edge.at[0], (shot, above), has_above, has_below),
        (dif_pack.at[1], dif_edge.at[1], (shot, below), has_below, has_above),
        (dif_t.at[1], dif_side.at[0], (right, slab), has_right, has_left),
        (dif_t.at[0], dif_side.at[1], (left, slab), has_left, has_right),
    ]
    dif_copies = [
        near(source, landing, dif_send.at[n], dif_recv.at[n], target, goes, comes)
        for n, (source, landing, target, goes, comes) in enumerate(dif_ways)
    ]
    near_ways = [
        (held, beyond_z.at[0], (shot, above), has_above, has_below),
        (held, beyond_z.at[1], (shot, below), has_below, has_above),
        (held, beyond_x.at[0], (right, slab), has_right, has_left),
        (held, beyond_x.at[1], (left, slab), has_left, has_right),
        (held.at[1], corner.at[0, 0], (right, above), has_right & has_above, has_left & has_below),
        (held.at[0], corner.at[0, 1], (left, above), has_left & has_above, has_right & has_below),
        (held.at[1], corner.at[1, 0], (right, below), has_right & has_below, has_left & has_above),
        (held.at[0], corner.at[1, 1], (left, below), has_left & has_below, has_right & has_above),
    ]
    near_copies = [
        near(source, landing, near_send.at[n], near_recv.at[n], target, goes, comes)
        for n, (source, landing, target, goes, comes) in enumerate(near_ways)
    ]

    loads[1].wait()
    near_part(0, 1)
    loads[4].wait()
    loads[5].wait()

    for copies in u0:
        arrive(copies)
    advance(0, 0)
    for copies in u1:
        start(copies)
    for copy, goes, _ in dif_copies:
        pl.when(goes)(copy.start)
    near_part(1, 0)

    for copies in q0:
        arrive(copies)
    advance(0, 1)
    pl.when(has_above)(q1[0][0].start)
    near_part(1, 1)

    def strip(i, c, r):
        return image[pl.ds(i * 4 + c * 2 + r, ROWS, stride=NX), :]

    def pair(half):
        groups = pl.ds(8 * half, 8)
        return pltpu.make_async_remote_copy(
            src_ref=pair_out.at[groups],
            dst_ref=pair_in.at[groups],
            send_sem=pair_sem.at[0, half],
            recv_sem=pair_sem.at[1, half],
            device_id=(at(cx, cy, 1 - core), slab),
            device_id_type=MESH,
        )

    def group(k):
        tx, ty = (cx + k // 4) % 4, (cy + k % 4) % 4
        return pltpu.make_async_remote_copy(
            src_ref=pair_sum.at[tx * 4 + ty],
            dst_ref=group_in.at[k],
            send_sem=group_send.at[k],
            recv_sem=group_recv.at[k],
            device_id=(at(tx, ty, core), slab),
            device_id_type=MESH,
        )

    for half in range(2):
        arrive(u1[half])
        advance(1, 0, half * (NX // 2), NX // 2)

        def part(i, carry):
            for r in range(2):
                pair_out[i, r] = strip(i, 1 - core, r)
            return carry

        lax.fori_loop(8 * half, 8 * half + 8, part, 0, unroll=2)
        pair(half).start()
        pair(half).wait_recv()

        def join(i, carry):
            for r in range(2):
                pair_sum[i, r] = strip(i, core, r) + pair_in[i, r]
            return carry

        lax.fori_loop(8 * half, 8 * half + 8, join, 0, unroll=2)
        for dy in (2, 1, 3, 0):
            for tx in (2 * half, 2 * half + 1):
                k = ((tx + 4 - cx) % 4) * 4 + dy
                if dy == 0:
                    pl.when(tx != cx)(group(k).start)
                else:
                    group(k).start()
    pl.when(has_below)(q1[0][1].start)
    start(q1[1])
    for copy, _, comes in dif_copies:
        pl.when(comes)(copy.wait_recv)

    def take_group(k, total):
        group(k).wait_recv()
        return total + group_in[k]

    total = lax.fori_loop(1, 16, take_group, pair_sum[cx * 4 + cy])

    depth = lax.broadcasted_iota(jnp.int32, (ROWS, NY), 0)
    along_y = lax.broadcasted_iota(jnp.int32, (ROWS, NY), 1)
    speed = []
    smooth = []
    for i in range(2):
        rows = [vel[z, pl.ds(shot * 2 + i, 1), :] for z in range(ROWS)]
        speed.append(jnp.concatenate(rows, axis=0))
        smooth.append((-0.2 * total[i]) / (speed[i] * SCALE))
    for i in range(2):
        held[i] = smooth[i]
    for n in (4, 5, 6, 7, 2, 3, 0, 1):
        copy, goes, _ = near_copies[n]
        pl.when(goes)(copy.start)

    for copies in q1:
        arrive(copies)
    advance(1, 1)

    def step(centre, down, up, before, after, kappas):
        sides = shifted(centre, 1, 1, along_y) + shifted(centre, -1, 1, along_y)
        return (
            centre
            + kappas[0] * (up - 2.0 * centre + down)
            + kappas[1] * (after - 2.0 * centre + before)
            + kappas[2] * (sides - 2.0 * centre)
        )

    def down_of(centre, low):
        return jnp.where(depth == 0, pltpu.roll(low, 1, 0), pltpu.roll(centre, 1, 0))

    def up_of(centre, high):
        last = ROWS - 1
        return jnp.where(depth == last, pltpu.roll(high, last, 0), pltpu.roll(centre, last, 0))

    own = [[dif_t[i, k] for k in range(3)] for i in range(2)]
    side = [[dif_side[i, k] for k in range(3)] for i in range(2)]
    edge = [
        [
            [jnp.broadcast_to(dif_edge[z, pl.ds(3 * i + k, 1), :], (ROWS, NY)) for k in range(3)]
            for i in range(2)
        ]
        for z in range(2)
    ]
    for copy, _, comes in near_copies:
        pl.when(comes)(copy.wait_recv)
    low, high = [[beyond_z[z, i] for i in range(2)] for z in range(2)]
    (far_left, near_left), (near_right, far_right) = [
        [beyond_x[x, i] for i in range(2)] for x in range(2)
    ]
    (low_left, low_right), (high_left, high_right) = [
        [corner[z, x] for x in range(2)] for z in range(2)
    ]
    before = [near_left, smooth[0]]
    after = [smooth[1], near_right]
    once = [
        step(
            smooth[i],
            down_of(smooth[i], low[i]),
            up_of(smooth[i], high[i]),
            before[i],
            after[i],
            own[i],
        )
        for i in range(2)
    ]
    once_left = step(
        near_left,
        down_of(near_left, low_left),
        up_of(near_left, high_left),
        far_left,
        smooth[0],
        side[0],
    )
    once_right = step(
        near_right,
        down_of(near_right, low_right),
        up_of(near_right, high_right),
        smooth[1],
        far_right,
        side[1],
    )
    once_left = jnp.where(has_left, once_left, 0.0)
    once_right = jnp.where(has_right, once_right, 0.0)
    low_before, low_after = [low_left, low[0]], [low[1], low_right]
    high_before, high_after = [high_left, high[0]], [high[1], high_right]
    last = ROWS - 1
    twice = []
    for i in range(2):
        once_low = step(
            low[i],
            pltpu.roll(low[i], 1, 0),
            up_of(low[i], smooth[i]),
            low_before[i],
            low_after[i],
            edge[0][i],
        )
        once_high = step(
            high[i],
            down_of(high[i], smooth[i]),
            pltpu.roll(high[i], last, 0),
            high_before[i],
            high_after[i],
            edge[1][i],
        )
        once_low = jnp.where(has_below, once_low, 0.0)
        once_high = jnp.where(has_above, once_high, 0.0)
        twice.append(
            step(
                once[i],
                down_of(once[i], once_low),
                up_of(once[i], once_high),
                once_left if i == 0 else once[0],
                once[1] if i == 0 else once_right,
                own[i],
            )
        )
    smooth = twice
    for i in range(2):
        updated = 0.9 * mom[:, i, :] + smooth[i]
        new_momentum[:, i, :] = updated
        new_velocity[:, i, :] = speed[i] - 0.02 * updated

    for copies in u0 + q0 + u1 + q1:
        leave(copies)
    for half in range(2):
        pair(half).wait_send()
    for copy, goes, _ in dif_copies + near_copies:
        pl.when(goes)(copy.wait_send)

    def drain_group(k, carry):
        group(k).wait_send()
        return carry

    lax.fori_loop(1, 16, drain_group, 0)


def store(*refs):
    sources, targets, sem = refs[:3], refs[3:6], refs[6]
    copies = [
        pltpu.make_async_copy(source, target, sem.at[n])
        for n, (source, target) in enumerate(zip(sources, targets))
    ]
    for copy in copies:
        copy.start()
    for copy in copies:
        copy.wait()


def on_device(
    velocity,
    wave_state,
    source_cells,
    source_codes,
    wavelets,
    receiver_cells,
    residuals,
    momentum,
    diffusivity,
):
    hbm = pl.BlockSpec(memory_space=pltpu.HBM)
    vmem = pl.BlockSpec(memory_space=pltpu.VMEM)
    f32 = jnp.float32
    results = (
        jax.ShapeDtypeStruct((1, 2, ROWS, NX, NY), f32),
        jax.ShapeDtypeStruct((ROWS, 2, NY), f32),
        jax.ShapeDtypeStruct((ROWS, 2, NY), f32),
    )
    held = pl.pallas_call(
        kernel,
        out_shape=results,
        in_specs=[hbm] * 9,
        out_specs=(vmem, vmem, vmem),
        scratch_shapes=[
            pltpu.SMEM(source_cells.shape, jnp.int32),
            pltpu.SMEM(source_codes.shape, jnp.int32),
            pltpu.SMEM(wavelets.shape[::-1], f32),
            pltpu.VMEM((STEPS, 2, 16, NX, NY), f32),
            pltpu.VMEM((2, ROWS, NX, NY), f32),
            pltpu.VMEM((ROWS, NX, NY), f32),
            pltpu.VMEM((2, ROWS, NX, NY), f32),
            pltpu.VMEM((2, STEPS, ROWS, NX, NY), f32),
            pltpu.VMEM(receiver_cells.shape, jnp.int32),
            pltpu.VMEM(residuals.shape, f32),
            pltpu.VMEM((3, STEPS * NY, receiver_cells.shape[1]), jnp.bfloat16),
            pltpu.VMEM((ROWS * NX, NY), f32),
            pltpu.VMEM((16, 2, ROWS, NY), f32),
            pltpu.VMEM((16, 2, ROWS, NY), f32),
            pltpu.VMEM((16, 2, ROWS, NY), f32),
            pltpu.VMEM((16, 2, ROWS, NY), f32),
            pltpu.VMEM((ROWS, 2, NY), f32),
            pltpu.VMEM((3, ROWS, 2, NY), f32),
            pltpu.VMEM((2, 3, ROWS, NY), f32),
            pltpu.VMEM((2, ROWS, NY), f32),
            pltpu.VMEM((2, 3, ROWS, NY), f32),
            pltpu.VMEM((2, ROWS, NY), f32),
            pltpu.VMEM((2, ROWS, NY), f32),
            pltpu.VMEM((2, 2, ROWS, NY), f32),
            pltpu.VMEM((2, 2, ROWS, NY), f32),
            pltpu.VMEM((2, 2, ROWS, NY), f32),
            pltpu.SemaphoreType.DMA((11,)),
            pltpu.SemaphoreType.DMA((STEPS, 2, 2, 2)),
            pltpu.SemaphoreType.DMA((STEPS, 2, 2, 2)),
            pltpu.SemaphoreType.DMA((2, 2)),
            pltpu.SemaphoreType.DMA((16,)),
            pltpu.SemaphoreType.DMA((16,)),
            pltpu.SemaphoreType.DMA((4,)),
            pltpu.SemaphoreType.DMA((4,)),
            pltpu.SemaphoreType.DMA((8,)),
            pltpu.SemaphoreType.DMA((8,)),
            pltpu.SemaphoreType.REGULAR((2,)),
        ],
        compiler_params=pltpu.CompilerParams(collective_id=0, has_side_effects=True, vmem_limit_bytes=16 * 2**20),
    )(
        *(
            pltpu.with_memory_space_constraint(operand, pltpu.HBM)
            for operand in (
                source_cells,
                source_codes,
                wavelets.T,
                velocity,
                wave_state,
                receiver_cells,
                residuals,
                momentum,
                diffusivity,
            )
        )
    )
    return pl.pallas_call(
        store,
        out_shape=results,
        in_specs=[vmem] * 3,
        out_specs=(hbm,) * 3,
        scratch_shapes=[pltpu.SemaphoreType.DMA((3,))],
        compiler_params=pltpu.CompilerParams(vmem_limit_bytes=2**20),
    )(*held)


def solution(mesh):
    return jax.shard_map(
        on_device,
        mesh=mesh,
        in_specs=(
            P("slab", None, None),
            P(None, "shot", None, "slab", None, None),
            P("shot", None),
            P("shot", None),
            P(),
            P("shot", None),
            P("shot", None, None),
            P("slab", "shot", None),
            P(None, "slab", "shot", None),
        ),
        out_specs=(
            P("shot", None, "slab", None, None),
            P("slab", "shot", None),
            P("slab", "shot", None),
        ),
        check_vma=False,
    )
```

```python
import math

import jax
import jax.numpy as jnp
from jax import lax
from jax.experimental import pallas as pl
from jax.experimental.pallas import tpu as pltpu
from jax.sharding import PartitionSpec as P

TAPS = (-205.0 / 72.0, 8.0 / 5.0, -1.0 / 5.0, 8.0 / 315.0, -1.0 / 560.0)
MESH = pl.DeviceIdType.MESH
ROWS, NX, NY = 8, 64, 128
SLABS, SHOTS = 32, 32
STEPS = 2
PARTS = 4
PLANE = NX * NY
SCALE = math.sqrt(SHOTS * STEPS)


def shifted(plane, offset, axis, index):
    size = plane.shape[axis]
    rolled = pltpu.roll(plane, (-offset) % size, axis)
    keep = index < size - offset if offset > 0 else index >= -offset
    return jnp.where(keep, rolled, 0.0)


def lateral(plane):
    along_x = lax.broadcasted_iota(jnp.int32, plane.shape, 0)
    along_y = lax.broadcasted_iota(jnp.int32, plane.shape, 1)
    total = (3.0 * TAPS[0]) * plane
    for r in range(1, 5):
        pairs = shifted(plane, r, 0, along_x) + shifted(plane, -r, 0, along_x)
        pairs = pairs + shifted(plane, r, 1, along_y) + shifted(plane, -r, 1, along_y)
        total = total + TAPS[r] * pairs
    return total


def kernel(
    src_cells_hbm,
    src_codes_hbm,
    wavelets_hbm,
    velocity,
    waves,
    rec_cells_hbm,
    residuals_hbm,
    momentum,
    diffusivity,
    fields,
    new_momentum,
    new_velocity,
    src_cells,
    src_codes,
    wavelets,
    ext,
    prev,
    vel,
    lat,
    inject,
    rec_cells,
    residuals,
    spread,
    image,
    pair_out,
    pair_in,
    pair_sum,
    group_in,
    mom,
    dif,
    dif_t,
    dif_pack,
    dif_side,
    dif_edge,
    held,
    beyond_z,
    beyond_x,
    corner,
    load_sem,
    halo_send,
    halo_recv,
    pair_sem,
    group_send,
    group_recv,
    dif_send,
    dif_recv,
    near_send,
    near_recv,
    ready,
):
    shot = lax.axis_index("shot")
    slab = lax.axis_index("slab")
    cx, cy, core = shot // 8, (shot // 2) % 4, shot % 2
    above, below = slab + 1, slab - 1
    left, right = shot - 1, shot + 1
    has_above, has_below = slab < SLABS - 1, slab > 0
    has_left, has_right = shot > 0, shot < SHOTS - 1

    def at(x, y, c):
        return (x % 4) * 8 + (y % 4) * 2 + c

    partners = [(at(cx, cy, 1 - core), slab)]
    partners += [(at(cx, cy + d, core), slab) for d in (1, 3)]
    partners += [(at(cx + d, cy, core), slab) for d in (1, 2, 3)]

    loads = [
        pltpu.make_async_copy(waves.at[1, 0, 0], ext.at[0, 0, pl.ds(4, ROWS)], load_sem.at[0]),
        pltpu.make_async_copy(waves.at[1, 0, 1], ext.at[0, 1, pl.ds(4, ROWS)], load_sem.at[1]),
        pltpu.make_async_copy(rec_cells_hbm, rec_cells, load_sem.at[2]),
        pltpu.make_async_copy(residuals_hbm, residuals, load_sem.at[3]),
        pltpu.make_async_copy(velocity, vel, load_sem.at[4]),
        pltpu.make_async_copy(waves.at[0, 0], prev, load_sem.at[5]),
        pltpu.make_async_copy(momentum, mom, load_sem.at[6]),
        pltpu.make_async_copy(diffusivity, dif, load_sem.at[7]),
        pltpu.make_async_copy(src_cells_hbm, src_cells, load_sem.at[8]),
        pltpu.make_async_copy(src_codes_hbm, src_codes, load_sem.at[9]),
        pltpu.make_async_copy(wavelets_hbm, wavelets, load_sem.at[10]),
    ]
    barrier = pltpu.get_barrier_semaphore()

    def greet(semaphore):
        for partner in partners:
            pl.semaphore_signal(semaphore, inc=1, device_id=partner, device_id_type=MESH)

    def meet(target):
        pl.semaphore_signal(barrier, inc=1, device_id=(shot, target), device_id_type=MESH)

    pl.when(has_above)(lambda: meet(above))
    pl.when(has_below)(lambda: meet(below))
    greet(barrier)
    for load in loads:
        load.start()

    @pl.when(slab == 0)
    def _():
        ext[:, :, pl.ds(0, 4)] = jnp.zeros((STEPS, 2, 4, NX, NY), jnp.float32)
        beyond_z[0] = jnp.zeros((2, ROWS, NY), jnp.float32)
        corner[0] = jnp.zeros((2, ROWS, NY), jnp.float32)

    @pl.when(slab == SLABS - 1)
    def _():
        ext[:, :, pl.ds(12, 4)] = jnp.zeros((STEPS, 2, 4, NX, NY), jnp.float32)
        beyond_z[1] = jnp.zeros((2, ROWS, NY), jnp.float32)
        corner[1] = jnp.zeros((2, ROWS, NY), jnp.float32)

    @pl.when(shot == 0)
    def _():
        beyond_x[0] = jnp.zeros((2, ROWS, NY), jnp.float32)
        corner[:, 0] = jnp.zeros((2, ROWS, NY), jnp.float32)

    @pl.when(shot == SHOTS - 1)
    def _():
        beyond_x[1] = jnp.zeros((2, ROWS, NY), jnp.float32)
        corner[:, 1] = jnp.zeros((2, ROWS, NY), jnp.float32)

    pl.semaphore_wait(
        barrier,
        len(partners) + has_above.astype(jnp.int32) + has_below.astype(jnp.int32),
    )

    width = NX // PARTS

    def halo(step, field, part):
        across = pl.ds(part * width, width) if step == 1 else pl.ds(0, NX)
        copies = []
        for way, (target, first, landing) in enumerate(((above, 4, 0), (below, 0, 12))):
            if step == 0:
                source = waves.at[1, 0, field, pl.ds(first, 4), across]
            else:
                source = ext.at[1, field, pl.ds(4 + first, 4), across]
            copies.append(
                pltpu.make_async_remote_copy(
                    src_ref=source,
                    dst_ref=ext.at[step, field, pl.ds(landing, 4), across],
                    send_sem=halo_send.at[step, field, part, way],
                    recv_sem=halo_recv.at[step, field, part, way],
                    device_id=(shot, target),
                    device_id_type=MESH,
                )
            )
        return copies

    def start(copies):
        pl.when(has_above)(copies[0].start)
        pl.when(has_below)(copies[1].start)

    def arrive(copies):
        pl.when(has_below)(copies[0].wait_recv)
        pl.when(has_above)(copies[1].wait_recv)

    def leave(copies):
        pl.when(has_above)(copies[0].wait_send)
        pl.when(has_below)(copies[1].wait_send)

    (u0, q0), (u1, q1) = [
        [[halo(step, field, part) for part in range(PARTS if step else 1)] for field in range(2)]
        for step in range(STEPS)
    ]
    for copies in u0 + q0:
        start(copies)
    greet(ready.at[0])

    def near_part(step, field):
        def body(z, carry):
            lat[field, z] = lateral(ext[step, field, 4 + z])
            return carry

        lax.fori_loop(0, ROWS, body, 0)

    def advance(step, field, first=0, count=NX):
        across = pl.ds(first, count)

        def body(z, carry):
            now = ext[step, field, 4 + z, across]
            total = lat[field, z, across] + inject[field, step, z, across]
            for r in range(1, 5):
                total = total + TAPS[r] * (
                    ext[step, field, 4 + z + r, across] + ext[step, field, 4 + z - r, across]
                )
            speed_here = vel[z, across]
            drive = (speed_here * speed_here) * total
            before = prev[field, z, across] if step == 0 else ext[0, field, 4 + z, across]
            after = 2.0 * now - before + drive
            if step == 0:
                ext[1, field, 4 + z, across] = after
            else:
                fields[0, field, z, across] = after
            if field == 0:
                rows = pl.ds(pl.multiple_of(z * NX + first, width), count)
                product = drive * ext[step, 1, 4 + z, across]
                image[rows, :] = product if step == 0 else image[rows, :] + product
            return carry

        lax.fori_loop(0, ROWS, body, 0)

    for load in loads[8:]:
        load.wait()
    base = slab * (ROWS * PLANE)
    cells = [src_cells[0, k] - base for k in range(4)]
    amounts = [[wavelets[t, src_codes[0, k]] for k in range(4)] for t in range(STEPS)]

    def source_row(z, carry):
        cell = lax.broadcasted_iota(jnp.int32, (NX, NY), 0) * NY
        cell = cell + lax.broadcasted_iota(jnp.int32, (NX, NY), 1) + z * PLANE
        grids = [jnp.zeros((NX, NY), jnp.float32) for _ in range(STEPS)]
        for k in range(4):
            here = cell == cells[k]
            for t in range(STEPS):
                grids[t] = grids[t] + jnp.where(here, amounts[t][k], 0.0)
        for t in range(STEPS):
            inject[0, t, z] = grids[t]
        return carry

    lax.fori_loop(0, ROWS, source_row, 0)

    loads[0].wait()
    near_part(0, 0)
    pl.semaphore_wait(ready.at[0], len(partners))
    greet(ready.at[1])

    loads[2].wait()
    loads[3].wait()
    cell = rec_cells[...] - base
    line = cell >> 7
    lane = cell & (NY - 1)
    count = cell.shape[1]
    for t in range(STEPS):
        here = lax.broadcasted_iota(jnp.int32, (NY, count), 0) == lane
        rest = jnp.where(here, residuals[0, pl.ds(t, 1), :], 0.0)
        for part in range(3):
            piece = rest.astype(jnp.bfloat16)
            spread[part, pl.ds(t * NY, NY), :] = piece
            rest = rest - piece.astype(jnp.float32)

    def receiver_row(z, carry):
        here = lax.broadcasted_iota(jnp.int32, (NX, count), 0) + z * NX == line
        chosen = jnp.where(here, 1.0, 0.0).astype(jnp.bfloat16)
        grid = jnp.zeros((NX, STEPS * NY), jnp.float32)
        for part in range(3):
            grid = grid + lax.dot_general(
                chosen,
                spread[part],
                (((1,), (1,)), ((), ())),
                preferred_element_type=jnp.float32,
            )
        for t in range(STEPS):
            inject[1, t, z] = grid[:, t * NY : (t + 1) * NY]
        return carry

    lax.fori_loop(0, ROWS, receiver_row, 0)
    pl.semaphore_wait(ready.at[1], len(partners))

    loads[6].wait()
    loads[7].wait()
    dif_pack[...] = jnp.zeros((2, ROWS, NY), jnp.float32)
    for i in range(2):
        for k in range(3):
            tile = dif[k, :, i, :]
            dif_t[i, k] = tile
            dif_pack[0, pl.ds(3 * i + k, 1), :] = tile[ROWS - 1 :]
            dif_pack[1, pl.ds(3 * i + k, 1), :] = tile[:1]

    def near(source, landing, send_sem, recv_sem, target, goes, comes):
        copy = pltpu.make_async_remote_copy(
            src_ref=source,
            dst_ref=landing,
            send_sem=send_sem,
            recv_sem=recv_sem,
            device_id=target,
            device_id_type=MESH,
        )
        return copy, goes, comes

    dif_ways = [
        (dif_pack.at[0], dif_edge.at[0], (shot, above), has_above, has_below),
        (dif_pack.at[1], dif_edge.at[1], (shot, below), has_below, has_above),
        (dif_t.at[1], dif_side.at[0], (right, slab), has_right, has_left),
        (dif_t.at[0], dif_side.at[1], (left, slab), has_left, has_right),
    ]
    dif_copies = [
        near(source, landing, dif_send.at[n], dif_recv.at[n], target, goes, comes)
        for n, (source, landing, target, goes, comes) in enumerate(dif_ways)
    ]
    near_ways = [
        (held, beyond_z.at[0], (shot, above), has_above, has_below),
        (held, beyond_z.at[1], (shot, below), has_below, has_above),
        (held, beyond_x.at[0], (right, slab), has_right, has_left),
        (held, beyond_x.at[1], (left, slab), has_left, has_right),
        (held.at[1], corner.at[0, 0], (right, above), has_right & has_above, has_left & has_below),
        (held.at[0], corner.at[0, 1], (left, above), has_left & has_above, has_right & has_below),
        (held.at[1], corner.at[1, 0], (right, below), has_right & has_below, has_left & has_above),
        (held.at[0], corner.at[1, 1], (left, below), has_left & has_below, has_right & has_above),
    ]
    near_copies = [
        near(source, landing, near_send.at[n], near_recv.at[n], target, goes, comes)
        for n, (source, landing, target, goes, comes) in enumerate(near_ways)
    ]

    loads[1].wait()
    near_part(0, 1)
    loads[4].wait()
    loads[5].wait()

    for copies in u0:
        arrive(copies)
    advance(0, 0)
    for copies in u1:
        start(copies)
    for copy, goes, _ in dif_copies:
        pl.when(goes)(copy.start)
    near_part(1, 0)

    for copies in q0:
        arrive(copies)
    advance(0, 1)
    start(q1[0])
    near_part(1, 1)

    def strip(i, c, r):
        return image[pl.ds(i * 4 + c * 2 + r, ROWS, stride=NX), :]

    def pair(part):
        groups = pl.ds(4 * part, 4)
        return pltpu.make_async_remote_copy(
            src_ref=pair_out.at[groups],
            dst_ref=pair_in.at[groups],
            send_sem=pair_sem.at[0, part],
            recv_sem=pair_sem.at[1, part],
            device_id=(at(cx, cy, 1 - core), slab),
            device_id_type=MESH,
        )

    def group(k):
        tx, ty = (cx + k // 4) % 4, (cy + k % 4) % 4
        return pltpu.make_async_remote_copy(
            src_ref=pair_sum.at[tx * 4 + ty],
            dst_ref=group_in.at[k],
            send_sem=group_send.at[k],
            recv_sem=group_recv.at[k],
            device_id=(at(tx, ty, core), slab),
            device_id_type=MESH,
        )

    def finish(part):
        pair(part).wait_recv()
        for i in range(4 * part, 4 * part + 4):
            for r in range(2):
                pair_sum[i, r] = strip(i, core, r) + pair_in[i, r]
        for dy in (2, 1, 3, 0):
            k = ((part + 4 - cx) % 4) * 4 + dy
            if dy == 0:
                pl.when(part != cx)(group(k).start)
            else:
                group(k).start()

    for part in range(PARTS):
        arrive(u1[part])
        advance(1, 0, part * width, width)
        for i in range(4 * part, 4 * part + 4):
            for r in range(2):
                pair_out[i, r] = strip(i, 1 - core, r)
        pair(part).start()
        if part > 0:
            finish(part - 1)
    finish(PARTS - 1)
    for copies in q1[1:]:
        start(copies)
    for copy, _, comes in dif_copies:
        pl.when(comes)(copy.wait_recv)

    def take_group(k, total):
        group(k).wait_recv()
        return total + group_in[k]

    total = lax.fori_loop(1, 16, take_group, pair_sum[cx * 4 + cy])

    depth = lax.broadcasted_iota(jnp.int32, (ROWS, NY), 0)
    along_y = lax.broadcasted_iota(jnp.int32, (ROWS, NY), 1)
    speed = []
    smooth = []
    for i in range(2):
        rows = [vel[z, pl.ds(shot * 2 + i, 1), :] for z in range(ROWS)]
        speed.append(jnp.concatenate(rows, axis=0))
        smooth.append((-0.2 * total[i]) / (speed[i] * SCALE))
    for i in range(2):
        held[i] = smooth[i]
    for n in (4, 5, 6, 7, 2, 3, 0, 1):
        copy, goes, _ = near_copies[n]
        pl.when(goes)(copy.start)

    for copies in q1:
        arrive(copies)
    advance(1, 1)

    for copies in u0 + q0 + u1 + q1:
        leave(copies)
    for part in range(PARTS):
        pair(part).wait_send()
    for copy, goes, _ in dif_copies:
        pl.when(goes)(copy.wait_send)

    def drain_group(k, carry):
        group(k).wait_send()
        return carry

    lax.fori_loop(1, 16, drain_group, 0)

    def step(centre, down, up, before, after, kappas):
        sides = shifted(centre, 1, 1, along_y) + shifted(centre, -1, 1, along_y)
        return (
            centre
            + kappas[0] * (up - 2.0 * centre + down)
            + kappas[1] * (after - 2.0 * centre + before)
            + kappas[2] * (sides - 2.0 * centre)
        )

    def down_of(centre, low):
        return jnp.where(depth == 0, pltpu.roll(low, 1, 0), pltpu.roll(centre, 1, 0))

    def up_of(centre, high):
        last = ROWS - 1
        return jnp.where(depth == last, pltpu.roll(high, last, 0), pltpu.roll(centre, last, 0))

    own = [[dif_t[i, k] for k in range(3)] for i in range(2)]
    side = [[dif_side[i, k] for k in range(3)] for i in range(2)]
    edge = [
        [
            [jnp.broadcast_to(dif_edge[z, pl.ds(3 * i + k, 1), :], (ROWS, NY)) for k in range(3)]
            for i in range(2)
        ]
        for z in range(2)
    ]
    for copy, _, comes in near_copies:
        pl.when(comes)(copy.wait_recv)
    low, high = [[beyond_z[z, i] for i in range(2)] for z in range(2)]
    (far_left, near_left), (near_right, far_right) = [
        [beyond_x[x, i] for i in range(2)] for x in range(2)
    ]
    (low_left, low_right), (high_left, high_right) = [
        [corner[z, x] for x in range(2)] for z in range(2)
    ]
    before = [near_left, smooth[0]]
    after = [smooth[1], near_right]
    once = [
        step(
            smooth[i],
            down_of(smooth[i], low[i]),
            up_of(smooth[i], high[i]),
            before[i],
            after[i],
            own[i],
        )
        for i in range(2)
    ]
    once_left = step(
        near_left,
        down_of(near_left, low_left),
        up_of(near_left, high_left),
        far_left,
        smooth[0],
        side[0],
    )
    once_right = step(
        near_right,
        down_of(near_right, low_right),
        up_of(near_right, high_right),
        smooth[1],
        far_right,
        side[1],
    )
    once_left = jnp.where(has_left, once_left, 0.0)
    once_right = jnp.where(has_right, once_right, 0.0)
    low_before, low_after = [low_left, low[0]], [low[1], low_right]
    high_before, high_after = [high_left, high[0]], [high[1], high_right]
    last = ROWS - 1
    twice = []
    for i in range(2):
        once_low = step(
            low[i],
            pltpu.roll(low[i], 1, 0),
            up_of(low[i], smooth[i]),
            low_before[i],
            low_after[i],
            edge[0][i],
        )
        once_high = step(
            high[i],
            down_of(high[i], smooth[i]),
            pltpu.roll(high[i], last, 0),
            high_before[i],
            high_after[i],
            edge[1][i],
        )
        once_low = jnp.where(has_below, once_low, 0.0)
        once_high = jnp.where(has_above, once_high, 0.0)
        twice.append(
            step(
                once[i],
                down_of(once[i], once_low),
                up_of(once[i], once_high),
                once_left if i == 0 else once[0],
                once[1] if i == 0 else once_right,
                own[i],
            )
        )
    smooth = twice
    for i in range(2):
        updated = 0.9 * mom[:, i, :] + smooth[i]
        new_momentum[:, i, :] = updated
        new_velocity[:, i, :] = speed[i] - 0.02 * updated

    for copy, goes, _ in near_copies:
        pl.when(goes)(copy.wait_send)


def store(*refs):
    sources, targets, sem = refs[:3], refs[3:6], refs[6]
    copies = [
        pltpu.make_async_copy(source, target, sem.at[n])
        for n, (source, target) in enumerate(zip(sources, targets))
    ]
    for copy in copies:
        copy.start()
    for copy in copies:
        copy.wait()


def on_device(
    velocity,
    wave_state,
    source_cells,
    source_codes,
    wavelets,
    receiver_cells,
    residuals,
    momentum,
    diffusivity,
):
    hbm = pl.BlockSpec(memory_space=pltpu.HBM)
    vmem = pl.BlockSpec(memory_space=pltpu.VMEM)
    f32 = jnp.float32
    results = (
        jax.ShapeDtypeStruct((1, 2, ROWS, NX, NY), f32),
        jax.ShapeDtypeStruct((ROWS, 2, NY), f32),
        jax.ShapeDtypeStruct((ROWS, 2, NY), f32),
    )
    held = pl.pallas_call(
        kernel,
        out_shape=results,
        in_specs=[hbm] * 9,
        out_specs=(vmem, vmem, vmem),
        scratch_shapes=[
            pltpu.SMEM(source_cells.shape, jnp.int32),
            pltpu.SMEM(source_codes.shape, jnp.int32),
            pltpu.SMEM(wavelets.shape[::-1], f32),
            pltpu.VMEM((STEPS, 2, 16, NX, NY), f32),
            pltpu.VMEM((2, ROWS, NX, NY), f32),
            pltpu.VMEM((ROWS, NX, NY), f32),
            pltpu.VMEM((2, ROWS, NX, NY), f32),
            pltpu.VMEM((2, STEPS, ROWS, NX, NY), f32),
            pltpu.VMEM(receiver_cells.shape, jnp.int32),
            pltpu.VMEM(residuals.shape, f32),
            pltpu.VMEM((3, STEPS * NY, receiver_cells.shape[1]), jnp.bfloat16),
            pltpu.VMEM((ROWS * NX, NY), f32),
            pltpu.VMEM((16, 2, ROWS, NY), f32),
            pltpu.VMEM((16, 2, ROWS, NY), f32),
            pltpu.VMEM((16, 2, ROWS, NY), f32),
            pltpu.VMEM((16, 2, ROWS, NY), f32),
            pltpu.VMEM((ROWS, 2, NY), f32),
            pltpu.VMEM((3, ROWS, 2, NY), f32),
            pltpu.VMEM((2, 3, ROWS, NY), f32),
            pltpu.VMEM((2, ROWS, NY), f32),
            pltpu.VMEM((2, 3, ROWS, NY), f32),
            pltpu.VMEM((2, ROWS, NY), f32),
            pltpu.VMEM((2, ROWS, NY), f32),
            pltpu.VMEM((2, 2, ROWS, NY), f32),
            pltpu.VMEM((2, 2, ROWS, NY), f32),
            pltpu.VMEM((2, 2, ROWS, NY), f32),
            pltpu.SemaphoreType.DMA((11,)),
            pltpu.SemaphoreType.DMA((STEPS, 2, PARTS, 2)),
            pltpu.SemaphoreType.DMA((STEPS, 2, PARTS, 2)),
            pltpu.SemaphoreType.DMA((2, PARTS)),
            pltpu.SemaphoreType.DMA((16,)),
            pltpu.SemaphoreType.DMA((16,)),
            pltpu.SemaphoreType.DMA((4,)),
            pltpu.SemaphoreType.DMA((4,)),
            pltpu.SemaphoreType.DMA((8,)),
            pltpu.SemaphoreType.DMA((8,)),
            pltpu.SemaphoreType.REGULAR((2,)),
        ],
        compiler_params=pltpu.CompilerParams(collective_id=0, has_side_effects=True, vmem_limit_bytes=16 * 2**20),
    )(
        *(
            pltpu.with_memory_space_constraint(operand, pltpu.HBM)
            for operand in (
                source_cells,
                source_codes,
                wavelets.T,
                velocity,
                wave_state,
                receiver_cells,
                residuals,
                momentum,
                diffusivity,
            )
        )
    )
    return pl.pallas_call(
        store,
        out_shape=results,
        in_specs=[vmem] * 3,
        out_specs=(hbm,) * 3,
        scratch_shapes=[pltpu.SemaphoreType.DMA((3,))],
        compiler_params=pltpu.CompilerParams(vmem_limit_bytes=2**20),
    )(*held)


def solution(mesh):
    return jax.shard_map(
        on_device,
        mesh=mesh,
        in_specs=(
            P("slab", None, None),
            P(None, "shot", None, "slab", None, None),
            P("shot", None),
            P("shot", None),
            P(),
            P("shot", None),
            P("shot", None, None),
            P("slab", "shot", None),
            P(None, "slab", "shot", None),
        ),
        out_specs=(
            P("shot", None, "slab", None, None),
            P("slab", "shot", None),
            P("slab", "shot", None),
        ),
        check_vma=False,
    )
```

```python
import math

import jax
import jax.numpy as jnp
from jax import lax
from jax.experimental import pallas as pl
from jax.experimental.pallas import tpu as pltpu
from jax.sharding import PartitionSpec as P

TAPS = (-205.0 / 72.0, 8.0 / 5.0, -1.0 / 5.0, 8.0 / 315.0, -1.0 / 560.0)
MESH = pl.DeviceIdType.MESH
ROWS, NX, NY = 8, 64, 128
SLABS, SHOTS = 32, 32
STEPS = 2
PARTS = 4
PLANE = NX * NY
SCALE = math.sqrt(SHOTS * STEPS)


def shifted(plane, offset, axis, index):
    size = plane.shape[axis]
    rolled = pltpu.roll(plane, (-offset) % size, axis)
    keep = index < size - offset if offset > 0 else index >= -offset
    return jnp.where(keep, rolled, 0.0)


def lateral(plane):
    along_x = lax.broadcasted_iota(jnp.int32, plane.shape, 0)
    along_y = lax.broadcasted_iota(jnp.int32, plane.shape, 1)
    total = (3.0 * TAPS[0]) * plane
    for r in range(1, 5):
        pairs = shifted(plane, r, 0, along_x) + shifted(plane, -r, 0, along_x)
        pairs = pairs + shifted(plane, r, 1, along_y) + shifted(plane, -r, 1, along_y)
        total = total + TAPS[r] * pairs
    return total


def kernel(
    src_cells_hbm,
    src_codes_hbm,
    wavelets_hbm,
    velocity,
    waves,
    rec_cells_hbm,
    residuals_hbm,
    momentum,
    diffusivity,
    fields,
    new_momentum,
    new_velocity,
    src_cells,
    src_codes,
    wavelets,
    ext,
    prev,
    vel,
    lat,
    inject,
    rec_cells,
    residuals,
    spread,
    image,
    pair_out,
    pair_in,
    pair_sum,
    group_in,
    mom,
    dif,
    dif_t,
    dif_pack,
    dif_side,
    dif_edge,
    held,
    beyond_z,
    beyond_x,
    corner,
    load_sem,
    halo_send,
    halo_recv,
    pair_sem,
    group_send,
    group_recv,
    dif_send,
    dif_recv,
    near_send,
    near_recv,
    ready,
):
    shot = lax.axis_index("shot")
    slab = lax.axis_index("slab")
    cx, cy, core = shot // 8, (shot // 2) % 4, shot % 2
    above, below = slab + 1, slab - 1
    left, right = shot - 1, shot + 1
    has_above, has_below = slab < SLABS - 1, slab > 0
    has_left, has_right = shot > 0, shot < SHOTS - 1

    def at(x, y, c):
        return (x % 4) * 8 + (y % 4) * 2 + c

    partners = [(at(cx, cy, 1 - core), slab)]
    partners += [(at(cx, cy + d, core), slab) for d in (1, 3)]
    partners += [(at(cx + d, cy, core), slab) for d in (1, 2, 3)]

    loads = [
        pltpu.make_async_copy(waves.at[1, 0, 0], ext.at[0, 0, pl.ds(4, ROWS)], load_sem.at[0]),
        pltpu.make_async_copy(waves.at[1, 0, 1], ext.at[0, 1, pl.ds(4, ROWS)], load_sem.at[1]),
        pltpu.make_async_copy(rec_cells_hbm, rec_cells, load_sem.at[2]),
        pltpu.make_async_copy(residuals_hbm, residuals, load_sem.at[3]),
        pltpu.make_async_copy(velocity, vel, load_sem.at[4]),
        pltpu.make_async_copy(waves.at[0, 0], prev, load_sem.at[5]),
        pltpu.make_async_copy(momentum, mom, load_sem.at[6]),
        pltpu.make_async_copy(diffusivity, dif, load_sem.at[7]),
        pltpu.make_async_copy(src_cells_hbm, src_cells, load_sem.at[8]),
        pltpu.make_async_copy(src_codes_hbm, src_codes, load_sem.at[9]),
        pltpu.make_async_copy(wavelets_hbm, wavelets, load_sem.at[10]),
    ]
    barrier = pltpu.get_barrier_semaphore()

    def greet(semaphore):
        for partner in partners:
            pl.semaphore_signal(semaphore, inc=1, device_id=partner, device_id_type=MESH)

    def meet(target):
        pl.semaphore_signal(barrier, inc=1, device_id=(shot, target), device_id_type=MESH)

    pl.when(has_above)(lambda: meet(above))
    pl.when(has_below)(lambda: meet(below))
    greet(barrier)
    for load in loads:
        load.start()

    @pl.when(slab == 0)
    def _():
        ext[:, :, pl.ds(0, 4)] = jnp.zeros((STEPS, 2, 4, NX, NY), jnp.float32)
        beyond_z[0] = jnp.zeros((2, ROWS, NY), jnp.float32)
        corner[0] = jnp.zeros((2, ROWS, NY), jnp.float32)

    @pl.when(slab == SLABS - 1)
    def _():
        ext[:, :, pl.ds(12, 4)] = jnp.zeros((STEPS, 2, 4, NX, NY), jnp.float32)
        beyond_z[1] = jnp.zeros((2, ROWS, NY), jnp.float32)
        corner[1] = jnp.zeros((2, ROWS, NY), jnp.float32)

    @pl.when(shot == 0)
    def _():
        beyond_x[0] = jnp.zeros((2, ROWS, NY), jnp.float32)
        corner[:, 0] = jnp.zeros((2, ROWS, NY), jnp.float32)

    @pl.when(shot == SHOTS - 1)
    def _():
        beyond_x[1] = jnp.zeros((2, ROWS, NY), jnp.float32)
        corner[:, 1] = jnp.zeros((2, ROWS, NY), jnp.float32)

    pl.semaphore_wait(
        barrier,
        len(partners) + has_above.astype(jnp.int32) + has_below.astype(jnp.int32),
    )

    width = NX // PARTS

    away = (2, 1, 3, 0)
    quarters = [(cx + d) % 4 for d in away]
    firsts = [pl.multiple_of(quarter * width, width) for quarter in quarters]

    def halo(step, field, turn):
        across = pl.ds(firsts[turn], width) if step == 1 else pl.ds(0, NX)
        copies = []
        for way, (target, first, landing) in enumerate(((above, 4, 0), (below, 0, 12))):
            if step == 0:
                source = waves.at[1, 0, field, pl.ds(first, 4), across]
            else:
                source = ext.at[1, field, pl.ds(4 + first, 4), across]
            copies.append(
                pltpu.make_async_remote_copy(
                    src_ref=source,
                    dst_ref=ext.at[step, field, pl.ds(landing, 4), across],
                    send_sem=halo_send.at[step, field, turn, way],
                    recv_sem=halo_recv.at[step, field, turn, way],
                    device_id=(shot, target),
                    device_id_type=MESH,
                )
            )
        return copies

    def start(copies):
        pl.when(has_above)(copies[0].start)
        pl.when(has_below)(copies[1].start)

    def arrive(copies):
        pl.when(has_below)(copies[0].wait_recv)
        pl.when(has_above)(copies[1].wait_recv)

    def leave(copies):
        pl.when(has_above)(copies[0].wait_send)
        pl.when(has_below)(copies[1].wait_send)

    (u0, q0), (u1, q1) = [
        [[halo(step, field, turn) for turn in range(PARTS if step else 1)] for field in range(2)]
        for step in range(STEPS)
    ]
    for copies in u0 + q0:
        start(copies)
    greet(ready.at[0])

    def near_part(step, field):
        def body(z, carry):
            lat[field, z] = lateral(ext[step, field, 4 + z])
            return carry

        lax.fori_loop(0, ROWS, body, 0)

    def advance(step, field, first=0, count=NX):
        across = pl.ds(first, count)

        def body(z, carry):
            now = ext[step, field, 4 + z, across]
            total = lat[field, z, across] + inject[field, step, z, across]
            for r in range(1, 5):
                total = total + TAPS[r] * (
                    ext[step, field, 4 + z + r, across] + ext[step, field, 4 + z - r, across]
                )
            speed_here = vel[z, across]
            drive = (speed_here * speed_here) * total
            before = prev[field, z, across] if step == 0 else ext[0, field, 4 + z, across]
            after = 2.0 * now - before + drive
            if step == 0:
                ext[1, field, 4 + z, across] = after
            else:
                fields[0, field, z, across] = after
            if field == 0:
                rows = pl.ds(pl.multiple_of(z * NX + first, width), count)
                product = drive * ext[step, 1, 4 + z, across]
                image[rows, :] = product if step == 0 else image[rows, :] + product
            return carry

        lax.fori_loop(0, ROWS, body, 0)

    for load in loads[8:]:
        load.wait()
    base = slab * (ROWS * PLANE)
    cells = [src_cells[0, k] - base for k in range(4)]
    amounts = [[wavelets[t, src_codes[0, k]] for k in range(4)] for t in range(STEPS)]

    def source_row(z, carry):
        cell = lax.broadcasted_iota(jnp.int32, (NX, NY), 0) * NY
        cell = cell + lax.broadcasted_iota(jnp.int32, (NX, NY), 1) + z * PLANE
        grids = [jnp.zeros((NX, NY), jnp.float32) for _ in range(STEPS)]
        for k in range(4):
            here = cell == cells[k]
            for t in range(STEPS):
                grids[t] = grids[t] + jnp.where(here, amounts[t][k], 0.0)
        for t in range(STEPS):
            inject[0, t, z] = grids[t]
        return carry

    lax.fori_loop(0, ROWS, source_row, 0)

    loads[0].wait()
    near_part(0, 0)
    pl.semaphore_wait(ready.at[0], len(partners))
    greet(ready.at[1])

    loads[2].wait()
    loads[3].wait()
    cell = rec_cells[...] - base
    line = cell >> 7
    lane = cell & (NY - 1)
    count = cell.shape[1]
    for t in range(STEPS):
        here = lax.broadcasted_iota(jnp.int32, (NY, count), 0) == lane
        rest = jnp.where(here, residuals[0, pl.ds(t, 1), :], 0.0)
        for part in range(3):
            piece = rest.astype(jnp.bfloat16)
            spread[part, pl.ds(t * NY, NY), :] = piece
            rest = rest - piece.astype(jnp.float32)

    def receiver_row(z, carry):
        here = lax.broadcasted_iota(jnp.int32, (NX, count), 0) + z * NX == line
        chosen = jnp.where(here, 1.0, 0.0).astype(jnp.bfloat16)
        grid = jnp.zeros((NX, STEPS * NY), jnp.float32)
        for part in range(3):
            grid = grid + lax.dot_general(
                chosen,
                spread[part],
                (((1,), (1,)), ((), ())),
                preferred_element_type=jnp.float32,
            )
        for t in range(STEPS):
            inject[1, t, z] = grid[:, t * NY : (t + 1) * NY]
        return carry

    lax.fori_loop(0, ROWS, receiver_row, 0)
    pl.semaphore_wait(ready.at[1], len(partners))

    loads[6].wait()
    loads[7].wait()
    dif_pack[...] = jnp.zeros((2, ROWS, NY), jnp.float32)
    for i in range(2):
        for k in range(3):
            tile = dif[k, :, i, :]
            dif_t[i, k] = tile
            dif_pack[0, pl.ds(3 * i + k, 1), :] = tile[ROWS - 1 :]
            dif_pack[1, pl.ds(3 * i + k, 1), :] = tile[:1]

    def near(source, landing, send_sem, recv_sem, target, goes, comes):
        copy = pltpu.make_async_remote_copy(
            src_ref=source,
            dst_ref=landing,
            send_sem=send_sem,
            recv_sem=recv_sem,
            device_id=target,
            device_id_type=MESH,
        )
        return copy, goes, comes

    dif_ways = [
        (dif_pack.at[0], dif_edge.at[0], (shot, above), has_above, has_below),
        (dif_pack.at[1], dif_edge.at[1], (shot, below), has_below, has_above),
        (dif_t.at[1], dif_side.at[0], (right, slab), has_right, has_left),
        (dif_t.at[0], dif_side.at[1], (left, slab), has_left, has_right),
    ]
    dif_copies = [
        near(source, landing, dif_send.at[n], dif_recv.at[n], target, goes, comes)
        for n, (source, landing, target, goes, comes) in enumerate(dif_ways)
    ]
    near_ways = [
        (held, beyond_z.at[0], (shot, above), has_above, has_below),
        (held, beyond_z.at[1], (shot, below), has_below, has_above),
        (held, beyond_x.at[0], (right, slab), has_right, has_left),
        (held, beyond_x.at[1], (left, slab), has_left, has_right),
        (held.at[1], corner.at[0, 0], (right, above), has_right & has_above, has_left & has_below),
        (held.at[0], corner.at[0, 1], (left, above), has_left & has_above, has_right & has_below),
        (held.at[1], corner.at[1, 0], (right, below), has_right & has_below, has_left & has_above),
        (held.at[0], corner.at[1, 1], (left, below), has_left & has_below, has_right & has_above),
    ]
    near_copies = [
        near(source, landing, near_send.at[n], near_recv.at[n], target, goes, comes)
        for n, (source, landing, target, goes, comes) in enumerate(near_ways)
    ]

    loads[1].wait()
    near_part(0, 1)
    loads[4].wait()
    loads[5].wait()

    for copies in u0:
        arrive(copies)
    advance(0, 0)
    for copies in u1:
        start(copies)
    for copy, goes, _ in dif_copies:
        pl.when(goes)(copy.start)
    near_part(1, 0)

    for copies in q0:
        arrive(copies)
    advance(0, 1)
    start(q1[0])
    near_part(1, 1)

    def strip(i, c, r):
        return image[pl.ds(i * 4 + c * 2 + r, ROWS, stride=NX), :]

    def pair(turn):
        groups = pl.ds(4 * quarters[turn], 4)
        return pltpu.make_async_remote_copy(
            src_ref=pair_out.at[groups],
            dst_ref=pair_in.at[groups],
            send_sem=pair_sem.at[0, turn],
            recv_sem=pair_sem.at[1, turn],
            device_id=(at(cx, cy, 1 - core), slab),
            device_id_type=MESH,
        )

    def group(k):
        tx, ty = (cx + k // 4) % 4, (cy + k % 4) % 4
        return pltpu.make_async_remote_copy(
            src_ref=pair_sum.at[tx * 4 + ty],
            dst_ref=group_in.at[k],
            send_sem=group_send.at[k],
            recv_sem=group_recv.at[k],
            device_id=(at(tx, ty, core), slab),
            device_id_type=MESH,
        )

    def finish(turn):
        pair(turn).wait_recv()
        for m in range(4):
            i = 4 * quarters[turn] + m
            for r in range(2):
                pair_sum[i, r] = strip(i, core, r) + pair_in[i, r]
        for dy in (2, 1, 3, 0):
            if away[turn] > 0 or dy > 0:
                group(away[turn] * 4 + dy).start()

    for turn in range(PARTS):
        arrive(u1[turn])
        advance(1, 0, firsts[turn], width)
        for m in range(4):
            i = 4 * quarters[turn] + m
            for r in range(2):
                pair_out[i, r] = strip(i, 1 - core, r)
        pair(turn).start()
        if turn > 0:
            finish(turn - 1)
    finish(PARTS - 1)
    for copies in q1[1:]:
        start(copies)
    for copy, _, comes in dif_copies:
        pl.when(comes)(copy.wait_recv)

    def take_group(k, total):
        group(k).wait_recv()
        return total + group_in[k]

    total = lax.fori_loop(4, 16, take_group, pair_sum[cx * 4 + cy])
    total = lax.fori_loop(1, 4, take_group, total)

    depth = lax.broadcasted_iota(jnp.int32, (ROWS, NY), 0)
    along_y = lax.broadcasted_iota(jnp.int32, (ROWS, NY), 1)
    speed = []
    smooth = []
    for i in range(2):
        rows = [vel[z, pl.ds(shot * 2 + i, 1), :] for z in range(ROWS)]
        speed.append(jnp.concatenate(rows, axis=0))
        smooth.append((-0.2 * total[i]) / (speed[i] * SCALE))
    for i in range(2):
        held[i] = smooth[i]
    for n in (4, 5, 6, 7, 2, 3, 0, 1):
        copy, goes, _ = near_copies[n]
        pl.when(goes)(copy.start)

    for copies in q1:
        arrive(copies)
    advance(1, 1)

    for copies in u0 + q0 + u1 + q1:
        leave(copies)
    for turn in range(PARTS):
        pair(turn).wait_send()
    for copy, goes, _ in dif_copies:
        pl.when(goes)(copy.wait_send)

    def drain_group(k, carry):
        group(k).wait_send()
        return carry

    lax.fori_loop(1, 16, drain_group, 0)

    def step(centre, down, up, before, after, kappas):
        sides = shifted(centre, 1, 1, along_y) + shifted(centre, -1, 1, along_y)
        return (
            centre
            + kappas[0] * (up - 2.0 * centre + down)
            + kappas[1] * (after - 2.0 * centre + before)
            + kappas[2] * (sides - 2.0 * centre)
        )

    def down_of(centre, low):
        return jnp.where(depth == 0, pltpu.roll(low, 1, 0), pltpu.roll(centre, 1, 0))

    def up_of(centre, high):
        last = ROWS - 1
        return jnp.where(depth == last, pltpu.roll(high, last, 0), pltpu.roll(centre, last, 0))

    own = [[dif_t[i, k] for k in range(3)] for i in range(2)]
    side = [[dif_side[i, k] for k in range(3)] for i in range(2)]
    edge = [
        [
            [jnp.broadcast_to(dif_edge[z, pl.ds(3 * i + k, 1), :], (ROWS, NY)) for k in range(3)]
            for i in range(2)
        ]
        for z in range(2)
    ]
    for copy, _, comes in near_copies:
        pl.when(comes)(copy.wait_recv)
    low, high = [[beyond_z[z, i] for i in range(2)] for z in range(2)]
    (far_left, near_left), (near_right, far_right) = [
        [beyond_x[x, i] for i in range(2)] for x in range(2)
    ]
    (low_left, low_right), (high_left, high_right) = [
        [corner[z, x] for x in range(2)] for z in range(2)
    ]
    before = [near_left, smooth[0]]
    after = [smooth[1], near_right]
    once = [
        step(
            smooth[i],
            down_of(smooth[i], low[i]),
            up_of(smooth[i], high[i]),
            before[i],
            after[i],
            own[i],
        )
        for i in range(2)
    ]
    once_left = step(
        near_left,
        down_of(near_left, low_left),
        up_of(near_left, high_left),
        far_left,
        smooth[0],
        side[0],
    )
    once_right = step(
        near_right,
        down_of(near_right, low_right),
        up_of(near_right, high_right),
        smooth[1],
        far_right,
        side[1],
    )
    once_left = jnp.where(has_left, once_left, 0.0)
    once_right = jnp.where(has_right, once_right, 0.0)
    low_before, low_after = [low_left, low[0]], [low[1], low_right]
    high_before, high_after = [high_left, high[0]], [high[1], high_right]
    last = ROWS - 1
    twice = []
    for i in range(2):
        once_low = step(
            low[i],
            pltpu.roll(low[i], 1, 0),
            up_of(low[i], smooth[i]),
            low_before[i],
            low_after[i],
            edge[0][i],
        )
        once_high = step(
            high[i],
            down_of(high[i], smooth[i]),
            pltpu.roll(high[i], last, 0),
            high_before[i],
            high_after[i],
            edge[1][i],
        )
        once_low = jnp.where(has_below, once_low, 0.0)
        once_high = jnp.where(has_above, once_high, 0.0)
        twice.append(
            step(
                once[i],
                down_of(once[i], once_low),
                up_of(once[i], once_high),
                once_left if i == 0 else once[0],
                once[1] if i == 0 else once_right,
                own[i],
            )
        )
    smooth = twice
    for i in range(2):
        updated = 0.9 * mom[:, i, :] + smooth[i]
        new_momentum[:, i, :] = updated
        new_velocity[:, i, :] = speed[i] - 0.02 * updated

    for copy, goes, _ in near_copies:
        pl.when(goes)(copy.wait_send)


def store(*refs):
    sources, targets, sem = refs[:3], refs[3:6], refs[6]
    copies = [
        pltpu.make_async_copy(source, target, sem.at[n])
        for n, (source, target) in enumerate(zip(sources, targets))
    ]
    for copy in copies:
        copy.start()
    for copy in copies:
        copy.wait()


def on_device(
    velocity,
    wave_state,
    source_cells,
    source_codes,
    wavelets,
    receiver_cells,
    residuals,
    momentum,
    diffusivity,
):
    hbm = pl.BlockSpec(memory_space=pltpu.HBM)
    vmem = pl.BlockSpec(memory_space=pltpu.VMEM)
    f32 = jnp.float32
    results = (
        jax.ShapeDtypeStruct((1, 2, ROWS, NX, NY), f32),
        jax.ShapeDtypeStruct((ROWS, 2, NY), f32),
        jax.ShapeDtypeStruct((ROWS, 2, NY), f32),
    )
    held = pl.pallas_call(
        kernel,
        out_shape=results,
        in_specs=[hbm] * 9,
        out_specs=(vmem, vmem, vmem),
        scratch_shapes=[
            pltpu.SMEM(source_cells.shape, jnp.int32),
            pltpu.SMEM(source_codes.shape, jnp.int32),
            pltpu.SMEM(wavelets.shape[::-1], f32),
            pltpu.VMEM((STEPS, 2, 16, NX, NY), f32),
            pltpu.VMEM((2, ROWS, NX, NY), f32),
            pltpu.VMEM((ROWS, NX, NY), f32),
            pltpu.VMEM((2, ROWS, NX, NY), f32),
            pltpu.VMEM((2, STEPS, ROWS, NX, NY), f32),
            pltpu.VMEM(receiver_cells.shape, jnp.int32),
            pltpu.VMEM(residuals.shape, f32),
            pltpu.VMEM((3, STEPS * NY, receiver_cells.shape[1]), jnp.bfloat16),
            pltpu.VMEM((ROWS * NX, NY), f32),
            pltpu.VMEM((16, 2, ROWS, NY), f32),
            pltpu.VMEM((16, 2, ROWS, NY), f32),
            pltpu.VMEM((16, 2, ROWS, NY), f32),
            pltpu.VMEM((16, 2, ROWS, NY), f32),
            pltpu.VMEM((ROWS, 2, NY), f32),
            pltpu.VMEM((3, ROWS, 2, NY), f32),
            pltpu.VMEM((2, 3, ROWS, NY), f32),
            pltpu.VMEM((2, ROWS, NY), f32),
            pltpu.VMEM((2, 3, ROWS, NY), f32),
            pltpu.VMEM((2, ROWS, NY), f32),
            pltpu.VMEM((2, ROWS, NY), f32),
            pltpu.VMEM((2, 2, ROWS, NY), f32),
            pltpu.VMEM((2, 2, ROWS, NY), f32),
            pltpu.VMEM((2, 2, ROWS, NY), f32),
            pltpu.SemaphoreType.DMA((11,)),
            pltpu.SemaphoreType.DMA((STEPS, 2, PARTS, 2)),
            pltpu.SemaphoreType.DMA((STEPS, 2, PARTS, 2)),
            pltpu.SemaphoreType.DMA((2, PARTS)),
            pltpu.SemaphoreType.DMA((16,)),
            pltpu.SemaphoreType.DMA((16,)),
            pltpu.SemaphoreType.DMA((4,)),
            pltpu.SemaphoreType.DMA((4,)),
            pltpu.SemaphoreType.DMA((8,)),
            pltpu.SemaphoreType.DMA((8,)),
            pltpu.SemaphoreType.REGULAR((2,)),
        ],
        compiler_params=pltpu.CompilerParams(collective_id=0, has_side_effects=True, vmem_limit_bytes=16 * 2**20),
    )(
        *(
            pltpu.with_memory_space_constraint(operand, pltpu.HBM)
            for operand in (
                source_cells,
                source_codes,
                wavelets.T,
                velocity,
                wave_state,
                receiver_cells,
                residuals,
                momentum,
                diffusivity,
            )
        )
    )
    return pl.pallas_call(
        store,
        out_shape=results,
        in_specs=[vmem] * 3,
        out_specs=(hbm,) * 3,
        scratch_shapes=[pltpu.SemaphoreType.DMA((3,))],
        compiler_params=pltpu.CompilerParams(vmem_limit_bytes=2**20),
    )(*held)


def solution(mesh):
    return jax.shard_map(
        on_device,
        mesh=mesh,
        in_specs=(
            P("slab", None, None),
            P(None, "shot", None, "slab", None, None),
            P("shot", None),
            P("shot", None),
            P(),
            P("shot", None),
            P("shot", None, None),
            P("slab", "shot", None),
            P(None, "slab", "shot", None),
        ),
        out_specs=(
            P("shot", None, "slab", None, None),
            P("slab", "shot", None),
            P("slab", "shot", None),
        ),
        check_vma=False,
    )
```

```python
import math

import jax
import jax.numpy as jnp
from jax import lax
from jax.experimental import pallas as pl
from jax.experimental.pallas import tpu as pltpu
from jax.sharding import PartitionSpec as P

TAPS = (-205.0 / 72.0, 8.0 / 5.0, -1.0 / 5.0, 8.0 / 315.0, -1.0 / 560.0)
MESH = pl.DeviceIdType.MESH
ROWS, NX, NY = 8, 64, 128
SLABS, SHOTS = 32, 32
STEPS = 2
PARTS = 4
PLANE = NX * NY
SCALE = math.sqrt(SHOTS * STEPS)


def shifted(plane, offset, axis, index):
    size = plane.shape[axis]
    rolled = pltpu.roll(plane, (-offset) % size, axis)
    keep = index < size - offset if offset > 0 else index >= -offset
    return jnp.where(keep, rolled, 0.0)


def lateral(plane):
    along_x = lax.broadcasted_iota(jnp.int32, plane.shape, 0)
    along_y = lax.broadcasted_iota(jnp.int32, plane.shape, 1)
    total = (3.0 * TAPS[0]) * plane
    for r in range(1, 5):
        pairs = shifted(plane, r, 0, along_x) + shifted(plane, -r, 0, along_x)
        pairs = pairs + shifted(plane, r, 1, along_y) + shifted(plane, -r, 1, along_y)
        total = total + TAPS[r] * pairs
    return total


def kernel(
    src_cells_hbm,
    src_codes_hbm,
    wavelets_hbm,
    velocity,
    waves,
    rec_cells_hbm,
    residuals_hbm,
    momentum,
    diffusivity,
    fields,
    new_momentum,
    new_velocity,
    src_cells,
    src_codes,
    wavelets,
    ext,
    prev,
    vel,
    lat,
    inject,
    rec_cells,
    residuals,
    spread,
    image,
    pair_out,
    pair_in,
    pair_sum,
    column_in,
    column_sum,
    row_in,
    mom,
    dif,
    dif_t,
    dif_pack,
    dif_side,
    dif_edge,
    held,
    beyond_z,
    beyond_x,
    corner,
    load_sem,
    halo_send,
    halo_recv,
    pair_sem,
    column_sem,
    row_sem,
    dif_send,
    dif_recv,
    near_send,
    near_recv,
    ready,
):
    shot = lax.axis_index("shot")
    slab = lax.axis_index("slab")
    cx, cy, core = shot // 8, (shot // 2) % 4, shot % 2
    above, below = slab + 1, slab - 1
    left, right = shot - 1, shot + 1
    has_above, has_below = slab < SLABS - 1, slab > 0
    has_left, has_right = shot > 0, shot < SHOTS - 1

    def at(x, y, c):
        return (x % 4) * 8 + (y % 4) * 2 + c

    partners = [(at(cx, cy, 1 - core), slab)]
    partners += [(at(cx, cy + d, core), slab) for d in (1, 3)]
    partners += [(at(cx + d, cy, core), slab) for d in (1, 2, 3)]

    loads = [
        pltpu.make_async_copy(waves.at[1, 0, 0], ext.at[0, 0, pl.ds(4, ROWS)], load_sem.at[0]),
        pltpu.make_async_copy(waves.at[1, 0, 1], ext.at[0, 1, pl.ds(4, ROWS)], load_sem.at[1]),
        pltpu.make_async_copy(rec_cells_hbm, rec_cells, load_sem.at[2]),
        pltpu.make_async_copy(residuals_hbm, residuals, load_sem.at[3]),
        pltpu.make_async_copy(velocity, vel, load_sem.at[4]),
        pltpu.make_async_copy(waves.at[0, 0], prev, load_sem.at[5]),
        pltpu.make_async_copy(momentum, mom, load_sem.at[6]),
        pltpu.make_async_copy(diffusivity, dif, load_sem.at[7]),
        pltpu.make_async_copy(src_cells_hbm, src_cells, load_sem.at[8]),
        pltpu.make_async_copy(src_codes_hbm, src_codes, load_sem.at[9]),
        pltpu.make_async_copy(wavelets_hbm, wavelets, load_sem.at[10]),
    ]
    barrier = pltpu.get_barrier_semaphore()

    def greet(semaphore):
        for partner in partners:
            pl.semaphore_signal(semaphore, inc=1, device_id=partner, device_id_type=MESH)

    def meet(target):
        pl.semaphore_signal(barrier, inc=1, device_id=(shot, target), device_id_type=MESH)

    pl.when(has_above)(lambda: meet(above))
    pl.when(has_below)(lambda: meet(below))
    greet(barrier)
    for load in loads:
        load.start()

    @pl.when(slab == 0)
    def _():
        ext[:, :, pl.ds(0, 4)] = jnp.zeros((STEPS, 2, 4, NX, NY), jnp.float32)
        beyond_z[0] = jnp.zeros((2, ROWS, NY), jnp.float32)
        corner[0] = jnp.zeros((2, ROWS, NY), jnp.float32)

    @pl.when(slab == SLABS - 1)
    def _():
        ext[:, :, pl.ds(12, 4)] = jnp.zeros((STEPS, 2, 4, NX, NY), jnp.float32)
        beyond_z[1] = jnp.zeros((2, ROWS, NY), jnp.float32)
        corner[1] = jnp.zeros((2, ROWS, NY), jnp.float32)

    @pl.when(shot == 0)
    def _():
        beyond_x[0] = jnp.zeros((2, ROWS, NY), jnp.float32)
        corner[:, 0] = jnp.zeros((2, ROWS, NY), jnp.float32)

    @pl.when(shot == SHOTS - 1)
    def _():
        beyond_x[1] = jnp.zeros((2, ROWS, NY), jnp.float32)
        corner[:, 1] = jnp.zeros((2, ROWS, NY), jnp.float32)

    pl.semaphore_wait(
        barrier,
        len(partners) + has_above.astype(jnp.int32) + has_below.astype(jnp.int32),
    )

    width = NX // PARTS

    away = (2, 1, 3, 0)
    quarters = [(cx + d) % 4 for d in away]
    firsts = [pl.multiple_of(quarter * width, width) for quarter in quarters]

    def halo(step, field, turn):
        across = pl.ds(firsts[turn], width) if step == 1 else pl.ds(0, NX)
        copies = []
        for way, (target, first, landing) in enumerate(((above, 4, 0), (below, 0, 12))):
            if step == 0:
                source = waves.at[1, 0, field, pl.ds(first, 4), across]
            else:
                source = ext.at[1, field, pl.ds(4 + first, 4), across]
            copies.append(
                pltpu.make_async_remote_copy(
                    src_ref=source,
                    dst_ref=ext.at[step, field, pl.ds(landing, 4), across],
                    send_sem=halo_send.at[step, field, turn, way],
                    recv_sem=halo_recv.at[step, field, turn, way],
                    device_id=(shot, target),
                    device_id_type=MESH,
                )
            )
        return copies

    def start(copies):
        pl.when(has_above)(copies[0].start)
        pl.when(has_below)(copies[1].start)

    def arrive(copies):
        pl.when(has_below)(copies[0].wait_recv)
        pl.when(has_above)(copies[1].wait_recv)

    def leave(copies):
        pl.when(has_above)(copies[0].wait_send)
        pl.when(has_below)(copies[1].wait_send)

    (u0, q0), (u1, q1) = [
        [[halo(step, field, turn) for turn in range(PARTS if step else 1)] for field in range(2)]
        for step in range(STEPS)
    ]
    for copies in u0 + q0:
        start(copies)
    greet(ready.at[0])

    def near_part(step, field):
        def body(z, carry):
            lat[field, z] = lateral(ext[step, field, 4 + z])
            return carry

        lax.fori_loop(0, ROWS, body, 0)

    def advance(step, field, first=0, count=NX):
        across = pl.ds(first, count)

        def body(z, carry):
            now = ext[step, field, 4 + z, across]
            total = lat[field, z, across] + inject[field, step, z, across]
            for r in range(1, 5):
                total = total + TAPS[r] * (
                    ext[step, field, 4 + z + r, across] + ext[step, field, 4 + z - r, across]
                )
            speed_here = vel[z, across]
            drive = (speed_here * speed_here) * total
            before = prev[field, z, across] if step == 0 else ext[0, field, 4 + z, across]
            after = 2.0 * now - before + drive
            if step == 0:
                ext[1, field, 4 + z, across] = after
            else:
                fields[0, field, z, across] = after
            if field == 0:
                rows = pl.ds(pl.multiple_of(z * NX + first, width), count)
                product = drive * ext[step, 1, 4 + z, across]
                image[rows, :] = product if step == 0 else image[rows, :] + product
            return carry

        lax.fori_loop(0, ROWS, body, 0)

    for load in loads[8:]:
        load.wait()
    base = slab * (ROWS * PLANE)
    cells = [src_cells[0, k] - base for k in range(4)]
    amounts = [[wavelets[t, src_codes[0, k]] for k in range(4)] for t in range(STEPS)]

    def source_row(z, carry):
        cell = lax.broadcasted_iota(jnp.int32, (NX, NY), 0) * NY
        cell = cell + lax.broadcasted_iota(jnp.int32, (NX, NY), 1) + z * PLANE
        grids = [jnp.zeros((NX, NY), jnp.float32) for _ in range(STEPS)]
        for k in range(4):
            here = cell == cells[k]
            for t in range(STEPS):
                grids[t] = grids[t] + jnp.where(here, amounts[t][k], 0.0)
        for t in range(STEPS):
            inject[0, t, z] = grids[t]
        return carry

    lax.fori_loop(0, ROWS, source_row, 0)

    loads[0].wait()
    near_part(0, 0)
    pl.semaphore_wait(ready.at[0], len(partners))
    greet(ready.at[1])

    loads[2].wait()
    loads[3].wait()
    cell = rec_cells[...] - base
    line = cell >> 7
    lane = cell & (NY - 1)
    count = cell.shape[1]
    for t in range(STEPS):
        here = lax.broadcasted_iota(jnp.int32, (NY, count), 0) == lane
        rest = jnp.where(here, residuals[0, pl.ds(t, 1), :], 0.0)
        for part in range(3):
            piece = rest.astype(jnp.bfloat16)
            spread[part, pl.ds(t * NY, NY), :] = piece
            rest = rest - piece.astype(jnp.float32)

    def receiver_row(z, carry):
        here = lax.broadcasted_iota(jnp.int32, (NX, count), 0) + z * NX == line
        chosen = jnp.where(here, 1.0, 0.0).astype(jnp.bfloat16)
        grid = jnp.zeros((NX, STEPS * NY), jnp.float32)
        for part in range(3):
            grid = grid + lax.dot_general(
                chosen,
                spread[part],
                (((1,), (1,)), ((), ())),
                preferred_element_type=jnp.float32,
            )
        for t in range(STEPS):
            inject[1, t, z] = grid[:, t * NY : (t + 1) * NY]
        return carry

    lax.fori_loop(0, ROWS, receiver_row, 0)
    pl.semaphore_wait(ready.at[1], len(partners))

    loads[6].wait()
    loads[7].wait()
    dif_pack[...] = jnp.zeros((2, ROWS, NY), jnp.float32)
    for i in range(2):
        for k in range(3):
            tile = dif[k, :, i, :]
            dif_t[i, k] = tile
            dif_pack[0, pl.ds(3 * i + k, 1), :] = tile[ROWS - 1 :]
            dif_pack[1, pl.ds(3 * i + k, 1), :] = tile[:1]

    def near(source, landing, send_sem, recv_sem, target, goes, comes):
        copy = pltpu.make_async_remote_copy(
            src_ref=source,
            dst_ref=landing,
            send_sem=send_sem,
            recv_sem=recv_sem,
            device_id=target,
            device_id_type=MESH,
        )
        return copy, goes, comes

    dif_ways = [
        (dif_pack.at[0], dif_edge.at[0], (shot, above), has_above, has_below),
        (dif_pack.at[1], dif_edge.at[1], (shot, below), has_below, has_above),
        (dif_t.at[1], dif_side.at[0], (right, slab), has_right, has_left),
        (dif_t.at[0], dif_side.at[1], (left, slab), has_left, has_right),
    ]
    dif_copies = [
        near(source, landing, dif_send.at[n], dif_recv.at[n], target, goes, comes)
        for n, (source, landing, target, goes, comes) in enumerate(dif_ways)
    ]
    near_ways = [
        (held, beyond_z.at[0], (shot, above), has_above, has_below),
        (held, beyond_z.at[1], (shot, below), has_below, has_above),
        (held, beyond_x.at[0], (right, slab), has_right, has_left),
        (held, beyond_x.at[1], (left, slab), has_left, has_right),
        (held.at[1], corner.at[0, 0], (right, above), has_right & has_above, has_left & has_below),
        (held.at[0], corner.at[0, 1], (left, above), has_left & has_above, has_right & has_below),
        (held.at[1], corner.at[1, 0], (right, below), has_right & has_below, has_left & has_above),
        (held.at[0], corner.at[1, 1], (left, below), has_left & has_below, has_right & has_above),
    ]
    near_copies = [
        near(source, landing, near_send.at[n], near_recv.at[n], target, goes, comes)
        for n, (source, landing, target, goes, comes) in enumerate(near_ways)
    ]

    loads[1].wait()
    near_part(0, 1)
    loads[4].wait()
    loads[5].wait()

    for copies in u0:
        arrive(copies)
    advance(0, 0)
    for copies in u1:
        start(copies)
    for copy, goes, _ in dif_copies:
        pl.when(goes)(copy.start)
    near_part(1, 0)

    for copies in q0:
        arrive(copies)
    advance(0, 1)
    start(q1[0])
    start(q1[1])
    near_part(1, 1)

    def strip(i, c, r):
        return image[pl.ds(i * 4 + c * 2 + r, ROWS, stride=NX), :]

    def pair(turn):
        groups = pl.ds(4 * quarters[turn], 4)
        return pltpu.make_async_remote_copy(
            src_ref=pair_out.at[groups],
            dst_ref=pair_in.at[groups],
            send_sem=pair_sem.at[0, turn],
            recv_sem=pair_sem.at[1, turn],
            device_id=(at(cx, cy, 1 - core), slab),
            device_id_type=MESH,
        )

    def column(d, turn):
        return pltpu.make_async_remote_copy(
            src_ref=pair_sum.at[pl.ds(4 * quarters[turn], 4)],
            dst_ref=column_in.at[d],
            send_sem=column_sem.at[0, d],
            recv_sem=column_sem.at[1, d],
            device_id=(at(cx + d, cy, core), slab),
            device_id_type=MESH,
        )

    def row(d):
        return pltpu.make_async_remote_copy(
            src_ref=column_sum.at[(cy + d) % 4],
            dst_ref=row_in.at[d],
            send_sem=row_sem.at[0, d],
            recv_sem=row_sem.at[1, d],
            device_id=(at(cx, cy + d, core), slab),
            device_id_type=MESH,
        )

    columns = [column(away[turn], turn) for turn in range(PARTS - 1)]
    crossing = [row(d) for d in (2, 1, 3)]

    def finish(turn):
        pair(turn).wait_recv()
        for m in range(4):
            i = 4 * quarters[turn] + m
            for r in range(2):
                pair_sum[i, r] = strip(i, core, r) + pair_in[i, r]
        if away[turn] > 0:
            columns[turn].start()

    for turn in range(PARTS):
        arrive(u1[turn])
        advance(1, 0, firsts[turn], width)
        for m in range(4):
            i = 4 * quarters[turn] + m
            for r in range(2):
                pair_out[i, r] = strip(i, 1 - core, r)
        pair(turn).start()
        if turn > 0:
            finish(turn - 1)
    finish(PARTS - 1)
    for copy in columns:
        copy.wait_recv()
    for m in range(4):
        column_sum[m] = (
            pair_sum[4 * cx + m] + column_in[1, m] + column_in[2, m] + column_in[3, m]
        )
    for copy in crossing:
        copy.start()
    for copies in q1[2:]:
        start(copies)
    for copy, _, comes in dif_copies:
        pl.when(comes)(copy.wait_recv)

    for copy in crossing:
        copy.wait_recv()
    total = column_sum[cy] + row_in[1] + row_in[2] + row_in[3]

    depth = lax.broadcasted_iota(jnp.int32, (ROWS, NY), 0)
    along_y = lax.broadcasted_iota(jnp.int32, (ROWS, NY), 1)
    speed = []
    smooth = []
    for i in range(2):
        rows = [vel[z, pl.ds(shot * 2 + i, 1), :] for z in range(ROWS)]
        speed.append(jnp.concatenate(rows, axis=0))
        smooth.append((-0.2 * total[i]) / (speed[i] * SCALE))
    for i in range(2):
        held[i] = smooth[i]
    for n in (4, 5, 6, 7, 2, 3, 0, 1):
        copy, goes, _ = near_copies[n]
        pl.when(goes)(copy.start)

    for copies in q1:
        arrive(copies)
    advance(1, 1)

    for copies in u0 + q0 + u1 + q1:
        leave(copies)
    for turn in range(PARTS):
        pair(turn).wait_send()
    for copy, goes, _ in dif_copies:
        pl.when(goes)(copy.wait_send)

    for copy in columns + crossing:
        copy.wait_send()

    def step(centre, down, up, before, after, kappas):
        sides = shifted(centre, 1, 1, along_y) + shifted(centre, -1, 1, along_y)
        return (
            centre
            + kappas[0] * (up - 2.0 * centre + down)
            + kappas[1] * (after - 2.0 * centre + before)
            + kappas[2] * (sides - 2.0 * centre)
        )

    def down_of(centre, low):
        return jnp.where(depth == 0, pltpu.roll(low, 1, 0), pltpu.roll(centre, 1, 0))

    def up_of(centre, high):
        last = ROWS - 1
        return jnp.where(depth == last, pltpu.roll(high, last, 0), pltpu.roll(centre, last, 0))

    own = [[dif_t[i, k] for k in range(3)] for i in range(2)]
    side = [[dif_side[i, k] for k in range(3)] for i in range(2)]
    edge = [
        [
            [jnp.broadcast_to(dif_edge[z, pl.ds(3 * i + k, 1), :], (ROWS, NY)) for k in range(3)]
            for i in range(2)
        ]
        for z in range(2)
    ]
    for copy, _, comes in near_copies:
        pl.when(comes)(copy.wait_recv)
    low, high = [[beyond_z[z, i] for i in range(2)] for z in range(2)]
    (far_left, near_left), (near_right, far_right) = [
        [beyond_x[x, i] for i in range(2)] for x in range(2)
    ]
    (low_left, low_right), (high_left, high_right) = [
        [corner[z, x] for x in range(2)] for z in range(2)
    ]
    before = [near_left, smooth[0]]
    after = [smooth[1], near_right]
    once = [
        step(
            smooth[i],
            down_of(smooth[i], low[i]),
            up_of(smooth[i], high[i]),
            before[i],
            after[i],
            own[i],
        )
        for i in range(2)
    ]
    once_left = step(
        near_left,
        down_of(near_left, low_left),
        up_of(near_left, high_left),
        far_left,
        smooth[0],
        side[0],
    )
    once_right = step(
        near_right,
        down_of(near_right, low_right),
        up_of(near_right, high_right),
        smooth[1],
        far_right,
        side[1],
    )
    once_left = jnp.where(has_left, once_left, 0.0)
    once_right = jnp.where(has_right, once_right, 0.0)
    low_before, low_after = [low_left, low[0]], [low[1], low_right]
    high_before, high_after = [high_left, high[0]], [high[1], high_right]
    last = ROWS - 1
    twice = []
    for i in range(2):
        once_low = step(
            low[i],
            pltpu.roll(low[i], 1, 0),
            up_of(low[i], smooth[i]),
            low_before[i],
            low_after[i],
            edge[0][i],
        )
        once_high = step(
            high[i],
            down_of(high[i], smooth[i]),
            pltpu.roll(high[i], last, 0),
            high_before[i],
            high_after[i],
            edge[1][i],
        )
        once_low = jnp.where(has_below, once_low, 0.0)
        once_high = jnp.where(has_above, once_high, 0.0)
        twice.append(
            step(
                once[i],
                down_of(once[i], once_low),
                up_of(once[i], once_high),
                once_left if i == 0 else once[0],
                once[1] if i == 0 else once_right,
                own[i],
            )
        )
    smooth = twice
    for i in range(2):
        updated = 0.9 * mom[:, i, :] + smooth[i]
        new_momentum[:, i, :] = updated
        new_velocity[:, i, :] = speed[i] - 0.02 * updated

    for copy, goes, _ in near_copies:
        pl.when(goes)(copy.wait_send)


def store(*refs):
    sources, targets, sem = refs[:3], refs[3:6], refs[6]
    copies = [
        pltpu.make_async_copy(source, target, sem.at[n])
        for n, (source, target) in enumerate(zip(sources, targets))
    ]
    for copy in copies:
        copy.start()
    for copy in copies:
        copy.wait()


def on_device(
    velocity,
    wave_state,
    source_cells,
    source_codes,
    wavelets,
    receiver_cells,
    residuals,
    momentum,
    diffusivity,
):
    hbm = pl.BlockSpec(memory_space=pltpu.HBM)
    vmem = pl.BlockSpec(memory_space=pltpu.VMEM)
    f32 = jnp.float32
    results = (
        jax.ShapeDtypeStruct((1, 2, ROWS, NX, NY), f32),
        jax.ShapeDtypeStruct((ROWS, 2, NY), f32),
        jax.ShapeDtypeStruct((ROWS, 2, NY), f32),
    )
    held = pl.pallas_call(
        kernel,
        out_shape=results,
        in_specs=[hbm] * 9,
        out_specs=(vmem, vmem, vmem),
        scratch_shapes=[
            pltpu.SMEM(source_cells.shape, jnp.int32),
            pltpu.SMEM(source_codes.shape, jnp.int32),
            pltpu.SMEM(wavelets.shape[::-1], f32),
            pltpu.VMEM((STEPS, 2, 16, NX, NY), f32),
            pltpu.VMEM((2, ROWS, NX, NY), f32),
            pltpu.VMEM((ROWS, NX, NY), f32),
            pltpu.VMEM((2, ROWS, NX, NY), f32),
            pltpu.VMEM((2, STEPS, ROWS, NX, NY), f32),
            pltpu.VMEM(receiver_cells.shape, jnp.int32),
            pltpu.VMEM(residuals.shape, f32),
            pltpu.VMEM((3, STEPS * NY, receiver_cells.shape[1]), jnp.bfloat16),
            pltpu.VMEM((ROWS * NX, NY), f32),
            pltpu.VMEM((16, 2, ROWS, NY), f32),
            pltpu.VMEM((16, 2, ROWS, NY), f32),
            pltpu.VMEM((16, 2, ROWS, NY), f32),
            pltpu.VMEM((4, 4, 2, ROWS, NY), f32),
            pltpu.VMEM((4, 2, ROWS, NY), f32),
            pltpu.VMEM((4, 2, ROWS, NY), f32),
            pltpu.VMEM((ROWS, 2, NY), f32),
            pltpu.VMEM((3, ROWS, 2, NY), f32),
            pltpu.VMEM((2, 3, ROWS, NY), f32),
            pltpu.VMEM((2, ROWS, NY), f32),
            pltpu.VMEM((2, 3, ROWS, NY), f32),
            pltpu.VMEM((2, ROWS, NY), f32),
            pltpu.VMEM((2, ROWS, NY), f32),
            pltpu.VMEM((2, 2, ROWS, NY), f32),
            pltpu.VMEM((2, 2, ROWS, NY), f32),
            pltpu.VMEM((2, 2, ROWS, NY), f32),
            pltpu.SemaphoreType.DMA((11,)),
            pltpu.SemaphoreType.DMA((STEPS, 2, PARTS, 2)),
            pltpu.SemaphoreType.DMA((STEPS, 2, PARTS, 2)),
            pltpu.SemaphoreType.DMA((2, PARTS)),
            pltpu.SemaphoreType.DMA((2, 4)),
            pltpu.SemaphoreType.DMA((2, 4)),
            pltpu.SemaphoreType.DMA((4,)),
            pltpu.SemaphoreType.DMA((4,)),
            pltpu.SemaphoreType.DMA((8,)),
            pltpu.SemaphoreType.DMA((8,)),
            pltpu.SemaphoreType.REGULAR((2,)),
        ],
        compiler_params=pltpu.CompilerParams(collective_id=0, has_side_effects=True, vmem_limit_bytes=16 * 2**20),
    )(
        *(
            pltpu.with_memory_space_constraint(operand, pltpu.HBM)
            for operand in (
                source_cells,
                source_codes,
                wavelets.T,
                velocity,
                wave_state,
                receiver_cells,
                residuals,
                momentum,
                diffusivity,
            )
        )
    )
    return pl.pallas_call(
        store,
        out_shape=results,
        in_specs=[vmem] * 3,
        out_specs=(hbm,) * 3,
        scratch_shapes=[pltpu.SemaphoreType.DMA((3,))],
        compiler_params=pltpu.CompilerParams(vmem_limit_bytes=2**20),
    )(*held)


def solution(mesh):
    return jax.shard_map(
        on_device,
        mesh=mesh,
        in_specs=(
            P("slab", None, None),
            P(None, "shot", None, "slab", None, None),
            P("shot", None),
            P("shot", None),
            P(),
            P("shot", None),
            P("shot", None, None),
            P("slab", "shot", None),
            P(None, "slab", "shot", None),
        ),
        out_specs=(
            P("shot", None, "slab", None, None),
            P("slab", "shot", None),
            P("slab", "shot", None),
        ),
        check_vma=False,
    )
```

```python
import math

import jax
import jax.numpy as jnp
from jax import lax
from jax.experimental import pallas as pl
from jax.experimental.pallas import tpu as pltpu
from jax.sharding import PartitionSpec as P

TAPS = (-205.0 / 72.0, 8.0 / 5.0, -1.0 / 5.0, 8.0 / 315.0, -1.0 / 560.0)
MESH = pl.DeviceIdType.MESH
ROWS, NX, NY = 8, 64, 128
SLABS, SHOTS = 32, 32
STEPS = 2
PARTS = 4
PLANE = NX * NY
SCALE = math.sqrt(SHOTS * STEPS)


def shifted(plane, offset, axis, index):
    size = plane.shape[axis]
    rolled = pltpu.roll(plane, (-offset) % size, axis)
    keep = index < size - offset if offset > 0 else index >= -offset
    return jnp.where(keep, rolled, 0.0)


def lateral(plane):
    along_x = lax.broadcasted_iota(jnp.int32, plane.shape, 0)
    along_y = lax.broadcasted_iota(jnp.int32, plane.shape, 1)
    total = (3.0 * TAPS[0]) * plane
    for r in range(1, 5):
        pairs = shifted(plane, r, 0, along_x) + shifted(plane, -r, 0, along_x)
        pairs = pairs + shifted(plane, r, 1, along_y) + shifted(plane, -r, 1, along_y)
        total = total + TAPS[r] * pairs
    return total


def kernel(
    src_cells_hbm,
    src_codes_hbm,
    wavelets_hbm,
    velocity,
    waves,
    rec_cells_hbm,
    residuals_hbm,
    momentum,
    diffusivity,
    fields,
    new_momentum,
    new_velocity,
    src_cells,
    src_codes,
    wavelets,
    ext,
    prev,
    vel,
    lat,
    inject,
    rec_cells,
    residuals,
    spread,
    image,
    pair_out,
    pair_in,
    pair_sum,
    group_in,
    mom,
    dif,
    dif_t,
    dif_pack,
    dif_side,
    dif_edge,
    held,
    beyond_z,
    beyond_x,
    corner,
    load_sem,
    halo_send,
    halo_recv,
    pair_sem,
    group_send,
    group_recv,
    dif_send,
    dif_recv,
    near_send,
    near_recv,
    ready,
):
    shot = lax.axis_index("shot")
    slab = lax.axis_index("slab")
    cx, cy, core = shot // 8, (shot // 2) % 4, shot % 2
    above, below = slab + 1, slab - 1
    left, right = shot - 1, shot + 1
    has_above, has_below = slab < SLABS - 1, slab > 0
    has_left, has_right = shot > 0, shot < SHOTS - 1

    def at(x, y, c):
        return (x % 4) * 8 + (y % 4) * 2 + c

    partners = [(at(cx, cy, 1 - core), slab)]
    partners += [(at(cx, cy + d, core), slab) for d in (1, 3)]
    partners += [(at(cx + d, cy, core), slab) for d in (1, 2, 3)]

    loads = [
        pltpu.make_async_copy(waves.at[1, 0, 0], ext.at[0, 0, pl.ds(4, ROWS)], load_sem.at[0]),
        pltpu.make_async_copy(waves.at[1, 0, 1], ext.at[0, 1, pl.ds(4, ROWS)], load_sem.at[1]),
        pltpu.make_async_copy(rec_cells_hbm, rec_cells, load_sem.at[2]),
        pltpu.make_async_copy(residuals_hbm, residuals, load_sem.at[3]),
        pltpu.make_async_copy(velocity, vel, load_sem.at[4]),
        pltpu.make_async_copy(waves.at[0, 0], prev, load_sem.at[5]),
        pltpu.make_async_copy(momentum, mom, load_sem.at[6]),
        pltpu.make_async_copy(diffusivity, dif, load_sem.at[7]),
        pltpu.make_async_copy(src_cells_hbm, src_cells, load_sem.at[8]),
        pltpu.make_async_copy(src_codes_hbm, src_codes, load_sem.at[9]),
        pltpu.make_async_copy(wavelets_hbm, wavelets, load_sem.at[10]),
    ]
    barrier = pltpu.get_barrier_semaphore()

    def greet(semaphore):
        for partner in partners:
            pl.semaphore_signal(semaphore, inc=1, device_id=partner, device_id_type=MESH)

    def meet(target):
        pl.semaphore_signal(barrier, inc=1, device_id=(shot, target), device_id_type=MESH)

    pl.when(has_above)(lambda: meet(above))
    pl.when(has_below)(lambda: meet(below))
    greet(barrier)
    for load in loads:
        load.start()

    @pl.when(slab == 0)
    def _():
        ext[:, :, pl.ds(0, 4)] = jnp.zeros((STEPS, 2, 4, NX, NY), jnp.float32)
        beyond_z[0] = jnp.zeros((2, ROWS, NY), jnp.float32)
        corner[0] = jnp.zeros((2, ROWS, NY), jnp.float32)

    @pl.when(slab == SLABS - 1)
    def _():
        ext[:, :, pl.ds(12, 4)] = jnp.zeros((STEPS, 2, 4, NX, NY), jnp.float32)
        beyond_z[1] = jnp.zeros((2, ROWS, NY), jnp.float32)
        corner[1] = jnp.zeros((2, ROWS, NY), jnp.float32)

    @pl.when(shot == 0)
    def _():
        beyond_x[0] = jnp.zeros((2, ROWS, NY), jnp.float32)
        corner[:, 0] = jnp.zeros((2, ROWS, NY), jnp.float32)

    @pl.when(shot == SHOTS - 1)
    def _():
        beyond_x[1] = jnp.zeros((2, ROWS, NY), jnp.float32)
        corner[:, 1] = jnp.zeros((2, ROWS, NY), jnp.float32)

    pl.semaphore_wait(
        barrier,
        len(partners) + has_above.astype(jnp.int32) + has_below.astype(jnp.int32),
    )

    width = NX // PARTS

    away = (2, 1, 3, 0)
    quarters = [(cx + d) % 4 for d in away]
    firsts = [pl.multiple_of(quarter * width, width) for quarter in quarters]

    def halo(step, field, turn):
        across = pl.ds(firsts[turn], width) if step == 1 else pl.ds(0, NX)
        copies = []
        for way, (target, first, landing) in enumerate(((above, 4, 0), (below, 0, 12))):
            if step == 0:
                source = waves.at[1, 0, field, pl.ds(first, 4), across]
            else:
                source = ext.at[1, field, pl.ds(4 + first, 4), across]
            copies.append(
                pltpu.make_async_remote_copy(
                    src_ref=source,
                    dst_ref=ext.at[step, field, pl.ds(landing, 4), across],
                    send_sem=halo_send.at[step, field, turn, way],
                    recv_sem=halo_recv.at[step, field, turn, way],
                    device_id=(shot, target),
                    device_id_type=MESH,
                )
            )
        return copies

    def start(copies):
        pl.when(has_above)(copies[0].start)
        pl.when(has_below)(copies[1].start)

    def arrive(copies):
        pl.when(has_below)(copies[0].wait_recv)
        pl.when(has_above)(copies[1].wait_recv)

    def leave(copies):
        pl.when(has_above)(copies[0].wait_send)
        pl.when(has_below)(copies[1].wait_send)

    (u0, q0), (u1, q1) = [
        [[halo(step, field, turn) for turn in range(PARTS if step else 1)] for field in range(2)]
        for step in range(STEPS)
    ]
    for copies in u0 + q0:
        start(copies)
    greet(ready.at[0])

    def near_part(step, field):
        def body(z, carry):
            lat[field, z] = lateral(ext[step, field, 4 + z])
            return carry

        lax.fori_loop(0, ROWS, body, 0)

    def advance(step, field, first=0, count=NX):
        across = pl.ds(first, count)

        def body(z, carry):
            now = ext[step, field, 4 + z, across]
            total = lat[field, z, across] + inject[field, step, z, across]
            for r in range(1, 5):
                total = total + TAPS[r] * (
                    ext[step, field, 4 + z + r, across] + ext[step, field, 4 + z - r, across]
                )
            speed_here = vel[z, across]
            drive = (speed_here * speed_here) * total
            before = prev[field, z, across] if step == 0 else ext[0, field, 4 + z, across]
            after = 2.0 * now - before + drive
            if step == 0:
                ext[1, field, 4 + z, across] = after
            else:
                fields[0, field, z, across] = after
            if field == 0:
                rows = pl.ds(pl.multiple_of(z * NX + first, width), count)
                product = drive * ext[step, 1, 4 + z, across]
                image[rows, :] = product if step == 0 else image[rows, :] + product
            return carry

        lax.fori_loop(0, ROWS, body, 0)

    for load in loads[8:]:
        load.wait()
    base = slab * (ROWS * PLANE)
    cells = [src_cells[0, k] - base for k in range(4)]
    amounts = [[wavelets[t, src_codes[0, k]] for k in range(4)] for t in range(STEPS)]

    def source_row(z, carry):
        cell = lax.broadcasted_iota(jnp.int32, (NX, NY), 0) * NY
        cell = cell + lax.broadcasted_iota(jnp.int32, (NX, NY), 1) + z * PLANE
        grids = [jnp.zeros((NX, NY), jnp.float32) for _ in range(STEPS)]
        for k in range(4):
            here = cell == cells[k]
            for t in range(STEPS):
                grids[t] = grids[t] + jnp.where(here, amounts[t][k], 0.0)
        for t in range(STEPS):
            inject[0, t, z] = grids[t]
        return carry

    lax.fori_loop(0, ROWS, source_row, 0)

    loads[0].wait()
    near_part(0, 0)
    pl.semaphore_wait(ready.at[0], len(partners))
    greet(ready.at[1])

    loads[2].wait()
    loads[3].wait()
    cell = rec_cells[...] - base
    line = cell >> 7
    lane = cell & (NY - 1)
    count = cell.shape[1]
    for t in range(STEPS):
        here = lax.broadcasted_iota(jnp.int32, (NY, count), 0) == lane
        rest = jnp.where(here, residuals[0, pl.ds(t, 1), :], 0.0)
        for part in range(3):
            piece = rest.astype(jnp.bfloat16)
            spread[part, pl.ds(t * NY, NY), :] = piece
            rest = rest - piece.astype(jnp.float32)

    def receiver_row(z, carry):
        here = lax.broadcasted_iota(jnp.int32, (NX, count), 0) + z * NX == line
        chosen = jnp.where(here, 1.0, 0.0).astype(jnp.bfloat16)
        grid = jnp.zeros((NX, STEPS * NY), jnp.float32)
        for part in range(3):
            grid = grid + lax.dot_general(
                chosen,
                spread[part],
                (((1,), (1,)), ((), ())),
                preferred_element_type=jnp.float32,
            )
        for t in range(STEPS):
            inject[1, t, z] = grid[:, t * NY : (t + 1) * NY]
        return carry

    lax.fori_loop(0, ROWS, receiver_row, 0)
    pl.semaphore_wait(ready.at[1], len(partners))

    loads[6].wait()
    loads[7].wait()
    dif_pack[...] = jnp.zeros((2, ROWS, NY), jnp.float32)
    for i in range(2):
        for k in range(3):
            tile = dif[k, :, i, :]
            dif_t[i, k] = tile
            dif_pack[0, pl.ds(3 * i + k, 1), :] = tile[ROWS - 1 :]
            dif_pack[1, pl.ds(3 * i + k, 1), :] = tile[:1]

    def near(source, landing, send_sem, recv_sem, target, goes, comes):
        copy = pltpu.make_async_remote_copy(
            src_ref=source,
            dst_ref=landing,
            send_sem=send_sem,
            recv_sem=recv_sem,
            device_id=target,
            device_id_type=MESH,
        )
        return copy, goes, comes

    dif_ways = [
        (dif_pack.at[0], dif_edge.at[0], (shot, above), has_above, has_below),
        (dif_pack.at[1], dif_edge.at[1], (shot, below), has_below, has_above),
        (dif_t.at[1], dif_side.at[0], (right, slab), has_right, has_left),
        (dif_t.at[0], dif_side.at[1], (left, slab), has_left, has_right),
    ]
    dif_copies = [
        near(source, landing, dif_send.at[n], dif_recv.at[n], target, goes, comes)
        for n, (source, landing, target, goes, comes) in enumerate(dif_ways)
    ]
    near_ways = [
        (held, beyond_z.at[0], (shot, above), has_above, has_below),
        (held, beyond_z.at[1], (shot, below), has_below, has_above),
        (held, beyond_x.at[0], (right, slab), has_right, has_left),
        (held, beyond_x.at[1], (left, slab), has_left, has_right),
        (held.at[1], corner.at[0, 0], (right, above), has_right & has_above, has_left & has_below),
        (held.at[0], corner.at[0, 1], (left, above), has_left & has_above, has_right & has_below),
        (held.at[1], corner.at[1, 0], (right, below), has_right & has_below, has_left & has_above),
        (held.at[0], corner.at[1, 1], (left, below), has_left & has_below, has_right & has_above),
    ]
    near_copies = [
        near(source, landing, near_send.at[n], near_recv.at[n], target, goes, comes)
        for n, (source, landing, target, goes, comes) in enumerate(near_ways)
    ]

    loads[1].wait()
    near_part(0, 1)
    loads[4].wait()
    loads[5].wait()

    for copies in u0:
        arrive(copies)
    advance(0, 0)
    for copies in u1:
        start(copies)
    for copy, goes, _ in dif_copies:
        pl.when(goes)(copy.start)
    near_part(1, 0)

    for copies in q0:
        arrive(copies)
    advance(0, 1)
    start(q1[0])

    def strip(i, c, r):
        return image[pl.ds(i * 4 + c * 2 + r, ROWS, stride=NX), :]

    def pair(turn):
        groups = pl.ds(4 * quarters[turn], 4)
        return pltpu.make_async_remote_copy(
            src_ref=pair_out.at[groups],
            dst_ref=pair_in.at[groups],
            send_sem=pair_sem.at[0, turn],
            recv_sem=pair_sem.at[1, turn],
            device_id=(at(cx, cy, 1 - core), slab),
            device_id_type=MESH,
        )

    def group(k):
        tx, ty = (cx + k // 4) % 4, (cy + k % 4) % 4
        return pltpu.make_async_remote_copy(
            src_ref=pair_sum.at[tx * 4 + ty],
            dst_ref=group_in.at[k],
            send_sem=group_send.at[k],
            recv_sem=group_recv.at[k],
            device_id=(at(tx, ty, core), slab),
            device_id_type=MESH,
        )

    def finish(turn):
        pair(turn).wait_recv()
        for m in range(4):
            i = 4 * quarters[turn] + m
            for r in range(2):
                pair_sum[i, r] = strip(i, core, r) + pair_in[i, r]
        for dy in (2, 1, 3, 0):
            if away[turn] > 0 or dy > 0:
                group(away[turn] * 4 + dy).start()

    for turn in range(PARTS):
        arrive(u1[turn])
        advance(1, 0, firsts[turn], width)
        for m in range(4):
            i = 4 * quarters[turn] + m
            for r in range(2):
                pair_out[i, r] = strip(i, 1 - core, r)
        pair(turn).start()
        if turn > 0:
            finish(turn - 1)
    finish(PARTS - 1)
    for copies in q1[1:]:
        start(copies)
    near_part(1, 1)
    for copy, _, comes in dif_copies:
        pl.when(comes)(copy.wait_recv)

    def take_group(k, total):
        group(k).wait_recv()
        return total + group_in[k]

    total = lax.fori_loop(4, 16, take_group, pair_sum[cx * 4 + cy])
    total = lax.fori_loop(1, 4, take_group, total)

    depth = lax.broadcasted_iota(jnp.int32, (ROWS, NY), 0)
    along_y = lax.broadcasted_iota(jnp.int32, (ROWS, NY), 1)
    speed = []
    smooth = []
    for i in range(2):
        rows = [vel[z, pl.ds(shot * 2 + i, 1), :] for z in range(ROWS)]
        speed.append(jnp.concatenate(rows, axis=0))
        smooth.append((-0.2 * total[i]) / (speed[i] * SCALE))
    for i in range(2):
        held[i] = smooth[i]
    for n in (4, 5, 6, 7, 2, 3, 0, 1):
        copy, goes, _ = near_copies[n]
        pl.when(goes)(copy.start)

    for copies in q1:
        arrive(copies)
    advance(1, 1)

    for copies in u0 + q0 + u1 + q1:
        leave(copies)
    for turn in range(PARTS):
        pair(turn).wait_send()
    for copy, goes, _ in dif_copies:
        pl.when(goes)(copy.wait_send)

    def drain_group(k, carry):
        group(k).wait_send()
        return carry

    lax.fori_loop(1, 16, drain_group, 0)

    def step(centre, down, up, before, after, kappas):
        sides = shifted(centre, 1, 1, along_y) + shifted(centre, -1, 1, along_y)
        return (
            centre
            + kappas[0] * (up - 2.0 * centre + down)
            + kappas[1] * (after - 2.0 * centre + before)
            + kappas[2] * (sides - 2.0 * centre)
        )

    def down_of(centre, low):
        return jnp.where(depth == 0, pltpu.roll(low, 1, 0), pltpu.roll(centre, 1, 0))

    def up_of(centre, high):
        last = ROWS - 1
        return jnp.where(depth == last, pltpu.roll(high, last, 0), pltpu.roll(centre, last, 0))

    own = [[dif_t[i, k] for k in range(3)] for i in range(2)]
    side = [[dif_side[i, k] for k in range(3)] for i in range(2)]
    edge = [
        [
            [jnp.broadcast_to(dif_edge[z, pl.ds(3 * i + k, 1), :], (ROWS, NY)) for k in range(3)]
            for i in range(2)
        ]
        for z in range(2)
    ]
    for copy, _, comes in near_copies:
        pl.when(comes)(copy.wait_recv)
    low, high = [[beyond_z[z, i] for i in range(2)] for z in range(2)]
    (far_left, near_left), (near_right, far_right) = [
        [beyond_x[x, i] for i in range(2)] for x in range(2)
    ]
    (low_left, low_right), (high_left, high_right) = [
        [corner[z, x] for x in range(2)] for z in range(2)
    ]
    before = [near_left, smooth[0]]
    after = [smooth[1], near_right]
    once = [
        step(
            smooth[i],
            down_of(smooth[i], low[i]),
            up_of(smooth[i], high[i]),
            before[i],
            after[i],
            own[i],
        )
        for i in range(2)
    ]
    once_left = step(
        near_left,
        down_of(near_left, low_left),
        up_of(near_left, high_left),
        far_left,
        smooth[0],
        side[0],
    )
    once_right = step(
        near_right,
        down_of(near_right, low_right),
        up_of(near_right, high_right),
        smooth[1],
        far_right,
        side[1],
    )
    once_left = jnp.where(has_left, once_left, 0.0)
    once_right = jnp.where(has_right, once_right, 0.0)
    low_before, low_after = [low_left, low[0]], [low[1], low_right]
    high_before, high_after = [high_left, high[0]], [high[1], high_right]
    last = ROWS - 1
    twice = []
    for i in range(2):
        once_low = step(
            low[i],
            pltpu.roll(low[i], 1, 0),
            up_of(low[i], smooth[i]),
            low_before[i],
            low_after[i],
            edge[0][i],
        )
        once_high = step(
            high[i],
            down_of(high[i], smooth[i]),
            pltpu.roll(high[i], last, 0),
            high_before[i],
            high_after[i],
            edge[1][i],
        )
        once_low = jnp.where(has_below, once_low, 0.0)
        once_high = jnp.where(has_above, once_high, 0.0)
        twice.append(
            step(
                once[i],
                down_of(once[i], once_low),
                up_of(once[i], once_high),
                once_left if i == 0 else once[0],
                once[1] if i == 0 else once_right,
                own[i],
            )
        )
    smooth = twice
    for i in range(2):
        updated = 0.9 * mom[:, i, :] + smooth[i]
        new_momentum[:, i, :] = updated
        new_velocity[:, i, :] = speed[i] - 0.02 * updated

    for copy, goes, _ in near_copies:
        pl.when(goes)(copy.wait_send)


def store(*refs):
    sources, targets, sem = refs[:3], refs[3:6], refs[6]
    copies = [
        pltpu.make_async_copy(source, target, sem.at[n])
        for n, (source, target) in enumerate(zip(sources, targets))
    ]
    for copy in copies:
        copy.start()
    for copy in copies:
        copy.wait()


def on_device(
    velocity,
    wave_state,
    source_cells,
    source_codes,
    wavelets,
    receiver_cells,
    residuals,
    momentum,
    diffusivity,
):
    hbm = pl.BlockSpec(memory_space=pltpu.HBM)
    vmem = pl.BlockSpec(memory_space=pltpu.VMEM)
    f32 = jnp.float32
    results = (
        jax.ShapeDtypeStruct((1, 2, ROWS, NX, NY), f32),
        jax.ShapeDtypeStruct((ROWS, 2, NY), f32),
        jax.ShapeDtypeStruct((ROWS, 2, NY), f32),
    )
    held = pl.pallas_call(
        kernel,
        out_shape=results,
        in_specs=[hbm] * 9,
        out_specs=(vmem, vmem, vmem),
        scratch_shapes=[
            pltpu.SMEM(source_cells.shape, jnp.int32),
            pltpu.SMEM(source_codes.shape, jnp.int32),
            pltpu.SMEM(wavelets.shape[::-1], f32),
            pltpu.VMEM((STEPS, 2, 16, NX, NY), f32),
            pltpu.VMEM((2, ROWS, NX, NY), f32),
            pltpu.VMEM((ROWS, NX, NY), f32),
            pltpu.VMEM((2, ROWS, NX, NY), f32),
            pltpu.VMEM((2, STEPS, ROWS, NX, NY), f32),
            pltpu.VMEM(receiver_cells.shape, jnp.int32),
            pltpu.VMEM(residuals.shape, f32),
            pltpu.VMEM((3, STEPS * NY, receiver_cells.shape[1]), jnp.bfloat16),
            pltpu.VMEM((ROWS * NX, NY), f32),
            pltpu.VMEM((16, 2, ROWS, NY), f32),
            pltpu.VMEM((16, 2, ROWS, NY), f32),
            pltpu.VMEM((16, 2, ROWS, NY), f32),
            pltpu.VMEM((16, 2, ROWS, NY), f32),
            pltpu.VMEM((ROWS, 2, NY), f32),
            pltpu.VMEM((3, ROWS, 2, NY), f32),
            pltpu.VMEM((2, 3, ROWS, NY), f32),
            pltpu.VMEM((2, ROWS, NY), f32),
            pltpu.VMEM((2, 3, ROWS, NY), f32),
            pltpu.VMEM((2, ROWS, NY), f32),
            pltpu.VMEM((2, ROWS, NY), f32),
            pltpu.VMEM((2, 2, ROWS, NY), f32),
            pltpu.VMEM((2, 2, ROWS, NY), f32),
            pltpu.VMEM((2, 2, ROWS, NY), f32),
            pltpu.SemaphoreType.DMA((11,)),
            pltpu.SemaphoreType.DMA((STEPS, 2, PARTS, 2)),
            pltpu.SemaphoreType.DMA((STEPS, 2, PARTS, 2)),
            pltpu.SemaphoreType.DMA((2, PARTS)),
            pltpu.SemaphoreType.DMA((16,)),
            pltpu.SemaphoreType.DMA((16,)),
            pltpu.SemaphoreType.DMA((4,)),
            pltpu.SemaphoreType.DMA((4,)),
            pltpu.SemaphoreType.DMA((8,)),
            pltpu.SemaphoreType.DMA((8,)),
            pltpu.SemaphoreType.REGULAR((2,)),
        ],
        compiler_params=pltpu.CompilerParams(collective_id=0, has_side_effects=True, vmem_limit_bytes=16 * 2**20),
    )(
        *(
            pltpu.with_memory_space_constraint(operand, pltpu.HBM)
            for operand in (
                source_cells,
                source_codes,
                wavelets.T,
                velocity,
                wave_state,
                receiver_cells,
                residuals,
                momentum,
                diffusivity,
            )
        )
    )
    return pl.pallas_call(
        store,
        out_shape=results,
        in_specs=[vmem] * 3,
        out_specs=(hbm,) * 3,
        scratch_shapes=[pltpu.SemaphoreType.DMA((3,))],
        compiler_params=pltpu.CompilerParams(vmem_limit_bytes=2**20),
    )(*held)


def solution(mesh):
    return jax.shard_map(
        on_device,
        mesh=mesh,
        in_specs=(
            P("slab", None, None),
            P(None, "shot", None, "slab", None, None),
            P("shot", None),
            P("shot", None),
            P(),
            P("shot", None),
            P("shot", None, None),
            P("slab", "shot", None),
            P(None, "slab", "shot", None),
        ),
        out_specs=(
            P("shot", None, "slab", None, None),
            P("slab", "shot", None),
            P("slab", "shot", None),
        ),
        check_vma=False,
    )
```

```python
import math

import jax
import jax.numpy as jnp
from jax import lax
from jax.experimental import pallas as pl
from jax.experimental.pallas import tpu as pltpu
from jax.sharding import PartitionSpec as P

TAPS = (-205.0 / 72.0, 8.0 / 5.0, -1.0 / 5.0, 8.0 / 315.0, -1.0 / 560.0)
MESH = pl.DeviceIdType.MESH
ROWS, NX, NY = 8, 64, 128
SLABS, SHOTS = 32, 32
STEPS = 2
PARTS = 4
PLANE = NX * NY
SCALE = math.sqrt(SHOTS * STEPS)


def shifted(plane, offset, axis, index):
    size = plane.shape[axis]
    rolled = pltpu.roll(plane, (-offset) % size, axis)
    keep = index < size - offset if offset > 0 else index >= -offset
    return jnp.where(keep, rolled, 0.0)


def lateral(plane):
    along_x = lax.broadcasted_iota(jnp.int32, plane.shape, 0)
    along_y = lax.broadcasted_iota(jnp.int32, plane.shape, 1)
    total = (3.0 * TAPS[0]) * plane
    for r in range(1, 5):
        pairs = shifted(plane, r, 0, along_x) + shifted(plane, -r, 0, along_x)
        pairs = pairs + shifted(plane, r, 1, along_y) + shifted(plane, -r, 1, along_y)
        total = total + TAPS[r] * pairs
    return total


def kernel(
    src_cells_hbm,
    src_codes_hbm,
    wavelets_hbm,
    velocity,
    waves,
    rec_cells_hbm,
    residuals_hbm,
    momentum,
    diffusivity,
    fields,
    new_momentum,
    new_velocity,
    src_cells,
    src_codes,
    wavelets,
    ext,
    prev,
    vel,
    lat,
    inject,
    rec_cells,
    residuals,
    spread,
    image,
    pair_out,
    pair_in,
    pair_sum,
    group_in,
    mom,
    dif,
    dif_t,
    dif_pack,
    dif_side,
    dif_edge,
    held,
    beyond_z,
    beyond_x,
    corner,
    load_sem,
    halo_send,
    halo_recv,
    pair_sem,
    group_send,
    group_recv,
    dif_send,
    dif_recv,
    near_send,
    near_recv,
    ready,
):
    shot = lax.axis_index("shot")
    slab = lax.axis_index("slab")
    cx, cy, core = shot // 8, (shot // 2) % 4, shot % 2
    above, below = slab + 1, slab - 1
    left, right = shot - 1, shot + 1
    has_above, has_below = slab < SLABS - 1, slab > 0
    has_left, has_right = shot > 0, shot < SHOTS - 1

    def at(x, y, c):
        return (x % 4) * 8 + (y % 4) * 2 + c

    partners = [(at(cx, cy, 1 - core), slab)]
    partners += [(at(cx, cy + d, core), slab) for d in (1, 3)]
    partners += [(at(cx + d, cy, core), slab) for d in (1, 2, 3)]

    loads = [
        pltpu.make_async_copy(waves.at[1, 0, 0], ext.at[0, 0, pl.ds(4, ROWS)], load_sem.at[0]),
        pltpu.make_async_copy(waves.at[1, 0, 1], ext.at[0, 1, pl.ds(4, ROWS)], load_sem.at[1]),
        pltpu.make_async_copy(rec_cells_hbm, rec_cells, load_sem.at[2]),
        pltpu.make_async_copy(residuals_hbm, residuals, load_sem.at[3]),
        pltpu.make_async_copy(velocity, vel, load_sem.at[4]),
        pltpu.make_async_copy(waves.at[0, 0], prev, load_sem.at[5]),
        pltpu.make_async_copy(momentum, mom, load_sem.at[6]),
        pltpu.make_async_copy(diffusivity, dif, load_sem.at[7]),
        pltpu.make_async_copy(src_cells_hbm, src_cells, load_sem.at[8]),
        pltpu.make_async_copy(src_codes_hbm, src_codes, load_sem.at[9]),
        pltpu.make_async_copy(wavelets_hbm, wavelets, load_sem.at[10]),
    ]
    barrier = pltpu.get_barrier_semaphore()

    def greet(semaphore):
        for partner in partners:
            pl.semaphore_signal(semaphore, inc=1, device_id=partner, device_id_type=MESH)

    def meet(target):
        pl.semaphore_signal(barrier, inc=1, device_id=(shot, target), device_id_type=MESH)

    pl.when(has_above)(lambda: meet(above))
    pl.when(has_below)(lambda: meet(below))
    greet(barrier)
    for load in loads:
        load.start()

    @pl.when(slab == 0)
    def _():
        ext[:, :, pl.ds(0, 4)] = jnp.zeros((STEPS, 2, 4, NX, NY), jnp.float32)
        beyond_z[0] = jnp.zeros((2, ROWS, NY), jnp.float32)
        corner[0] = jnp.zeros((2, ROWS, NY), jnp.float32)

    @pl.when(slab == SLABS - 1)
    def _():
        ext[:, :, pl.ds(12, 4)] = jnp.zeros((STEPS, 2, 4, NX, NY), jnp.float32)
        beyond_z[1] = jnp.zeros((2, ROWS, NY), jnp.float32)
        corner[1] = jnp.zeros((2, ROWS, NY), jnp.float32)

    @pl.when(shot == 0)
    def _():
        beyond_x[0] = jnp.zeros((2, ROWS, NY), jnp.float32)
        corner[:, 0] = jnp.zeros((2, ROWS, NY), jnp.float32)

    @pl.when(shot == SHOTS - 1)
    def _():
        beyond_x[1] = jnp.zeros((2, ROWS, NY), jnp.float32)
        corner[:, 1] = jnp.zeros((2, ROWS, NY), jnp.float32)

    pl.semaphore_wait(
        barrier,
        len(partners) + has_above.astype(jnp.int32) + has_below.astype(jnp.int32),
    )

    width = NX // PARTS

    away = (2, 1, 3, 0)
    quarters = [(cx + d) % 4 for d in away]
    firsts = [pl.multiple_of(quarter * width, width) for quarter in quarters]

    def halo(step, field, turn):
        across = pl.ds(firsts[turn], width) if step == 1 else pl.ds(0, NX)
        copies = []
        for way, (target, first, landing) in enumerate(((above, 4, 0), (below, 0, 12))):
            if step == 0:
                source = waves.at[1, 0, field, pl.ds(first, 4), across]
            else:
                source = ext.at[1, field, pl.ds(4 + first, 4), across]
            copies.append(
                pltpu.make_async_remote_copy(
                    src_ref=source,
                    dst_ref=ext.at[step, field, pl.ds(landing, 4), across],
                    send_sem=halo_send.at[step, field, turn, way],
                    recv_sem=halo_recv.at[step, field, turn, way],
                    device_id=(shot, target),
                    device_id_type=MESH,
                )
            )
        return copies

    def start(copies):
        pl.when(has_above)(copies[0].start)
        pl.when(has_below)(copies[1].start)

    def arrive(copies):
        pl.when(has_below)(copies[0].wait_recv)
        pl.when(has_above)(copies[1].wait_recv)

    def leave(copies):
        pl.when(has_above)(copies[0].wait_send)
        pl.when(has_below)(copies[1].wait_send)

    (u0, q0), (u1, q1) = [
        [[halo(step, field, turn) for turn in range(PARTS if step else 1)] for field in range(2)]
        for step in range(STEPS)
    ]
    for copies in u0 + q0:
        start(copies)
    greet(ready.at[0])

    def near_part(step, field):
        def body(z, carry):
            lat[field, z] = lateral(ext[step, field, 4 + z])
            return carry

        lax.fori_loop(0, ROWS, body, 0)

    def advance(step, field, first=0, count=NX):
        across = pl.ds(first, count)

        def body(z, carry):
            now = ext[step, field, 4 + z, across]
            total = lat[field, z, across] + inject[field, step, z, across]
            for r in range(1, 5):
                total = total + TAPS[r] * (
                    ext[step, field, 4 + z + r, across] + ext[step, field, 4 + z - r, across]
                )
            speed_here = vel[z, across]
            drive = (speed_here * speed_here) * total
            before = prev[field, z, across] if step == 0 else ext[0, field, 4 + z, across]
            after = 2.0 * now - before + drive
            if step == 0:
                ext[1, field, 4 + z, across] = after
            else:
                fields[0, field, z, across] = after
            if field == 0:
                rows = pl.ds(pl.multiple_of(z * NX + first, width), count)
                product = drive * ext[step, 1, 4 + z, across]
                image[rows, :] = product if step == 0 else image[rows, :] + product
            return carry

        lax.fori_loop(0, ROWS, body, 0)

    for load in loads[8:]:
        load.wait()
    base = slab * (ROWS * PLANE)
    cells = [src_cells[0, k] - base for k in range(4)]
    amounts = [[wavelets[t, src_codes[0, k]] for k in range(4)] for t in range(STEPS)]

    def source_row(z, carry):
        cell = lax.broadcasted_iota(jnp.int32, (NX, NY), 0) * NY
        cell = cell + lax.broadcasted_iota(jnp.int32, (NX, NY), 1) + z * PLANE
        grids = [jnp.zeros((NX, NY), jnp.float32) for _ in range(STEPS)]
        for k in range(4):
            here = cell == cells[k]
            for t in range(STEPS):
                grids[t] = grids[t] + jnp.where(here, amounts[t][k], 0.0)
        for t in range(STEPS):
            inject[0, t, z] = grids[t]
        return carry

    lax.fori_loop(0, ROWS, source_row, 0)

    loads[0].wait()
    near_part(0, 0)
    pl.semaphore_wait(ready.at[0], len(partners))
    greet(ready.at[1])

    loads[1].wait()
    loads[4].wait()
    loads[5].wait()

    for copies in u0:
        arrive(copies)
    advance(0, 0)
    for copies in u1:
        start(copies)

    loads[2].wait()
    loads[3].wait()
    cell = rec_cells[...] - base
    line = cell >> 7
    lane = cell & (NY - 1)
    count = cell.shape[1]
    for t in range(STEPS):
        here = lax.broadcasted_iota(jnp.int32, (NY, count), 0) == lane
        rest = jnp.where(here, residuals[0, pl.ds(t, 1), :], 0.0)
        for part in range(3):
            piece = rest.astype(jnp.bfloat16)
            spread[part, pl.ds(t * NY, NY), :] = piece
            rest = rest - piece.astype(jnp.float32)

    def receiver_row(z, carry):
        here = lax.broadcasted_iota(jnp.int32, (NX, count), 0) + z * NX == line
        chosen = jnp.where(here, 1.0, 0.0).astype(jnp.bfloat16)
        grid = jnp.zeros((NX, STEPS * NY), jnp.float32)
        for part in range(3):
            grid = grid + lax.dot_general(
                chosen,
                spread[part],
                (((1,), (1,)), ((), ())),
                preferred_element_type=jnp.float32,
            )
        for t in range(STEPS):
            inject[1, t, z] = grid[:, t * NY : (t + 1) * NY]
        return carry

    lax.fori_loop(0, ROWS, receiver_row, 0)
    pl.semaphore_wait(ready.at[1], len(partners))

    loads[6].wait()
    loads[7].wait()
    dif_pack[...] = jnp.zeros((2, ROWS, NY), jnp.float32)
    for i in range(2):
        for k in range(3):
            tile = dif[k, :, i, :]
            dif_t[i, k] = tile
            dif_pack[0, pl.ds(3 * i + k, 1), :] = tile[ROWS - 1 :]
            dif_pack[1, pl.ds(3 * i + k, 1), :] = tile[:1]

    def near(source, landing, send_sem, recv_sem, target, goes, comes):
        copy = pltpu.make_async_remote_copy(
            src_ref=source,
            dst_ref=landing,
            send_sem=send_sem,
            recv_sem=recv_sem,
            device_id=target,
            device_id_type=MESH,
        )
        return copy, goes, comes

    dif_ways = [
        (dif_pack.at[0], dif_edge.at[0], (shot, above), has_above, has_below),
        (dif_pack.at[1], dif_edge.at[1], (shot, below), has_below, has_above),
        (dif_t.at[1], dif_side.at[0], (right, slab), has_right, has_left),
        (dif_t.at[0], dif_side.at[1], (left, slab), has_left, has_right),
    ]
    dif_copies = [
        near(source, landing, dif_send.at[n], dif_recv.at[n], target, goes, comes)
        for n, (source, landing, target, goes, comes) in enumerate(dif_ways)
    ]
    near_ways = [
        (held, beyond_z.at[0], (shot, above), has_above, has_below),
        (held, beyond_z.at[1], (shot, below), has_below, has_above),
        (held, beyond_x.at[0], (right, slab), has_right, has_left),
        (held, beyond_x.at[1], (left, slab), has_left, has_right),
        (held.at[1], corner.at[0, 0], (right, above), has_right & has_above, has_left & has_below),
        (held.at[0], corner.at[0, 1], (left, above), has_left & has_above, has_right & has_below),
        (held.at[1], corner.at[1, 0], (right, below), has_right & has_below, has_left & has_above),
        (held.at[0], corner.at[1, 1], (left, below), has_left & has_below, has_right & has_above),
    ]
    near_copies = [
        near(source, landing, near_send.at[n], near_recv.at[n], target, goes, comes)
        for n, (source, landing, target, goes, comes) in enumerate(near_ways)
    ]

    near_part(0, 1)
    for copy, goes, _ in dif_copies:
        pl.when(goes)(copy.start)
    near_part(1, 0)

    for copies in q0:
        arrive(copies)
    advance(0, 1)
    start(q1[0])

    def strip(i, c, r):
        return image[pl.ds(i * 4 + c * 2 + r, ROWS, stride=NX), :]

    def pair(turn):
        groups = pl.ds(4 * quarters[turn], 4)
        return pltpu.make_async_remote_copy(
            src_ref=pair_out.at[groups],
            dst_ref=pair_in.at[groups],
            send_sem=pair_sem.at[0, turn],
            recv_sem=pair_sem.at[1, turn],
            device_id=(at(cx, cy, 1 - core), slab),
            device_id_type=MESH,
        )

    def group(k):
        tx, ty = (cx + k // 4) % 4, (cy + k % 4) % 4
        return pltpu.make_async_remote_copy(
            src_ref=pair_sum.at[tx * 4 + ty],
            dst_ref=group_in.at[k],
            send_sem=group_send.at[k],
            recv_sem=group_recv.at[k],
            device_id=(at(tx, ty, core), slab),
            device_id_type=MESH,
        )

    def finish(turn):
        pair(turn).wait_recv()
        for m in range(4):
            i = 4 * quarters[turn] + m
            for r in range(2):
                pair_sum[i, r] = strip(i, core, r) + pair_in[i, r]
        for dy in (2, 1, 3, 0):
            if away[turn] > 0 or dy > 0:
                group(away[turn] * 4 + dy).start()

    for turn in range(PARTS):
        arrive(u1[turn])
        advance(1, 0, firsts[turn], width)
        for m in range(4):
            i = 4 * quarters[turn] + m
            for r in range(2):
                pair_out[i, r] = strip(i, 1 - core, r)
        pair(turn).start()
        if turn > 0:
            finish(turn - 1)
    finish(PARTS - 1)
    for copies in q1[1:]:
        start(copies)
    near_part(1, 1)
    for copy, _, comes in dif_copies:
        pl.when(comes)(copy.wait_recv)

    def take_group(k, total):
        group(k).wait_recv()
        return total + group_in[k]

    total = lax.fori_loop(4, 16, take_group, pair_sum[cx * 4 + cy])
    total = lax.fori_loop(1, 4, take_group, total)

    depth = lax.broadcasted_iota(jnp.int32, (ROWS, NY), 0)
    along_y = lax.broadcasted_iota(jnp.int32, (ROWS, NY), 1)
    speed = []
    smooth = []
    for i in range(2):
        rows = [vel[z, pl.ds(shot * 2 + i, 1), :] for z in range(ROWS)]
        speed.append(jnp.concatenate(rows, axis=0))
        smooth.append((-0.2 * total[i]) / (speed[i] * SCALE))
    for i in range(2):
        held[i] = smooth[i]
    for n in (4, 5, 6, 7, 2, 3, 0, 1):
        copy, goes, _ = near_copies[n]
        pl.when(goes)(copy.start)

    for copies in q1:
        arrive(copies)
    advance(1, 1)

    for copies in u0 + q0 + u1 + q1:
        leave(copies)
    for turn in range(PARTS):
        pair(turn).wait_send()
    for copy, goes, _ in dif_copies:
        pl.when(goes)(copy.wait_send)

    def drain_group(k, carry):
        group(k).wait_send()
        return carry

    lax.fori_loop(1, 16, drain_group, 0)

    def step(centre, down, up, before, after, kappas):
        sides = shifted(centre, 1, 1, along_y) + shifted(centre, -1, 1, along_y)
        return (
            centre
            + kappas[0] * (up - 2.0 * centre + down)
            + kappas[1] * (after - 2.0 * centre + before)
            + kappas[2] * (sides - 2.0 * centre)
        )

    def down_of(centre, low):
        return jnp.where(depth == 0, pltpu.roll(low, 1, 0), pltpu.roll(centre, 1, 0))

    def up_of(centre, high):
        last = ROWS - 1
        return jnp.where(depth == last, pltpu.roll(high, last, 0), pltpu.roll(centre, last, 0))

    own = [[dif_t[i, k] for k in range(3)] for i in range(2)]
    side = [[dif_side[i, k] for k in range(3)] for i in range(2)]
    edge = [
        [
            [jnp.broadcast_to(dif_edge[z, pl.ds(3 * i + k, 1), :], (ROWS, NY)) for k in range(3)]
            for i in range(2)
        ]
        for z in range(2)
    ]
    for copy, _, comes in near_copies:
        pl.when(comes)(copy.wait_recv)
    low, high = [[beyond_z[z, i] for i in range(2)] for z in range(2)]
    (far_left, near_left), (near_right, far_right) = [
        [beyond_x[x, i] for i in range(2)] for x in range(2)
    ]
    (low_left, low_right), (high_left, high_right) = [
        [corner[z, x] for x in range(2)] for z in range(2)
    ]
    before = [near_left, smooth[0]]
    after = [smooth[1], near_right]
    once = [
        step(
            smooth[i],
            down_of(smooth[i], low[i]),
            up_of(smooth[i], high[i]),
            before[i],
            after[i],
            own[i],
        )
        for i in range(2)
    ]
    once_left = step(
        near_left,
        down_of(near_left, low_left),
        up_of(near_left, high_left),
        far_left,
        smooth[0],
        side[0],
    )
    once_right = step(
        near_right,
        down_of(near_right, low_right),
        up_of(near_right, high_right),
        smooth[1],
        far_right,
        side[1],
    )
    once_left = jnp.where(has_left, once_left, 0.0)
    once_right = jnp.where(has_right, once_right, 0.0)
    low_before, low_after = [low_left, low[0]], [low[1], low_right]
    high_before, high_after = [high_left, high[0]], [high[1], high_right]
    last = ROWS - 1
    twice = []
    for i in range(2):
        once_low = step(
            low[i],
            pltpu.roll(low[i], 1, 0),
            up_of(low[i], smooth[i]),
            low_before[i],
            low_after[i],
            edge[0][i],
        )
        once_high = step(
            high[i],
            down_of(high[i], smooth[i]),
            pltpu.roll(high[i], last, 0),
            high_before[i],
            high_after[i],
            edge[1][i],
        )
        once_low = jnp.where(has_below, once_low, 0.0)
        once_high = jnp.where(has_above, once_high, 0.0)
        twice.append(
            step(
                once[i],
                down_of(once[i], once_low),
                up_of(once[i], once_high),
                once_left if i == 0 else once[0],
                once[1] if i == 0 else once_right,
                own[i],
            )
        )
    smooth = twice
    for i in range(2):
        updated = 0.9 * mom[:, i, :] + smooth[i]
        new_momentum[:, i, :] = updated
        new_velocity[:, i, :] = speed[i] - 0.02 * updated

    for copy, goes, _ in near_copies:
        pl.when(goes)(copy.wait_send)


def store(*refs):
    sources, targets, sem = refs[:3], refs[3:6], refs[6]
    copies = [
        pltpu.make_async_copy(source, target, sem.at[n])
        for n, (source, target) in enumerate(zip(sources, targets))
    ]
    for copy in copies:
        copy.start()
    for copy in copies:
        copy.wait()


def on_device(
    velocity,
    wave_state,
    source_cells,
    source_codes,
    wavelets,
    receiver_cells,
    residuals,
    momentum,
    diffusivity,
):
    hbm = pl.BlockSpec(memory_space=pltpu.HBM)
    vmem = pl.BlockSpec(memory_space=pltpu.VMEM)
    f32 = jnp.float32
    results = (
        jax.ShapeDtypeStruct((1, 2, ROWS, NX, NY), f32),
        jax.ShapeDtypeStruct((ROWS, 2, NY), f32),
        jax.ShapeDtypeStruct((ROWS, 2, NY), f32),
    )
    held = pl.pallas_call(
        kernel,
        out_shape=results,
        in_specs=[hbm] * 9,
        out_specs=(vmem, vmem, vmem),
        scratch_shapes=[
            pltpu.SMEM(source_cells.shape, jnp.int32),
            pltpu.SMEM(source_codes.shape, jnp.int32),
            pltpu.SMEM(wavelets.shape[::-1], f32),
            pltpu.VMEM((STEPS, 2, 16, NX, NY), f32),
            pltpu.VMEM((2, ROWS, NX, NY), f32),
            pltpu.VMEM((ROWS, NX, NY), f32),
            pltpu.VMEM((2, ROWS, NX, NY), f32),
            pltpu.VMEM((2, STEPS, ROWS, NX, NY), f32),
            pltpu.VMEM(receiver_cells.shape, jnp.int32),
            pltpu.VMEM(residuals.shape, f32),
            pltpu.VMEM((3, STEPS * NY, receiver_cells.shape[1]), jnp.bfloat16),
            pltpu.VMEM((ROWS * NX, NY), f32),
            pltpu.VMEM((16, 2, ROWS, NY), f32),
            pltpu.VMEM((16, 2, ROWS, NY), f32),
            pltpu.VMEM((16, 2, ROWS, NY), f32),
            pltpu.VMEM((16, 2, ROWS, NY), f32),
            pltpu.VMEM((ROWS, 2, NY), f32),
            pltpu.VMEM((3, ROWS, 2, NY), f32),
            pltpu.VMEM((2, 3, ROWS, NY), f32),
            pltpu.VMEM((2, ROWS, NY), f32),
            pltpu.VMEM((2, 3, ROWS, NY), f32),
            pltpu.VMEM((2, ROWS, NY), f32),
            pltpu.VMEM((2, ROWS, NY), f32),
            pltpu.VMEM((2, 2, ROWS, NY), f32),
            pltpu.VMEM((2, 2, ROWS, NY), f32),
            pltpu.VMEM((2, 2, ROWS, NY), f32),
            pltpu.SemaphoreType.DMA((11,)),
            pltpu.SemaphoreType.DMA((STEPS, 2, PARTS, 2)),
            pltpu.SemaphoreType.DMA((STEPS, 2, PARTS, 2)),
            pltpu.SemaphoreType.DMA((2, PARTS)),
            pltpu.SemaphoreType.DMA((16,)),
            pltpu.SemaphoreType.DMA((16,)),
            pltpu.SemaphoreType.DMA((4,)),
            pltpu.SemaphoreType.DMA((4,)),
            pltpu.SemaphoreType.DMA((8,)),
            pltpu.SemaphoreType.DMA((8,)),
            pltpu.SemaphoreType.REGULAR((2,)),
        ],
        compiler_params=pltpu.CompilerParams(collective_id=0, has_side_effects=True, vmem_limit_bytes=16 * 2**20),
    )(
        *(
            pltpu.with_memory_space_constraint(operand, pltpu.HBM)
            for operand in (
                source_cells,
                source_codes,
                wavelets.T,
                velocity,
                wave_state,
                receiver_cells,
                residuals,
                momentum,
                diffusivity,
            )
        )
    )
    return pl.pallas_call(
        store,
        out_shape=results,
        in_specs=[vmem] * 3,
        out_specs=(hbm,) * 3,
        scratch_shapes=[pltpu.SemaphoreType.DMA((3,))],
        compiler_params=pltpu.CompilerParams(vmem_limit_bytes=2**20),
    )(*held)


def solution(mesh):
    return jax.shard_map(
        on_device,
        mesh=mesh,
        in_specs=(
            P("slab", None, None),
            P(None, "shot", None, "slab", None, None),
            P("shot", None),
            P("shot", None),
            P(),
            P("shot", None),
            P("shot", None, None),
            P("slab", "shot", None),
            P(None, "slab", "shot", None),
        ),
        out_specs=(
            P("shot", None, "slab", None, None),
            P("slab", "shot", None),
            P("slab", "shot", None),
        ),
        check_vma=False,
    )
```
